128 devices in a mesh: req: 32 (over y, z, core), tp: 4 (over x).
Axes of the slice: x: 4, y: 4, z: 4, core: 2. Of those that a mesh axis runs over, the one named last changes fastest.
Arguments:
- tokens: bfloat16 [512, 2048], P('req'), may hold values from -6 to 6
- lengths: int32 [512], P('req'), may hold values from 1 to 8192, 131072 in all
- pool_order: int32 [512], replicated, may hold values from 0 to 511, each once
- positions: int32 [512], P('req'), may hold values from 0 to 16383
- slot_mask: int32 [131072], P('req'), may hold values 0 or 1
- kv_cache: bfloat16 [131072, 2, 1024], P('req', None, 'tp'), may hold values from -420 to 420
- attn_gain: bfloat16 [2048], replicated, may hold values from 0.25 to 1.75
- w_query: bfloat16 [2048, 2048], P(None, 'tp'), may hold values from -0.125 to 0.125
- w_key: bfloat16 [2048, 1024], P(None, 'tp'), may hold values from -0.125 to 0.125
- w_value: bfloat16 [2048, 1024], P(None, 'tp'), may hold values from -0.125 to 0.125
- w_out: bfloat16 [2048, 2048], P('tp'), may hold values from -0.125 to 0.125
- ffn_gain: bfloat16 [2048], replicated, may hold values from 0.25 to 1.75
- w_gate: bfloat16 [2048, 4096], P(None, 'tp'), may hold values from -0.125 to 0.125
- w_up: bfloat16 [2048, 4096], P(None, 'tp'), may hold values from -0.125 to 0.125
- w_down: bfloat16 [4096, 2048], P('tp'), may hold values from -0.09375 to 0.09375
Outputs:
- hidden_out: float32 [512, 2048], P('req')
- new_kv: float32 [512, 2, 1024], P('req', None, 'tp')
The draws below stay inside these ranges and needn't reach their ends.
Inputs may be any that keep to these rules, and one draw needn't show every extreme that they name: The lengths add up to 131072, so the requests' caches fill the pool end to end; the largest is exactly 8192. `pool_order`: each request appears exactly once.
All inputs are finite; a program needn't handle non-finite values. No bound on the sum of `lengths` or of `slot_mask` on one device may be relied on, other than what follows from the above.
Results may differ from the reference program's by a relative error of at most 0.013.
The reference program's roundings to bfloat16 on the way count: a program that leaves them out, or rounds other values in their place, can miss the bound.
Values may be sent and summed in bfloat16 or wider, within the bound.
A program may use at most 192 MiB of HBM per device.

```python
import math
import jax
import jax.numpy as jnp
import numpy as np
from jax import lax

D = 2048
HEADS = 16
KV_HEADS = 8
HEAD_DIM = 128
FF = 4096
MOST = 8192
REQS = 512
SLOT_DEV = 4096
SLOTS = 131072
N_REQ = 32


def draw_kv_cache(key, part):
    shape = (SLOTS, 2, KV_HEADS * HEAD_DIM)
    first = jax.random.fold_in(jax.random.fold_in(key, 17), 0)
    scales = jnp.array([1.5, 2.0], jnp.float32)[None, :, None]
    base = jnp.clip(jax.random.normal(first, shape, jnp.float32), -5.0, 5.0)
    return (base * scales).astype(jnp.bfloat16)


def touch_ends(result, own_key, low, top_value):
    extent = result.shape
    spot = [jax.random.randint(jax.random.fold_in(own_key, axis), (), 0, extent[axis]) for axis in range(len(extent))]
    result = result.at[tuple(spot)].set(low)
    longest = extent.index(max(extent))
    spot[longest] = (spot[longest] + 1) % extent[longest]
    return result.at[tuple(spot)].set(top_value)


def level_of(own_key, dims, cuts, least, largest):
    def one(position, shards_of):
        draws = jax.random.uniform(jax.random.fold_in(jax.random.fold_in(own_key, 6), position), (shards_of,), jnp.float32, least / len(cuts), largest / len(cuts))
        return jnp.repeat(jnp.exp(draws), dims[position] // shards_of).reshape((-1,) + (1,) * (len(dims) - position - 1))

    factor_of = one(*cuts[0])
    for cut in cuts[1:]:
        factor_of = factor_of * one(*cut)
    return factor_of


def length_profile(number_of, total, reach, skew):
    loads = [(1 << 20) // math.isqrt(grade ** skew) + 1 for grade in range(2, number_of + 1)]
    surplus, given = total - reach - (number_of - 1), [1] * (number_of - 1)
    while surplus > 0:
        free = [i for i in range(number_of - 1) if given[i] < reach]
        whole, remaining = sum([loads[i] for i in free]), surplus
        for i in free:
            addition = min(reach - given[i], max(1, remaining * loads[i] // whole), surplus)
            given[i] = given[i] + addition
            surplus = surplus - addition
    return np.array([reach] + given)


def uneven(stream_key, amount, total, reach, slope):
    if amount == 2:
        one = jax.random.randint(stream_key, (), max(1, total - reach), min(reach, total - 1) + 1)
        return jnp.stack([one, total - one])
    sizes = jnp.asarray(length_profile(amount, total, reach, slope), jnp.int32)
    pairs = (amount - 1) // 2
    source_of, receiver = sizes[1:1 + 2 * pairs:2], sizes[2:2 + 2 * pairs:2]
    margin = jnp.minimum(source_of - 1, reach - receiver)
    shifted = jax.random.randint(jax.random.fold_in(stream_key, 1), (pairs,), 0, 1 << 20) % (margin + 1)
    sizes = sizes.at[1:1 + 2 * pairs:2].set(source_of - shifted).at[2:2 + 2 * pairs:2].set(receiver + shifted)
    return sizes[jax.random.permutation(jax.random.fold_in(stream_key, 2), amount)]


def gaussian(stream_key, shape, deviation, reach, cuts=(), kind=jnp.bfloat16):
    values = jax.random.normal(stream_key, shape, jnp.float32) * deviation
    if len(cuts) > 0:
        values = level_of(stream_key, shape, cuts, -0.22, 0.18) * values
    return jnp.clip(values, min=-reach, max=reach).astype(kind)


def setup_inputs(seed: int = 0) -> dict:
    key_list = jax.random.split(jax.random.key(seed), 16)
    return {
        "tokens": gaussian(key_list[0], (REQS, D), 1.0, 6.0, ((0, 32),)),
        "lengths": uneven(key_list[1], REQS, SLOTS, MOST, 2).astype(jnp.int32),
        "pool_order": jax.random.permutation(key_list[2], REQS).astype(jnp.int32),
        "positions": touch_ends(jax.random.randint(key_list[3], (REQS,), 0, 16384), jax.random.fold_in(key_list[3], 1), 0, 16383).astype(jnp.int32),
        "slot_mask": touch_ends((jax.random.randint(key_list[4], (SLOTS,), 0, 8) < 7).astype(jnp.int32), jax.random.fold_in(key_list[4], 1), 0, 1),
        "kv_cache": draw_kv_cache(jax.random.fold_in(key_list[15], 71), 0),
        "attn_gain": jnp.clip(1.0 + 0.15 * jax.random.normal(key_list[6], (D,), jnp.float32), 0.25, 1.75).astype(jnp.bfloat16),
        "w_query": gaussian(key_list[7], (D, HEADS * HEAD_DIM), D ** -0.5, 0.125, ((1, 4),)),
        "w_key": gaussian(key_list[8], (D, KV_HEADS * HEAD_DIM), D ** -0.5, 0.125, ((1, 4),)),
        "w_value": gaussian(key_list[9], (D, KV_HEADS * HEAD_DIM), D ** -0.5, 0.125, ((1, 4),)),
        "w_out": gaussian(key_list[10], (HEADS * HEAD_DIM, D), (HEADS * HEAD_DIM) ** -0.5, 0.125, ((0, 4),)),
        "ffn_gain": jnp.clip(1.0 + 0.15 * jax.random.normal(key_list[11], (D,), jnp.float32), 0.25, 1.75).astype(jnp.bfloat16),
        "w_gate": gaussian(key_list[12], (D, FF), D ** -0.5, 0.125, ((1, 4),)),
        "w_up": gaussian(key_list[13], (D, FF), D ** -0.5, 0.125, ((1, 4),)),
        "w_down": gaussian(key_list[14], (FF, D), FF ** -0.5, 0.09375, ((0, 4),)),
    }


ROPE_BASE = 1000000.0
EPS = 1e-05
FLOOR = -1e+30

def rms_norm(rows, gain):
    mean_sq = lax.optimization_barrier(jnp.mean(rows * rows, axis=-1, keepdims=True))
    return rows * lax.rsqrt(mean_sq + EPS) * gain.astype(jnp.float32)

def rotate(vectors, places):
    width = vectors.shape[-1]
    half = width // 2
    freq = ROPE_BASE ** (-(jnp.arange(half, dtype=jnp.float32) * 2.0) / width)
    angle = places.astype(jnp.float32)[:, None] * freq[None, :]
    cosine = jnp.cos(angle)[:, None, :]
    sine = jnp.sin(angle)[:, None, :]
    first = vectors[..., :half]
    second = vectors[..., half:]
    return jnp.concatenate([first * cosine - second * sine, second * cosine + first * sine], axis=-1)

def reference(tokens, lengths, pool_order, positions, slot_mask, kv_cache, attn_gain, w_query, w_key, w_value, w_out, ffn_gain, w_gate, w_up, w_down):
    group = HEADS // KV_HEADS
    scale = 1.0 / math.sqrt(HEAD_DIM)
    rows = tokens.astype(jnp.float32)
    normed = rms_norm(rows, attn_gain).astype(jnp.bfloat16)
    query = rotate(jnp.dot(normed, w_query, preferred_element_type=jnp.float32).reshape(REQS, HEADS, HEAD_DIM), positions).astype(jnp.bfloat16)
    key_full = rotate(jnp.dot(normed, w_key, preferred_element_type=jnp.float32).reshape(REQS, KV_HEADS, HEAD_DIM), positions)
    value_full = jnp.dot(normed, w_value, preferred_element_type=jnp.float32)
    new_kv = jnp.stack([key_full.reshape(REQS, KV_HEADS * HEAD_DIM), value_full], axis=1)
    new_key = key_full.astype(jnp.bfloat16)
    new_value = value_full.astype(jnp.bfloat16)
    ordered = lengths[pool_order]
    ends = jnp.cumsum(ordered).astype(jnp.int32)
    place = jnp.searchsorted(ends, jnp.arange(SLOTS, dtype=jnp.int32), side='right').astype(jnp.int32)
    owner = pool_order[place].astype(jnp.int32)
    grouped = query.reshape(REQS, KV_HEADS, group, HEAD_DIM)

    def block_scores(index):
        low = (index * SLOT_DEV).astype(jnp.int32)
        owners = lax.dynamic_slice_in_dim(owner, low, SLOT_DEV, 0)
        keys = lax.dynamic_slice_in_dim(kv_cache, low, SLOT_DEV, 0)[:, 0, :].reshape(SLOT_DEV, KV_HEADS, HEAD_DIM)
        return jnp.einsum('skgd,skd->skg', grouped[owners].astype(jnp.float32), keys.astype(jnp.float32)) * scale
    scores = lax.map(block_scores, jnp.arange(N_REQ, dtype=jnp.int32)).reshape(SLOTS, KV_HEADS, group)
    live = (slot_mask == 1)[:, None, None]
    scores = jnp.where(live, scores, FLOOR)
    cache_peak = jnp.full((REQS, KV_HEADS, group), FLOOR, jnp.float32).at[owner].max(scores)
    own_score = jnp.einsum('nkgd,nkd->nkg', grouped.astype(jnp.float32), new_key.astype(jnp.float32)) * scale
    peak = jnp.maximum(cache_peak, own_score)
    weights = jnp.where(live, jnp.exp(scores - peak[owner]), 0.0)
    own_weight = jnp.exp(own_score - peak)
    total = jax.ops.segment_sum(weights, owner, num_segments=REQS) + own_weight

    def add_block(carry, index):
        low = (index * SLOT_DEV).astype(jnp.int32)
        owners = lax.dynamic_slice_in_dim(owner, low, SLOT_DEV, 0)
        part = lax.dynamic_slice_in_dim(weights, low, SLOT_DEV, 0)
        values = lax.dynamic_slice_in_dim(kv_cache, low, SLOT_DEV, 0)[:, 1, :].reshape(SLOT_DEV, KV_HEADS, HEAD_DIM)
        term = part[..., None] * values[:, :, None, :].astype(jnp.float32)
        return (carry + jax.ops.segment_sum(term, owners, num_segments=REQS), None)
    summed, _ = lax.scan(add_block, jnp.zeros((REQS, KV_HEADS, group, HEAD_DIM), jnp.float32), jnp.arange(N_REQ, dtype=jnp.int32))
    summed = summed + own_weight[..., None] * new_value.reshape(REQS, KV_HEADS, 1, HEAD_DIM).astype(jnp.float32)
    context = (summed / total[..., None]).reshape(REQS, HEADS * HEAD_DIM).astype(jnp.bfloat16)
    mid = rows + jnp.dot(context, w_out, preferred_element_type=jnp.float32)
    normed_mid = rms_norm(mid, ffn_gain).astype(jnp.bfloat16)
    gate = jnp.dot(normed_mid, w_gate, preferred_element_type=jnp.float32)
    upper = jnp.dot(normed_mid, w_up, preferred_element_type=jnp.float32)
    act = (jax.nn.silu(gate) * upper).astype(jnp.bfloat16)
    hidden_out = mid + jnp.dot(act, w_down, preferred_element_type=jnp.float32)
    return (hidden_out, new_kv)
```

```python
import functools
import math

import jax
import jax.numpy as jnp
import numpy as np
from jax import lax
from jax.experimental import pallas as pl
from jax.experimental.pallas import tpu as pltpu
from jax.sharding import PartitionSpec as P

MESH = pl.DeviceIdType.MESH
HEAD_DIM = 128
ROPE_BASE = 1000000.0
EPS = 1e-05
FLOOR = -1e30
SCALE = 1.0 / math.sqrt(HEAD_DIM)
SIDE = 4
CHIPS = SIDE * SIDE
ROWS = 16
REQS = 512
SLOTS = 4096
HALF = REQS // 2
QW = 512
PW = QW + 128
WIN = 32
BF16 = jnp.bfloat16
F32 = jnp.float32


def place():
    me = lax.axis_index("req")
    core = lax.rem(me, 2)
    chip = me // 2
    return core, chip // SIDE, lax.rem(chip, SIDE), lax.axis_index("tp")


def chip_at(y, z, k):
    return lax.rem(y + k // SIDE, SIDE) * SIDE + lax.rem(z + k % SIDE, SIDE)


def device(chip, core, tp):
    return {"req": chip * 2 + core, "tp": tp}


def rms_norm(rows, gain):
    mean_sq = jnp.mean(rows * rows, axis=-1, keepdims=True)
    return rows * lax.rsqrt(mean_sq + EPS) * gain.astype(F32)


def frequency_table():
    half = HEAD_DIM // 2
    turns = ROPE_BASE ** (-(np.arange(half, dtype=np.float64) * 2.0) / HEAD_DIM) / (2.0 * np.pi)
    first = np.round(turns * 2.0**12) / 2.0**12
    second = np.round((turns - first) * 2.0**23) / 2.0**23
    third = turns - first - second
    table = np.zeros((8, HEAD_DIM), np.float64)
    for i, term in enumerate((first, second, third)):
        table[i] = np.concatenate([term, term])
    return table.astype(np.float32)


def cos_sin(where, table):
    turn = where * table[0:1, :]
    turn = turn - jnp.floor(turn + 0.5)
    turn = turn + where * table[1:2, :]
    turn = turn - jnp.floor(turn + 0.5)
    turn = turn + where * table[2:3, :]
    quarter = jnp.floor(turn * 4.0 + 0.5)
    x = (turn - quarter * 0.25) * np.float32(2.0 * np.pi)
    sq = x * x
    sine = x * (1.0 + sq * (-1.0 / 6 + sq * (1.0 / 120 + sq * (-1.0 / 5040 + sq * (1.0 / 362880)))))
    cosine = 1.0 + sq * (
        -0.5 + sq * (1.0 / 24 + sq * (-1.0 / 720 + sq * (1.0 / 40320 + sq * (-1.0 / 3628800))))
    )
    odd = (quarter == 1.0) | (quarter == -1.0)
    far = (quarter == 2.0) | (quarter == -2.0)
    c = jnp.where(odd, -quarter * sine, jnp.where(far, -cosine, cosine))
    s = jnp.where(odd, quarter * cosine, jnp.where(far, -sine, sine))
    return c, s


def project_kernel(
    len_s, pos_s, tok, gain, table, wq_h, wk_h, wv_h, pool_h,
    qall_o, lens_o, qown_o, newkv_o, kvd_o,
    wq, wk, wv, pool, kvd, tmp, qall, lens,
    w_sem, pool_sem, out_sem, ls_sem, lr_sem, lf_sem, qs_sem, qr_sem, fs_sem, fr_sem,
):
    core, y, z, tp = place()
    chip = y * SIDE + z
    loads = [
        pltpu.make_async_copy(src, dst, w_sem.at[i])
        for i, (src, dst) in enumerate(((wq_h, wq), (wk_h, wk), (wv_h, wv)))
    ]
    piece = 4 * SLOTS // 4
    pool_loads = [
        pltpu.make_async_copy(pool_h.at[pl.ds(i * piece, piece)], pool.at[pl.ds(i * piece, piece)], pool_sem.at[i])
        for i in range(4)
    ]
    for copy in loads + pool_loads:
        copy.start()

    barrier = pltpu.get_barrier_semaphore()
    sibling = device(chip, 1 - core, tp)
    peers = [sibling] + [device(chip_at(y, z, k), core, tp) for k in range(1, CHIPS)]
    for peer in peers:
        pl.semaphore_signal(barrier, inc=1, device_id=peer, device_id_type=MESH)

    lane = lax.broadcasted_iota(jnp.int32, (1, 128), 1)
    mine = jnp.zeros((1, 128), jnp.int32)
    first_lane = lax.rem(chip, 8) * ROWS
    for i in range(ROWS):
        mine = jnp.where(lane == first_lane + i, len_s[i], mine)
    lens[pl.ds(core * CHIPS + chip, 1), :] = mine

    row = lax.broadcasted_iota(jnp.int32, (ROWS, 128), 0)
    where = jnp.zeros((ROWS, 128), jnp.int32)
    for i in range(ROWS):
        where = jnp.where(row == i, pos_s[i], where)
    cosine, sine = cos_sin(where.astype(F32), table[...])
    low = lax.broadcasted_iota(jnp.int32, (ROWS, 128), 1) < HEAD_DIM // 2
    sine = jnp.where(low, -sine, sine)

    def rotate(vectors):
        return vectors * cosine + pltpu.roll(vectors, HEAD_DIM // 2, axis=1) * sine

    normed = rms_norm(tok[...].astype(F32), gain[...]).astype(BF16)

    pl.semaphore_wait(barrier, len(peers))
    my_len = lens.at[pl.ds(core * CHIPS + chip, 1)]
    len_sends = [
        pltpu.make_async_remote_copy(
            src_ref=my_len, dst_ref=my_len, send_sem=ls_sem.at[k], recv_sem=lr_sem.at[k],
            device_id=peers[k], device_id_type=MESH,
        )
        for k in range(1, CHIPS)
    ]
    for copy in len_sends:
        copy.start()

    loads[0].wait()
    query = jnp.dot(normed, wq[...], preferred_element_type=F32)
    mine_at = pl.multiple_of(core * HALF + chip * ROWS, ROWS)
    for h in range(QW // HEAD_DIM):
        cols = pl.ds(h * HEAD_DIM, HEAD_DIM)
        turned = rotate(query[:, h * HEAD_DIM:(h + 1) * HEAD_DIM]).astype(BF16)
        qall[pl.ds(mine_at, ROWS), cols] = turned
        qown_o[:, cols] = turned
    my_rows = qall.at[pl.ds(mine_at, ROWS)]
    q_sends = []
    for k in (10, 5, 7, 13, 15, 2, 8, 6, 14, 9, 11, 1, 3, 4, 12):
        q_sends.append(
            pltpu.make_async_remote_copy(
                src_ref=my_rows, dst_ref=my_rows, send_sem=qs_sem.at[k], recv_sem=qr_sem.at[k],
                device_id=peers[k], device_id_type=MESH,
            )
        )

    def forward(k):
        source = lax.rem(y + SIDE - k // SIDE, SIDE) * SIDE + lax.rem(z + SIDE - k % SIDE, SIDE)
        rows = qall.at[pl.ds(pl.multiple_of(core * HALF + source * ROWS, ROWS), ROWS)]
        return pltpu.make_async_remote_copy(
            src_ref=rows, dst_ref=rows, send_sem=fs_sem.at[k], recv_sem=fr_sem.at[k],
            device_id=sibling, device_id_type=MESH,
        )

    for copy in q_sends:
        copy.start()
    forwards = [forward(0)]
    forwards[0].start()

    loads[1].wait()
    key = jnp.dot(normed, wk[...], preferred_element_type=F32)
    loads[2].wait()
    value = jnp.dot(normed, wv[...], preferred_element_type=F32)
    for h in range(2):
        cols = slice(h * HEAD_DIM, (h + 1) * HEAD_DIM)
        newkv_o[pl.ds(2 * h, ROWS, stride=4), :] = rotate(key[:, cols])
        newkv_o[pl.ds(2 * h + 1, ROWS, stride=4), :] = value[:, cols]

    for copy in len_sends:
        copy.wait()
    group = lens.at[pl.ds(pl.multiple_of(core * CHIPS, CHIPS), CHIPS)]
    len_forward = pltpu.make_async_remote_copy(
        src_ref=group, dst_ref=group, send_sem=lf_sem.at[0], recv_sem=lf_sem.at[1],
        device_id=sibling, device_id_type=MESH,
    )
    len_forward.start()

    def untangle(i):
        tmp[...] = pool[pl.ds(i * 1024, 1024), :].astype(F32)
        for j in range(4):
            kvd[pl.ds(i * 256, 256), pl.ds(j * 128, 128)] = tmp[pl.ds(j, 256, stride=4), :].astype(BF16)

    for i in range(4):
        pool_loads[i].wait()
    outs = []
    order = (1, 3, 4, 12, 2, 8, 5, 7, 13, 15, 6, 14, 9, 11, 10)
    sends = dict(zip((10, 5, 7, 13, 15, 2, 8, 6, 14, 9, 11, 1, 3, 4, 12), q_sends))
    for i in range(16):
        if i < len(order):
            k = order[i]
            sends[k].wait_recv()
            forwards.append(forward(k))
            forwards[-1].start()
        untangle(i)
        if i % 4 == 3:
            rows = pl.ds((i - 3) * 256, 1024)
            outs.append(pltpu.make_async_copy(kvd.at[rows], kvd_o.at[rows], out_sem.at[i // 4]))
            outs[-1].start()
    len_forward.wait()
    lens_o[...] = lens[...]
    for copy in forwards:
        copy.wait()
    last = pltpu.make_async_copy(qall, qall_o, out_sem.at[4])
    last.start()
    for copy in q_sends:
        copy.wait_send()
    for copy in outs:
        copy.wait()
    last.wait()


def attend_kernel(
    base_s, qall, lens, order, mask, kvd_h, part,
    kvd, scores, order_b, first_b, last_b, pooled, kv_sem,
):
    loads = []
    for i in range(8):
        rows = pl.ds(i * 512, 512)
        loads.append(pltpu.make_async_copy(kvd_h.at[rows], kvd.at[rows], kv_sem.at[i]))
        loads[-1].start()
    base = base_s[0]

    def request_of(n):
        return ((n >> 4) & 15) * 32 + (n >> 8) * 16 + (n & 15)

    n_lane = [request_of(lax.broadcasted_iota(jnp.int32, (1, 128), 1) + 128 * t) for t in range(4)]
    len_lane = [jnp.sum(lens[8 * t:8 * t + 8, :], axis=0, keepdims=True).astype(F32) for t in range(4)]
    pos_lane = [jnp.zeros((1, 128), F32) for _ in range(4)]
    for t in range(4):
        tile = jnp.broadcast_to(order[t:t + 1, :], (128, 128)).astype(F32)
        order_b[pl.ds(128 * t, 128), :] = jnp.transpose(tile).astype(jnp.int32)
    p_sub = lax.broadcasted_iota(jnp.int32, (REQS, 128), 0).astype(F32)
    for t in range(4):
        here = order_b[...] == n_lane[t]
        pos_lane[t] = jnp.sum(jnp.where(here, p_sub, 0.0), axis=0, keepdims=True)
    upto = jnp.zeros((REQS, 128), F32)
    before = jnp.zeros((REQS, 128), F32)
    for t in range(4):
        upto += jnp.where(pos_lane[t] <= p_sub, len_lane[t], 0.0)
        before += jnp.where(pos_lane[t] < p_sub, len_lane[t], 0.0)
    ends = jnp.sum(upto, axis=1, keepdims=True).astype(jnp.int32) - base
    starts = jnp.sum(before, axis=1, keepdims=True).astype(jnp.int32) - base
    first_b[...] = jnp.broadcast_to(starts, (REQS, 128))
    last_b[...] = jnp.broadcast_to(ends, (REQS, 128))
    low = jnp.sum((ends <= 0).astype(jnp.int32))
    high = jnp.sum((starts < SLOTS).astype(jnp.int32))
    low = (low // 16) * 16
    windows = (high - low + (WIN - 1)) // WIN

    pooled[...] = jnp.zeros_like(pooled)
    for copy in loads:
        copy.wait()

    slot = lax.broadcasted_iota(jnp.int32, (8, 128), 1)

    @pl.loop(0, windows)
    def _(w):
        at = pl.multiple_of(jnp.minimum(low + w * WIN, REQS - WIN), 16)
        own = order_b[pl.ds(at, WIN), :]
        pick = jnp.concatenate([(own == n_lane[t]).astype(F32).astype(BF16) for t in range(4)], axis=1)
        query = jnp.dot(pick, qall[...], preferred_element_type=F32).astype(BF16)
        first = first_b[pl.ds(at, WIN), :]
        last = last_b[pl.ds(at, WIN), :]
        first = jnp.concatenate([first, first], axis=0)
        last = jnp.concatenate([last, last], axis=0)
        stats = jnp.zeros((WIN, 128), F32)
        lane = lax.broadcasted_iota(jnp.int32, (WIN, 128), 1)
        for j in range(2):
            q = jnp.concatenate(
                [query[:, (2 * j + g) * HEAD_DIM:(2 * j + g + 1) * HEAD_DIM] for g in range(2)], axis=0
            )

            def score(c, peak):
                start = pl.multiple_of(c * 512, 512)
                keys = kvd[pl.ds(start, 512), pl.ds(2 * j * 128, 128)]
                s = lax.dot_general(q, keys, (((1,), (1,)), ((), ())), preferred_element_type=F32) * SCALE
                for i in range(4):
                    live = mask[pl.ds(c * 4 + i, 1), :] == 1
                    index = jnp.where(live, slot[0:1, :] + (c * 512 + i * 128), -REQS * 8192)
                    ok = (index >= first) & (index < last)
                    part_s = jnp.where(ok, s[:, i * 128:(i + 1) * 128], FLOOR)
                    scores[:, pl.ds(pl.multiple_of(start + i * 128, 128), 128)] = part_s
                    peak = jnp.maximum(peak, part_s)
                return peak

            peak = lax.fori_loop(0, 8, score, jnp.full((2 * WIN, 128), FLOOR, F32))
            peak = jnp.max(peak, axis=1, keepdims=True)
            peak = jnp.where(peak > 0.5 * FLOOR, peak, 0.0)

            def weigh(c, state):
                total, summed = state
                start = pl.multiple_of(c * 512, 512)
                weight = jnp.exp(scores[:, pl.ds(start, 512)] - peak).astype(BF16)
                values = kvd[pl.ds(start, 512), pl.ds((2 * j + 1) * 128, 128)]
                summed = summed + jnp.dot(weight, values, preferred_element_type=F32)
                wide = weight.astype(F32)
                for i in range(4):
                    total = total + wide[:, i * 128:(i + 1) * 128]
                return total, summed

            zero = jnp.zeros((2 * WIN, 128), F32)
            total, summed = lax.fori_loop(0, 8, weigh, (zero, zero))
            total = jnp.sum(total, axis=1, keepdims=True)
            mean = (summed / jnp.where(total > 0.0, total, 1.0)).astype(BF16)
            for g in range(2):
                h = 2 * j + g
                pooled[pl.ds(at, WIN), pl.ds(h * HEAD_DIM, HEAD_DIM)] = mean[g * WIN:(g + 1) * WIN]
                stats = jnp.where(lane == h, peak[g * WIN:(g + 1) * WIN], stats)
                stats = jnp.where(lane == 4 + h, total[g * WIN:(g + 1) * WIN], stats)
        pooled[pl.ds(at, WIN), pl.ds(QW, 128)] = pack_stats(stats)

    n_sub = request_of(lax.broadcasted_iota(jnp.int32, (REQS, 128), 0))
    place_n = jnp.concatenate([(order[t:t + 1, :] == n_sub).astype(F32).astype(BF16) for t in range(4)], axis=1)
    part[...] = jnp.dot(place_n, pooled[...], preferred_element_type=F32).astype(BF16)


def pack_stats(stats):
    top = stats.astype(BF16).astype(F32)
    rest = stats - top
    middle = rest.astype(BF16).astype(F32)
    rest = rest - middle
    return (top + pltpu.roll(middle, 8, axis=1) + pltpu.roll(rest, 16, axis=1)).astype(BF16)


def peaks_totals(tile):
    tile = tile.astype(F32)
    values = tile + pltpu.roll(tile, 120, axis=1) + pltpu.roll(tile, 112, axis=1)
    totals = pltpu.roll(values, 124, axis=1)
    return jnp.where(totals > 0.0, values, FLOOR), totals


def head(block, h):
    return block[:, h * HEAD_DIM:(h + 1) * HEAD_DIM]


def finish_kernel(
    part_h, qown, newkv, tok, gain, wo_h, wg_h, wu_h, wd_h, out,
    own, came, comb, rx, mix, down, wo, wg, wu, wd,
    w_sem, own_sem, ps_sem, pr_sem, cs_sem, cr_sem, ms_sem, mr_sem, ds_sem, dr_sem,
):
    core, y, z, tp = place()
    chip = y * SIDE + z
    barrier = pltpu.get_barrier_semaphore()
    sibling = device(chip, 1 - core, tp)
    peers = [sibling] + [device(chip_at(y, z, k), core, tp) for k in range(1, CHIPS)]
    beside = [device(chip, core, lax.rem(tp + d, 4)) for d in range(1, 4)]
    for peer in peers + beside:
        pl.semaphore_signal(barrier, inc=1, device_id=peer, device_id_type=MESH)
    mine = pltpu.make_async_copy(part_h.at[pl.ds(pl.multiple_of(core * HALF, HALF), HALF)], own, own_sem)
    mine.start()
    pl.semaphore_wait(barrier, len(peers) + len(beside))

    def rows_of(dy):
        return pl.multiple_of(lax.rem(y + dy, SIDE) * 64, 64)

    turns = (2, 1, 3, 0)
    swaps = []
    for dy in turns:
        swaps.append(
            pltpu.make_async_remote_copy(
                src_ref=part_h.at[pl.ds(pl.multiple_of((1 - core) * HALF + rows_of(dy), 64), 64)],
                dst_ref=came.at[pl.ds(rows_of(dy), 64)],
                send_sem=ps_sem.at[dy], recv_sem=pr_sem.at[dy], device_id=sibling, device_id_type=MESH,
            )
        )
        swaps[-1].start()
    loads = [
        pltpu.make_async_copy(src, dst, w_sem.at[i])
        for i, (src, dst) in enumerate(((wo_h, wo), (wg_h, wg), (wu_h, wu), (wd_h, wd)))
    ]
    for copy in loads:
        copy.start()

    mine.wait()
    lane64 = lax.broadcasted_iota(jnp.int32, (64, 128), 1)
    sends = []
    for dy, swap in zip(turns, swaps):
        swap.wait_recv()
        rows = pl.ds(rows_of(dy), 64)
        peak_a, total_a = peaks_totals(own[rows, pl.ds(QW, 128)])
        peak_b, total_b = peaks_totals(came[rows, pl.ds(QW, 128)])
        peak = jnp.maximum(peak_a, peak_b)
        left = total_a * jnp.exp(peak_a - peak)
        right = total_b * jnp.exp(peak_b - peak)
        total = left + right
        share = 1.0 / jnp.where(total > 0.0, total, 1.0)
        for h in range(4):
            cols = pl.ds(h * HEAD_DIM, HEAD_DIM)
            comb[rows, cols] = (
                own[rows, cols].astype(F32) * (left * share)[:, h:h + 1]
                + came[rows, cols].astype(F32) * (right * share)[:, h:h + 1]
            ).astype(BF16)
        stats = jnp.where(lane64 < 4, jnp.where(total > 0.0, peak, 0.0), 0.0)
        shifted = pltpu.roll(jnp.where(lane64 < 4, total, 0.0), 4, axis=1)
        comb[rows, pl.ds(QW, 128)] = pack_stats(stats + shifted)
        for dz in (2, 1, 3, 0):
            k = dy * SIDE + dz
            if k == 0:
                continue
            block = comb.at[pl.ds(pl.multiple_of(chip_at(y, z, k) * ROWS, ROWS), ROWS)]
            sends.append(
                pltpu.make_async_remote_copy(
                    src_ref=block, dst_ref=rx.at[k], send_sem=cs_sem.at[k], recv_sem=cr_sem.at[k],
                    device_id=peers[k], device_id_type=MESH,
                )
            )
            sends[-1].start()

    peaks, totals, blocks = [], [], []
    for h in range(4):
        keys = newkv[pl.ds(2 * (h // 2), ROWS, stride=4), :].astype(BF16).astype(F32)
        query = head(qown[...], h).astype(F32)
        peaks.append(jnp.sum(query * keys, axis=1, keepdims=True) * SCALE)
    lane = lax.broadcasted_iota(jnp.int32, (ROWS, 128), 1)
    own_peak = jnp.full((ROWS, 128), FLOOR, F32)
    for h in range(4):
        own_peak = jnp.where(lane == h, peaks[h], own_peak)

    for copy in sends:
        copy.wait_recv()
    mine_rows = pl.ds(pl.multiple_of(chip * ROWS, ROWS), ROWS)

    def block_of(k, cols):
        return comb[mine_rows, cols] if k == 0 else rx[k, :, cols]

    found = [peaks_totals(block_of(k, pl.ds(QW, 128))) for k in range(CHIPS)]
    peak = own_peak
    for other, _ in found:
        peak = jnp.maximum(peak, other)
    scales = [total * jnp.exp(other - peak) for other, total in found]
    own_scale = jnp.where(lane < 4, jnp.exp(own_peak - peak), 0.0)
    total = own_scale
    for one in scales:
        total = total + one
    total = jnp.where(lane < 4, total, 1.0)
    context = []
    for h in range(4):
        cols = pl.ds(h * HEAD_DIM, HEAD_DIM)
        values = newkv[pl.ds(2 * (h // 2) + 1, ROWS, stride=4), :].astype(BF16).astype(F32)
        summed = own_scale[:, h:h + 1] * values
        for k in range(CHIPS):
            summed = summed + scales[k][:, h:h + 1] * block_of(k, cols).astype(F32)
        context.append((summed / total[:, h:h + 1]).astype(BF16))
    context = jnp.concatenate(context, axis=1)

    def over_tp(left, right, width, terms, send, recv):
        copies = []
        for n in range(4):
            cols = pl.ds(n * width, width)
            terms[tp, :, cols] = jnp.dot(left, right[:, cols], preferred_element_type=F32).astype(BF16)
            for d in range(3):
                ref = terms.at[tp, :, cols]
                copies.append(
                    pltpu.make_async_remote_copy(
                        src_ref=ref, dst_ref=ref, send_sem=send.at[n, d], recv_sem=recv.at[n, d],
                        device_id=beside[d], device_id_type=MESH,
                    )
                )
                copies[-1].start()
        return copies

    def summed_terms(terms):
        total = terms[0].astype(F32)
        for t in range(1, 4):
            total = total + terms[t].astype(F32)
        return total

    loads[0].wait()
    mixes = over_tp(context, wo, 512, mix, ms_sem, mr_sem)
    for copy in mixes:
        copy.wait_recv()
    mid = tok[...].astype(F32) + summed_terms(mix)
    normed = rms_norm(mid, gain[...]).astype(BF16)
    loads[1].wait()
    loads[2].wait()
    acts = []
    for n in range(2):
        cols = pl.ds(n * 512, 512)
        gate = jnp.dot(normed, wg[:, cols], preferred_element_type=F32)
        upper = jnp.dot(normed, wu[:, cols], preferred_element_type=F32)
        acts.append((gate / (1.0 + jnp.exp(-gate)) * upper).astype(BF16))
    act = jnp.concatenate(acts, axis=1)
    loads[3].wait()
    downs = over_tp(act, wd, 512, down, ds_sem, dr_sem)
    for copy in downs:
        copy.wait_recv()
    out[...] = mid + summed_terms(down)
    for copy in swaps + sends + mixes + downs:
        copy.wait_send()


def per_device(
    tokens, lengths, pool_order, positions, slot_mask, kv_cache, attn_gain,
    w_query, w_key, w_value, w_out, ffn_gain, w_gate, w_up, w_down,
):
    vmem = pl.BlockSpec(memory_space=pltpu.VMEM)
    smem = pl.BlockSpec(memory_space=pltpu.SMEM)
    hbm = pl.BlockSpec(memory_space=pl.ANY)
    dma = pltpu.SemaphoreType.DMA
    pool = kv_cache.reshape(SLOTS, 2, 2, HEAD_DIM).transpose(0, 2, 1, 3).reshape(4 * SLOTS, HEAD_DIM)
    qall, lens, qown, newkv, kvd = pl.pallas_call(
        project_kernel,
        out_shape=(
            jax.ShapeDtypeStruct((REQS, QW), BF16),
            jax.ShapeDtypeStruct((32, 128), jnp.int32),
            jax.ShapeDtypeStruct((ROWS, QW), BF16),
            jax.ShapeDtypeStruct((4 * ROWS, HEAD_DIM), F32),
            jax.ShapeDtypeStruct((SLOTS, QW), BF16),
        ),
        in_specs=[smem, smem, vmem, vmem, vmem, hbm, hbm, hbm, hbm],
        out_specs=(hbm, vmem, vmem, vmem, hbm),
        scratch_shapes=[
            pltpu.VMEM((2048, 512), BF16),
            pltpu.VMEM((2048, 256), BF16),
            pltpu.VMEM((2048, 256), BF16),
            pltpu.VMEM((4 * SLOTS, HEAD_DIM), BF16),
            pltpu.VMEM((SLOTS, QW), BF16),
            pltpu.VMEM((1024, HEAD_DIM), F32),
            pltpu.VMEM((REQS, QW), BF16),
            pltpu.VMEM((32, 128), jnp.int32),
            dma((3,)), dma((4,)), dma((5,)), dma((16,)), dma((16,)), dma((2,)),
            dma((16,)), dma((16,)), dma((16,)), dma((16,)),
        ],
        compiler_params=pltpu.CompilerParams(
            collective_id=0, has_side_effects=True, vmem_limit_bytes=40 << 20
        ),
        name="project",
    )(
        lengths, positions, tokens, attn_gain.reshape(1, -1), jnp.asarray(frequency_table()),
        w_query, w_key, w_value, pool,
    )
    base = (lax.axis_index("req") * SLOTS).astype(jnp.int32).reshape(1)
    part = pl.pallas_call(
        attend_kernel,
        out_shape=jax.ShapeDtypeStruct((REQS, PW), BF16),
        in_specs=[smem, vmem, vmem, vmem, vmem, hbm],
        out_specs=vmem,
        scratch_shapes=[
            pltpu.VMEM((SLOTS, QW), BF16),
            pltpu.VMEM((2 * WIN, SLOTS), F32),
            pltpu.VMEM((REQS, 128), jnp.int32),
            pltpu.VMEM((REQS, 128), jnp.int32),
            pltpu.VMEM((REQS, 128), jnp.int32),
            pltpu.VMEM((REQS, PW), BF16),
            dma((8,)),
        ],
        compiler_params=pltpu.CompilerParams(vmem_limit_bytes=40 << 20),
        name="attend",
    )(base, qall, lens, pool_order.reshape(4, 128), slot_mask.reshape(32, 128), kvd)
    hidden = pl.pallas_call(
        finish_kernel,
        out_shape=jax.ShapeDtypeStruct((ROWS, 2048), F32),
        in_specs=[hbm, vmem, vmem, vmem, vmem, hbm, hbm, hbm, hbm],
        out_specs=vmem,
        scratch_shapes=[
            pltpu.VMEM((HALF, PW), BF16),
            pltpu.VMEM((HALF, PW), BF16),
            pltpu.VMEM((HALF, PW), BF16),
            pltpu.VMEM((CHIPS, ROWS, PW), BF16),
            pltpu.VMEM((4, ROWS, 2048), BF16),
            pltpu.VMEM((4, ROWS, 2048), BF16),
            pltpu.VMEM((512, 2048), BF16),
            pltpu.VMEM((2048, 1024), BF16),
            pltpu.VMEM((2048, 1024), BF16),
            pltpu.VMEM((1024, 2048), BF16),
            dma((4,)), dma, dma((4,)), dma((4,)), dma((16,)), dma((16,)),
            dma((4, 3)), dma((4, 3)), dma((4, 3)), dma((4, 3)),
        ],
        compiler_params=pltpu.CompilerParams(
            collective_id=1, has_side_effects=True, vmem_limit_bytes=40 << 20
        ),
        name="finish",
    )(part, qown, newkv, tokens, ffn_gain.reshape(1, -1), w_out, w_gate, w_up, w_down)
    new_kv = newkv.reshape(ROWS, 2, 2, HEAD_DIM).transpose(0, 2, 1, 3).reshape(ROWS, 2, 256)
    return hidden, new_kv


def solution(mesh):
    placed = (
        P("req", None), P("req"), P(), P("req"), P("req"), P("req", None, "tp"), P(),
        P(None, "tp"), P(None, "tp"), P(None, "tp"), P("tp", None), P(),
        P(None, "tp"), P(None, "tp"), P("tp", None),
    )
    return jax.shard_map(
        per_device,
        mesh=mesh,
        in_specs=placed,
        out_specs=(P("req", None), P("req", None, "tp")),
        check_vma=False,
    )
```

```python
import functools
import math

import jax
import jax.numpy as jnp
import numpy as np
from jax import lax
from jax.experimental import pallas as pl
from jax.experimental.pallas import tpu as pltpu
from jax.sharding import PartitionSpec as P

MESH = pl.DeviceIdType.MESH
HEAD_DIM = 128
ROPE_BASE = 1000000.0
EPS = 1e-05
FLOOR = -1e30
SCALE = 1.0 / math.sqrt(HEAD_DIM)
SIDE = 4
CHIPS = SIDE * SIDE
ROWS = 16
REQS = 512
SLOTS = 4096
HALF = REQS // 2
QW = 512
PW = QW + 128
WIN = 32
BF16 = jnp.bfloat16
F32 = jnp.float32


def place():
    me = lax.axis_index("req")
    core = lax.rem(me, 2)
    chip = me // 2
    return core, chip // SIDE, lax.rem(chip, SIDE), lax.axis_index("tp")


def chip_at(y, z, k):
    return lax.rem(y + k // SIDE, SIDE) * SIDE + lax.rem(z + k % SIDE, SIDE)


def device(chip, core, tp):
    return {"req": chip * 2 + core, "tp": tp}


def rms_norm(rows, gain):
    scale = lax.rsqrt(jnp.mean(rows * rows, axis=-1, keepdims=True) + EPS)
    gain = gain.astype(F32)
    tiles = [rows[:, i * 128:(i + 1) * 128] * scale * gain[i:i + 1, :] for i in range(gain.shape[0])]
    return jnp.concatenate(tiles, axis=1).astype(BF16)


def frequency_table():
    half = HEAD_DIM // 2
    turns = ROPE_BASE ** (-(np.arange(half, dtype=np.float64) * 2.0) / HEAD_DIM) / (2.0 * np.pi)
    first = np.round(turns * 2.0**12) / 2.0**12
    second = np.round((turns - first) * 2.0**23) / 2.0**23
    third = turns - first - second
    table = np.zeros((8, HEAD_DIM), np.float64)
    for i, term in enumerate((first, second, third)):
        table[i] = np.concatenate([term, term])
    return table.astype(np.float32)


def cos_sin(where, table):
    turn = where * table[0:1, :]
    turn = turn - jnp.floor(turn + 0.5)
    turn = turn + where * table[1:2, :]
    turn = turn - jnp.floor(turn + 0.5)
    turn = turn + where * table[2:3, :]
    quarter = jnp.floor(turn * 4.0 + 0.5)
    x = (turn - quarter * 0.25) * np.float32(2.0 * np.pi)
    sq = x * x
    sine = x * (1.0 + sq * (-1.0 / 6 + sq * (1.0 / 120 + sq * (-1.0 / 5040 + sq * (1.0 / 362880)))))
    cosine = 1.0 + sq * (
        -0.5 + sq * (1.0 / 24 + sq * (-1.0 / 720 + sq * (1.0 / 40320 + sq * (-1.0 / 3628800))))
    )
    odd = (quarter == 1.0) | (quarter == -1.0)
    far = (quarter == 2.0) | (quarter == -2.0)
    c = jnp.where(odd, -quarter * sine, jnp.where(far, -cosine, cosine))
    s = jnp.where(odd, quarter * cosine, jnp.where(far, -sine, sine))
    return c, s


def project_kernel(
    len_h, pos_h, tok_h, gain_h, table_h, wq_h, wk_h, wv_h, pool_h,
    qall, lens, qown_o, newkv_o, kvd,
    len_s, pos_s, tok, gain, table, wq, wk, wv, pool, tmp,
    s_sem, w_sem, pool_sem, ls_sem, lr_sem, lf_sem, qs_sem, qr_sem, fs_sem, fr_sem,
):
    core, y, z, tp = place()
    chip = y * SIDE + z
    small = [
        pltpu.make_async_copy(src, dst, s_sem.at[i])
        for i, (src, dst) in enumerate(
            ((len_h, len_s), (pos_h, pos_s), (table_h, table), (tok_h, tok), (gain_h, gain))
        )
    ]
    loads = [
        pltpu.make_async_copy(src, dst, w_sem.at[i])
        for i, (src, dst) in enumerate(((wq_h, wq), (wk_h, wk), (wv_h, wv)))
    ]
    piece = 4 * SLOTS // 4
    pool_loads = [
        pltpu.make_async_copy(pool_h.at[pl.ds(i * piece, piece)], pool.at[pl.ds(i * piece, piece)], pool_sem.at[i])
        for i in range(4)
    ]
    for copy in small + loads + pool_loads:
        copy.start()

    barrier = pltpu.get_barrier_semaphore()
    sibling = device(chip, 1 - core, tp)
    peers = [sibling] + [device(chip_at(y, z, k), core, tp) for k in range(1, CHIPS)]
    for peer in peers:
        pl.semaphore_signal(barrier, inc=1, device_id=peer, device_id_type=MESH)

    for copy in small:
        copy.wait()
    lane = lax.broadcasted_iota(jnp.int32, (1, 128), 1)
    mine = jnp.zeros((1, 128), jnp.int32)
    first_lane = lax.rem(chip, 8) * ROWS
    for i in range(ROWS):
        mine = jnp.where(lane == first_lane + i, len_s[i], mine)
    lens[pl.ds(core * CHIPS + chip, 1), :] = mine

    row = lax.broadcasted_iota(jnp.int32, (ROWS, 128), 0)
    where = jnp.zeros((ROWS, 128), jnp.int32)
    for i in range(ROWS):
        where = jnp.where(row == i, pos_s[i], where)
    cosine, sine = cos_sin(where.astype(F32), table[...])
    low = lax.broadcasted_iota(jnp.int32, (ROWS, 128), 1) < HEAD_DIM // 2
    sine = jnp.where(low, -sine, sine)

    def rotate(vectors):
        return vectors * cosine + pltpu.roll(vectors, HEAD_DIM // 2, axis=1) * sine

    normed = rms_norm(tok[...].astype(F32), gain[...])

    pl.semaphore_wait(barrier, len(peers))
    my_len = lens.at[pl.ds(core * CHIPS + chip, 1)]
    len_sends = [
        pltpu.make_async_remote_copy(
            src_ref=my_len, dst_ref=my_len, send_sem=ls_sem.at[k], recv_sem=lr_sem.at[k],
            device_id=peers[k], device_id_type=MESH,
        )
        for k in range(1, CHIPS)
    ]
    for copy in len_sends:
        copy.start()

    loads[0].wait()
    query = jnp.dot(normed, wq[...], preferred_element_type=F32)
    mine_at = pl.multiple_of(core * HALF + chip * ROWS, ROWS)
    for h in range(QW // HEAD_DIM):
        cols = pl.ds(h * HEAD_DIM, HEAD_DIM)
        turned = rotate(query[:, h * HEAD_DIM:(h + 1) * HEAD_DIM]).astype(BF16)
        qall[pl.ds(mine_at, ROWS), cols] = turned
        qown_o[:, cols] = turned
    my_rows = qall.at[pl.ds(mine_at, ROWS)]
    q_sends = []
    for k in (10, 5, 7, 13, 15, 2, 8, 6, 14, 9, 11, 1, 3, 4, 12):
        q_sends.append(
            pltpu.make_async_remote_copy(
                src_ref=my_rows, dst_ref=my_rows, send_sem=qs_sem.at[k], recv_sem=qr_sem.at[k],
                device_id=peers[k], device_id_type=MESH,
            )
        )

    def forward(k):
        source = lax.rem(y + SIDE - k // SIDE, SIDE) * SIDE + lax.rem(z + SIDE - k % SIDE, SIDE)
        rows = qall.at[pl.ds(pl.multiple_of(core * HALF + source * ROWS, ROWS), ROWS)]
        return pltpu.make_async_remote_copy(
            src_ref=rows, dst_ref=rows, send_sem=fs_sem.at[k], recv_sem=fr_sem.at[k],
            device_id=sibling, device_id_type=MESH,
        )

    for copy in q_sends:
        copy.start()
    forwards = [forward(0)]
    forwards[0].start()

    loads[1].wait()
    key = jnp.dot(normed, wk[...], preferred_element_type=F32)
    loads[2].wait()
    value = jnp.dot(normed, wv[...], preferred_element_type=F32)
    for h in range(2):
        cols = slice(h * HEAD_DIM, (h + 1) * HEAD_DIM)
        newkv_o[pl.ds(2 * h, ROWS, stride=4), :] = rotate(key[:, cols])
        newkv_o[pl.ds(2 * h + 1, ROWS, stride=4), :] = value[:, cols]

    for copy in len_sends:
        copy.wait()
    group = lens.at[pl.ds(pl.multiple_of(core * CHIPS, CHIPS), CHIPS)]
    len_forward = pltpu.make_async_remote_copy(
        src_ref=group, dst_ref=group, send_sem=lf_sem.at[0], recv_sem=lf_sem.at[1],
        device_id=sibling, device_id_type=MESH,
    )
    len_forward.start()

    def untangle(i):
        tmp[...] = pool[pl.ds(i * 1024, 1024), :].astype(F32)
        for j in range(4):
            kvd[pl.ds(i * 256, 256), pl.ds(j * 128, 128)] = tmp[pl.ds(j, 256, stride=4), :].astype(BF16)

    for i in range(4):
        pool_loads[i].wait()
    order = (1, 3, 4, 12, 2, 8, 5, 7, 13, 15, 6, 14, 9, 11, 10)
    sends = dict(zip((10, 5, 7, 13, 15, 2, 8, 6, 14, 9, 11, 1, 3, 4, 12), q_sends))
    for i in range(16):
        if i < len(order):
            k = order[i]
            sends[k].wait_recv()
            forwards.append(forward(k))
            forwards[-1].start()
        untangle(i)
    len_forward.wait()
    for copy in forwards:
        copy.wait()
    for copy in q_sends:
        copy.wait_send()


def attend_kernel(
    base_s, qall, lens, order, mask, kvd, part,
    scores, order_b, first_b, last_b, pooled,
):
    base = base_s[0]

    def request_of(n):
        return ((n >> 4) & 15) * 32 + (n >> 8) * 16 + (n & 15)

    n_lane = [request_of(lax.broadcasted_iota(jnp.int32, (1, 128), 1) + 128 * t) for t in range(4)]
    len_lane = [jnp.sum(lens[8 * t:8 * t + 8, :], axis=0, keepdims=True).astype(F32) for t in range(4)]
    pos_lane = [jnp.zeros((1, 128), F32) for _ in range(4)]
    for t in range(4):
        tile = jnp.broadcast_to(order[t:t + 1, :], (128, 128)).astype(F32)
        order_b[pl.ds(128 * t, 128), :] = jnp.transpose(tile).astype(jnp.int32)
    p_sub = lax.broadcasted_iota(jnp.int32, (REQS, 128), 0).astype(F32)
    for t in range(4):
        here = order_b[...] == n_lane[t]
        pos_lane[t] = jnp.sum(jnp.where(here, p_sub, 0.0), axis=0, keepdims=True)
    upto = jnp.zeros((REQS, 128), F32)
    before = jnp.zeros((REQS, 128), F32)
    for t in range(4):
        upto += jnp.where(pos_lane[t] <= p_sub, len_lane[t], 0.0)
        before += jnp.where(pos_lane[t] < p_sub, len_lane[t], 0.0)
    ends = jnp.sum(upto, axis=1, keepdims=True).astype(jnp.int32) - base
    starts = jnp.sum(before, axis=1, keepdims=True).astype(jnp.int32) - base
    first_b[...] = jnp.broadcast_to(starts, (REQS, 128))
    last_b[...] = jnp.broadcast_to(ends, (REQS, 128))
    low = jnp.sum((ends <= 0).astype(jnp.int32))
    high = jnp.sum((starts < SLOTS).astype(jnp.int32))
    low = (low // 16) * 16
    windows = (high - low + (WIN - 1)) // WIN

    pooled[...] = jnp.zeros_like(pooled)

    slot = lax.broadcasted_iota(jnp.int32, (8, 128), 1)

    @pl.loop(0, windows)
    def _(w):
        at = pl.multiple_of(jnp.minimum(low + w * WIN, REQS - WIN), 16)
        own = order_b[pl.ds(at, WIN), :]
        pick = jnp.concatenate([(own == n_lane[t]).astype(F32).astype(BF16) for t in range(4)], axis=1)
        query = jnp.dot(pick, qall[...], preferred_element_type=F32).astype(BF16)
        first = first_b[pl.ds(at, WIN), :]
        last = last_b[pl.ds(at, WIN), :]
        chunk_from = jnp.maximum(jnp.min(first), 0) // 512
        chunk_to = (jnp.minimum(jnp.max(last), SLOTS) + 511) // 512
        first = jnp.concatenate([first, first], axis=0)
        last = jnp.concatenate([last, last], axis=0)
        stats = jnp.zeros((WIN, 128), F32)
        lane = lax.broadcasted_iota(jnp.int32, (WIN, 128), 1)
        for j in range(2):
            q = jnp.concatenate(
                [query[:, (2 * j + g) * HEAD_DIM:(2 * j + g + 1) * HEAD_DIM] for g in range(2)], axis=0
            )

            def score(c, peak):
                start = pl.multiple_of(c * 512, 512)
                keys = kvd[pl.ds(start, 512), pl.ds(2 * j * 128, 128)]
                s = lax.dot_general(q, keys, (((1,), (1,)), ((), ())), preferred_element_type=F32) * SCALE
                for i in range(4):
                    live = mask[pl.ds(c * 4 + i, 1), :] == 1
                    index = jnp.where(live, slot[0:1, :] + (c * 512 + i * 128), -REQS * 8192)
                    ok = (index >= first) & (index < last)
                    part_s = jnp.where(ok, s[:, i * 128:(i + 1) * 128], FLOOR)
                    scores[:, pl.ds(pl.multiple_of(start + i * 128, 128), 128)] = part_s
                    peak = jnp.maximum(peak, part_s)
                return peak

            peak = lax.fori_loop(chunk_from, chunk_to, score, jnp.full((2 * WIN, 128), FLOOR, F32))
            peak = jnp.max(peak, axis=1, keepdims=True)
            peak = jnp.where(peak > 0.5 * FLOOR, peak, 0.0)

            def weigh(c, state):
                total, summed = state
                start = pl.multiple_of(c * 512, 512)
                weight = jnp.exp(scores[:, pl.ds(start, 512)] - peak).astype(BF16)
                values = kvd[pl.ds(start, 512), pl.ds((2 * j + 1) * 128, 128)]
                summed = summed + jnp.dot(weight, values, preferred_element_type=F32)
                wide = weight.astype(F32)
                for i in range(4):
                    total = total + wide[:, i * 128:(i + 1) * 128]
                return total, summed

            zero = jnp.zeros((2 * WIN, 128), F32)
            total, summed = lax.fori_loop(chunk_from, chunk_to, weigh, (zero, zero))
            total = jnp.sum(total, axis=1, keepdims=True)
            mean = (summed / jnp.where(total > 0.0, total, 1.0)).astype(BF16)
            for g in range(2):
                h = 2 * j + g
                pooled[pl.ds(at, WIN), pl.ds(h * HEAD_DIM, HEAD_DIM)] = mean[g * WIN:(g + 1) * WIN]
                stats = jnp.where(lane == h, peak[g * WIN:(g + 1) * WIN], stats)
                stats = jnp.where(lane == 4 + h, total[g * WIN:(g + 1) * WIN], stats)
        pooled[pl.ds(at, WIN), pl.ds(QW, 128)] = pack_stats(stats)

    n_sub = request_of(lax.broadcasted_iota(jnp.int32, (REQS, 128), 0))
    place_n = jnp.concatenate([(order[t:t + 1, :] == n_sub).astype(F32).astype(BF16) for t in range(4)], axis=1)
    part[...] = jnp.dot(place_n, pooled[...], preferred_element_type=F32).astype(BF16)


def pack_stats(stats):
    top = stats.astype(BF16).astype(F32)
    rest = stats - top
    middle = rest.astype(BF16).astype(F32)
    rest = rest - middle
    return (top + pltpu.roll(middle, 8, axis=1) + pltpu.roll(rest, 16, axis=1)).astype(BF16)


def peaks_totals(tile):
    tile = tile.astype(F32)
    values = tile + pltpu.roll(tile, 120, axis=1) + pltpu.roll(tile, 112, axis=1)
    totals = pltpu.roll(values, 124, axis=1)
    return jnp.where(totals > 0.0, values, FLOOR), totals


def head(block, h):
    return block[:, h * HEAD_DIM:(h + 1) * HEAD_DIM]


def finish_kernel(
    part, qown, newkv, tok, gain, wo_h, wg_h, wu_h, wd_h, out,
    came, comb, rx, mix, down, wo, wg, wu, wd,
    w_sem, ps_sem, pr_sem, cs_sem, cr_sem, ms_sem, mr_sem, ds_sem, dr_sem,
):
    core, y, z, tp = place()
    chip = y * SIDE + z
    barrier = pltpu.get_barrier_semaphore()
    sibling = device(chip, 1 - core, tp)
    peers = [sibling] + [device(chip_at(y, z, k), core, tp) for k in range(1, CHIPS)]
    beside = [device(chip, core, lax.rem(tp + d, 4)) for d in range(1, 4)]
    for peer in peers + beside:
        pl.semaphore_signal(barrier, inc=1, device_id=peer, device_id_type=MESH)
    pl.semaphore_wait(barrier, len(peers) + len(beside))

    def rows_of(dy):
        return pl.multiple_of(lax.rem(y + dy, SIDE) * 64, 64)

    turns = (2, 1, 3, 0)
    swaps = []
    for dy in turns:
        swaps.append(
            pltpu.make_async_remote_copy(
                src_ref=part.at[pl.ds(pl.multiple_of((1 - core) * HALF + rows_of(dy), 64), 64)],
                dst_ref=came.at[pl.ds(rows_of(dy), 64)],
                send_sem=ps_sem.at[dy], recv_sem=pr_sem.at[dy], device_id=sibling, device_id_type=MESH,
            )
        )
        swaps[-1].start()
    loads = [
        pltpu.make_async_copy(src, dst, w_sem.at[i])
        for i, (src, dst) in enumerate(((wo_h, wo), (wg_h, wg), (wu_h, wu), (wd_h, wd)))
    ]
    for copy in loads:
        copy.start()

    lane64 = lax.broadcasted_iota(jnp.int32, (64, 128), 1)
    sends = []
    for dy, swap in zip(turns, swaps):
        swap.wait_recv()
        rows = pl.ds(rows_of(dy), 64)
        mine = pl.ds(pl.multiple_of(core * HALF + rows_of(dy), 64), 64)
        peak_a, total_a = peaks_totals(part[mine, pl.ds(QW, 128)])
        peak_b, total_b = peaks_totals(came[rows, pl.ds(QW, 128)])
        peak = jnp.maximum(peak_a, peak_b)
        left = total_a * jnp.exp(peak_a - peak)
        right = total_b * jnp.exp(peak_b - peak)
        total = left + right
        share = 1.0 / jnp.where(total > 0.0, total, 1.0)
        for h in range(4):
            cols = pl.ds(h * HEAD_DIM, HEAD_DIM)
            comb[rows, cols] = (
                part[mine, cols].astype(F32) * (left * share)[:, h:h + 1]
                + came[rows, cols].astype(F32) * (right * share)[:, h:h + 1]
            ).astype(BF16)
        stats = jnp.where(lane64 < 4, jnp.where(total > 0.0, peak, 0.0), 0.0)
        shifted = pltpu.roll(jnp.where(lane64 < 4, total, 0.0), 4, axis=1)
        comb[rows, pl.ds(QW, 128)] = pack_stats(stats + shifted)
        for dz in (2, 1, 3, 0):
            k = dy * SIDE + dz
            if k == 0:
                continue
            block = comb.at[pl.ds(pl.multiple_of(chip_at(y, z, k) * ROWS, ROWS), ROWS)]
            sends.append(
                pltpu.make_async_remote_copy(
                    src_ref=block, dst_ref=rx.at[k], send_sem=cs_sem.at[k], recv_sem=cr_sem.at[k],
                    device_id=peers[k], device_id_type=MESH,
                )
            )
            sends[-1].start()

    peaks, totals, blocks = [], [], []
    for h in range(4):
        keys = newkv[pl.ds(2 * (h // 2), ROWS, stride=4), :].astype(BF16).astype(F32)
        query = head(qown[...], h).astype(F32)
        peaks.append(jnp.sum(query * keys, axis=1, keepdims=True) * SCALE)
    lane = lax.broadcasted_iota(jnp.int32, (ROWS, 128), 1)
    own_peak = jnp.full((ROWS, 128), FLOOR, F32)
    for h in range(4):
        own_peak = jnp.where(lane == h, peaks[h], own_peak)

    for copy in sends:
        copy.wait_recv()
    mine_rows = pl.ds(pl.multiple_of(chip * ROWS, ROWS), ROWS)

    def block_of(k, cols):
        return comb[mine_rows, cols] if k == 0 else rx[k, :, cols]

    found = [peaks_totals(block_of(k, pl.ds(QW, 128))) for k in range(CHIPS)]
    peak = own_peak
    for other, _ in found:
        peak = jnp.maximum(peak, other)
    scales = [total * jnp.exp(other - peak) for other, total in found]
    own_scale = jnp.where(lane < 4, jnp.exp(own_peak - peak), 0.0)
    total = own_scale
    for one in scales:
        total = total + one
    total = jnp.where(lane < 4, total, 1.0)
    context = []
    for h in range(4):
        cols = pl.ds(h * HEAD_DIM, HEAD_DIM)
        values = newkv[pl.ds(2 * (h // 2) + 1, ROWS, stride=4), :].astype(BF16).astype(F32)
        summed = own_scale[:, h:h + 1] * values
        for k in range(CHIPS):
            summed = summed + scales[k][:, h:h + 1] * block_of(k, cols).astype(F32)
        context.append((summed / total[:, h:h + 1]).astype(BF16))
    context = jnp.concatenate(context, axis=1)

    def over_tp(left, right, width, terms, send, recv):
        copies = []
        for n in range(4):
            cols = pl.ds(n * width, width)
            terms[tp, :, cols] = jnp.dot(left, right[:, cols], preferred_element_type=F32).astype(BF16)
            for d in range(3):
                ref = terms.at[tp, :, cols]
                copies.append(
                    pltpu.make_async_remote_copy(
                        src_ref=ref, dst_ref=ref, send_sem=send.at[n, d], recv_sem=recv.at[n, d],
                        device_id=beside[d], device_id_type=MESH,
                    )
                )
                copies[-1].start()
        return copies

    def summed_terms(terms):
        total = terms[0].astype(F32)
        for t in range(1, 4):
            total = total + terms[t].astype(F32)
        return total

    loads[0].wait()
    mixes = over_tp(context, wo, 512, mix, ms_sem, mr_sem)
    for copy in mixes:
        copy.wait_recv()
    mid = tok[...].astype(F32) + summed_terms(mix)
    normed = rms_norm(mid, gain[...])
    loads[1].wait()
    loads[2].wait()
    acts = []
    for n in range(2):
        cols = pl.ds(n * 512, 512)
        gate = jnp.dot(normed, wg[:, cols], preferred_element_type=F32)
        upper = jnp.dot(normed, wu[:, cols], preferred_element_type=F32)
        acts.append((gate / (1.0 + jnp.exp(-gate)) * upper).astype(BF16))
    act = jnp.concatenate(acts, axis=1)
    loads[3].wait()
    downs = over_tp(act, wd, 512, down, ds_sem, dr_sem)
    for copy in downs:
        copy.wait_recv()
    out[...] = mid + summed_terms(down)
    for copy in swaps + sends + mixes + downs:
        copy.wait_send()


def per_device(
    tokens, lengths, pool_order, positions, slot_mask, kv_cache, attn_gain,
    w_query, w_key, w_value, w_out, ffn_gain, w_gate, w_up, w_down,
):
    def stay(*arrays):
        return [pltpu.with_memory_space_constraint(a, pltpu.HBM) for a in arrays]

    vmem = pl.BlockSpec(memory_space=pltpu.VMEM)
    smem = pl.BlockSpec(memory_space=pltpu.SMEM)
    hbm = pl.BlockSpec(memory_space=pltpu.HBM)
    dma = pltpu.SemaphoreType.DMA
    pool = kv_cache.reshape(SLOTS, 2, 2, HEAD_DIM).transpose(0, 2, 1, 3).reshape(4 * SLOTS, HEAD_DIM)
    qall, lens, qown, newkv, kvd = pl.pallas_call(
        project_kernel,
        out_shape=(
            jax.ShapeDtypeStruct((REQS, QW), BF16),
            jax.ShapeDtypeStruct((32, 128), jnp.int32),
            jax.ShapeDtypeStruct((ROWS, QW), BF16),
            jax.ShapeDtypeStruct((4 * ROWS, HEAD_DIM), F32),
            jax.ShapeDtypeStruct((SLOTS, QW), BF16),
        ),
        in_specs=[hbm] * 9,
        out_specs=(vmem,) * 5,
        scratch_shapes=[
            pltpu.SMEM((ROWS,), jnp.int32),
            pltpu.SMEM((ROWS,), jnp.int32),
            pltpu.VMEM((ROWS, 2048), BF16),
            pltpu.VMEM((16, 128), BF16),
            pltpu.VMEM((8, 128), F32),
            pltpu.VMEM((2048, 512), BF16),
            pltpu.VMEM((2048, 256), BF16),
            pltpu.VMEM((2048, 256), BF16),
            pltpu.VMEM((4 * SLOTS, HEAD_DIM), BF16),
            pltpu.VMEM((1024, HEAD_DIM), F32),
            dma((5,)), dma((3,)), dma((4,)), dma((16,)), dma((16,)), dma((2,)),
            dma((16,)), dma((16,)), dma((16,)), dma((16,)),
        ],
        compiler_params=pltpu.CompilerParams(
            collective_id=0, has_side_effects=True, vmem_limit_bytes=40 << 20
        ),
        name="project",
    )(
        *stay(
            lengths, positions, tokens, attn_gain.reshape(16, 128), jnp.asarray(frequency_table()),
            w_query, w_key, w_value, pool,
        )
    )
    base = (lax.axis_index("req") * SLOTS).astype(jnp.int32).reshape(1)
    part = pl.pallas_call(
        attend_kernel,
        out_shape=jax.ShapeDtypeStruct((REQS, PW), BF16),
        in_specs=[smem, vmem, vmem, vmem, vmem, vmem],
        out_specs=vmem,
        scratch_shapes=[
            pltpu.VMEM((2 * WIN, SLOTS), F32),
            pltpu.VMEM((REQS, 128), jnp.int32),
            pltpu.VMEM((REQS, 128), jnp.int32),
            pltpu.VMEM((REQS, 128), jnp.int32),
            pltpu.VMEM((REQS, PW), BF16),
        ],
        compiler_params=pltpu.CompilerParams(vmem_limit_bytes=40 << 20),
        name="attend",
    )(base, qall, lens, pool_order.reshape(4, 128), slot_mask.reshape(32, 128), kvd)
    hidden = pl.pallas_call(
        finish_kernel,
        out_shape=jax.ShapeDtypeStruct((ROWS, 2048), F32),
        in_specs=[vmem, vmem, vmem, vmem, vmem, hbm, hbm, hbm, hbm],
        out_specs=vmem,
        scratch_shapes=[
            pltpu.VMEM((HALF, PW), BF16),
            pltpu.VMEM((HALF, PW), BF16),
            pltpu.VMEM((CHIPS, ROWS, PW), BF16),
            pltpu.VMEM((4, ROWS, 2048), BF16),
            pltpu.VMEM((4, ROWS, 2048), BF16),
            pltpu.VMEM((512, 2048), BF16),
            pltpu.VMEM((2048, 1024), BF16),
            pltpu.VMEM((2048, 1024), BF16),
            pltpu.VMEM((1024, 2048), BF16),
            dma((4,)), dma((4,)), dma((4,)), dma((16,)), dma((16,)),
            dma((4, 3)), dma((4, 3)), dma((4, 3)), dma((4, 3)),
        ],
        compiler_params=pltpu.CompilerParams(
            collective_id=1, has_side_effects=True, vmem_limit_bytes=40 << 20
        ),
        name="finish",
    )(part, qown, newkv, tokens, ffn_gain.reshape(16, 128), *stay(w_out, w_gate, w_up, w_down))
    new_kv = newkv.reshape(ROWS, 2, 2, HEAD_DIM).transpose(0, 2, 1, 3).reshape(ROWS, 2, 256)
    return hidden, new_kv


def solution(mesh):
    placed = (
        P("req", None), P("req"), P(), P("req"), P("req"), P("req", None, "tp"), P(),
        P(None, "tp"), P(None, "tp"), P(None, "tp"), P("tp", None), P(),
        P(None, "tp"), P(None, "tp"), P("tp", None),
    )
    return jax.shard_map(
        per_device,
        mesh=mesh,
        in_specs=placed,
        out_specs=(P("req", None), P("req", None, "tp")),
        check_vma=False,
    )
```

```python
import functools
import math

import jax
import jax.numpy as jnp
import numpy as np
from jax import lax
from jax.experimental import pallas as pl
from jax.experimental.pallas import tpu as pltpu
from jax.sharding import PartitionSpec as P

MESH = pl.DeviceIdType.MESH
HEAD_DIM = 128
ROPE_BASE = 1000000.0
EPS = 1e-05
FLOOR = -1e30
SCALE = 1.0 / math.sqrt(HEAD_DIM)
SIDE = 4
CHIPS = SIDE * SIDE
ROWS = 16
REQS = 512
SLOTS = 4096
HALF = REQS // 2
QW = 512
PW = QW + 128
WIN = 64
CHUNK = 2048
LOG2E = 1.4426950408889634
BF16 = jnp.bfloat16
F32 = jnp.float32


def place():
    me = lax.axis_index("req")
    core = lax.rem(me, 2)
    chip = me // 2
    return core, chip // SIDE, lax.rem(chip, SIDE), lax.axis_index("tp")


def chip_at(y, z, k):
    return lax.rem(y + k // SIDE, SIDE) * SIDE + lax.rem(z + k % SIDE, SIDE)


def device(chip, core, tp):
    return {"req": chip * 2 + core, "tp": tp}


def rms_norm(rows, gain):
    scale = lax.rsqrt(jnp.mean(rows * rows, axis=-1, keepdims=True) + EPS)
    gain = gain.astype(F32)
    tiles = [rows[:, i * 128:(i + 1) * 128] * scale * gain[i:i + 1, :] for i in range(gain.shape[0])]
    return jnp.concatenate(tiles, axis=1).astype(BF16)


def frequency_table():
    half = HEAD_DIM // 2
    turns = ROPE_BASE ** (-(np.arange(half, dtype=np.float64) * 2.0) / HEAD_DIM) / (2.0 * np.pi)
    first = np.round(turns * 2.0**12) / 2.0**12
    second = np.round((turns - first) * 2.0**23) / 2.0**23
    third = turns - first - second
    table = np.zeros((8, HEAD_DIM), np.float64)
    for i, term in enumerate((first, second, third)):
        table[i] = np.concatenate([term, term])
    return table.astype(np.float32)


def cos_sin(where, table):
    turn = where * table[0:1, :]
    turn = turn - jnp.floor(turn + 0.5)
    turn = turn + where * table[1:2, :]
    turn = turn - jnp.floor(turn + 0.5)
    turn = turn + where * table[2:3, :]
    quarter = jnp.floor(turn * 4.0 + 0.5)
    x = (turn - quarter * 0.25) * np.float32(2.0 * np.pi)
    sq = x * x
    sine = x * (1.0 + sq * (-1.0 / 6 + sq * (1.0 / 120 + sq * (-1.0 / 5040 + sq * (1.0 / 362880)))))
    cosine = 1.0 + sq * (
        -0.5 + sq * (1.0 / 24 + sq * (-1.0 / 720 + sq * (1.0 / 40320 + sq * (-1.0 / 3628800))))
    )
    odd = (quarter == 1.0) | (quarter == -1.0)
    far = (quarter == 2.0) | (quarter == -2.0)
    c = jnp.where(odd, -quarter * sine, jnp.where(far, -cosine, cosine))
    s = jnp.where(odd, quarter * cosine, jnp.where(far, -sine, sine))
    return c, s


def project_kernel(
    len_h, pos_h, tok_h, gain_h, table_h, wq_h, wk_h, wv_h, pool_h,
    qall, qown_o, newkv_o, kvd,
    len_s, pos_s, tok, gain, table, wq, wk, wv, pool, tmp,
    s_sem, w_sem, pool_sem, qs_sem, qr_sem, fs_sem, fr_sem,
):
    core, y, z, tp = place()
    chip = y * SIDE + z
    small = [
        pltpu.make_async_copy(src, dst, s_sem.at[i])
        for i, (src, dst) in enumerate(
            ((len_h, len_s), (pos_h, pos_s), (table_h, table), (tok_h, tok), (gain_h, gain))
        )
    ]
    loads = [
        pltpu.make_async_copy(src, dst, w_sem.at[i])
        for i, (src, dst) in enumerate(((wq_h, wq), (wk_h, wk), (wv_h, wv)))
    ]
    piece = 4 * SLOTS // 4
    pool_loads = [
        pltpu.make_async_copy(pool_h.at[pl.ds(i * piece, piece)], pool.at[pl.ds(i * piece, piece)], pool_sem.at[i])
        for i in range(4)
    ]
    for copy in small + loads + pool_loads:
        copy.start()

    barrier = pltpu.get_barrier_semaphore()
    sibling = device(chip, 1 - core, tp)
    peers = [sibling] + [device(chip_at(y, z, k), core, tp) for k in range(1, CHIPS)]
    for peer in peers:
        pl.semaphore_signal(barrier, inc=1, device_id=peer, device_id_type=MESH)

    for copy in small:
        copy.wait()
    row = lax.broadcasted_iota(jnp.int32, (ROWS, 128), 0)
    lane = lax.broadcasted_iota(jnp.int32, (ROWS, 128), 1)
    where = jnp.zeros((ROWS, 128), jnp.int32)
    digits = jnp.zeros((ROWS, 128), jnp.int32)
    for i in range(ROWS):
        where = jnp.where(row == i, pos_s[i], where)
        digits = jnp.where(row == i, len_s[i], digits)
    digits = jnp.where(lane == 0, digits >> 7, jnp.where(lane == 1, digits & 127, 0)).astype(F32).astype(BF16)
    cosine, sine = cos_sin(where.astype(F32), table[...])
    sine = jnp.where(lane < HEAD_DIM // 2, -sine, sine)

    def rotate(vectors):
        return vectors * cosine + pltpu.roll(vectors, HEAD_DIM // 2, axis=1) * sine

    normed = rms_norm(tok[...].astype(F32), gain[...])

    pl.semaphore_wait(barrier, len(peers))
    loads[0].wait()
    query = jnp.dot(normed, wq[...], preferred_element_type=F32)
    mine_at = pl.multiple_of(core * HALF + chip * ROWS, ROWS)
    for h in range(QW // HEAD_DIM):
        cols = pl.ds(h * HEAD_DIM, HEAD_DIM)
        turned = rotate(query[:, h * HEAD_DIM:(h + 1) * HEAD_DIM]).astype(BF16)
        qall[pl.ds(mine_at, ROWS), cols] = turned
        qown_o[:, cols] = turned
    qall[pl.ds(mine_at, ROWS), pl.ds(QW, 128)] = digits
    my_rows = qall.at[pl.ds(mine_at, ROWS)]
    q_sends = {}
    for k in range(1, CHIPS):
        q_sends[k] = pltpu.make_async_remote_copy(
            src_ref=my_rows, dst_ref=my_rows, send_sem=qs_sem.at[k], recv_sem=qr_sem.at[k],
            device_id=peers[k], device_id_type=MESH,
        )
    far_first = (10, 9, 11, 8, 6, 5, 7, 4, 14, 13, 15, 12, 2, 1, 3)
    for k in far_first:
        q_sends[k].start()

    def forward(dy):
        source = lax.rem(y + SIDE - dy, SIDE) * SIDE * ROWS
        rows = qall.at[pl.ds(pl.multiple_of(core * HALF + source, SIDE * ROWS), SIDE * ROWS)]
        return pltpu.make_async_remote_copy(
            src_ref=rows, dst_ref=rows, send_sem=fs_sem.at[dy], recv_sem=fr_sem.at[dy],
            device_id=sibling, device_id_type=MESH,
        )

    loads[1].wait()
    key = jnp.dot(normed, wk[...], preferred_element_type=F32)
    loads[2].wait()
    value = jnp.dot(normed, wv[...], preferred_element_type=F32)
    for h in range(2):
        cols = slice(h * HEAD_DIM, (h + 1) * HEAD_DIM)
        newkv_o[pl.ds(2 * h, ROWS, stride=4), :] = rotate(key[:, cols])
        newkv_o[pl.ds(2 * h + 1, ROWS, stride=4), :] = value[:, cols]

    def untangle(i):
        tmp[...] = pool[pl.ds(i * 1024, 1024), :].astype(F32)
        for j in range(4):
            kvd[pl.ds(i * 256, 256), pl.ds(j * 128, 128)] = tmp[pl.ds(j, 256, stride=4), :].astype(BF16)

    for i in range(4):
        pool_loads[i].wait()
    forwards = []
    for i, dy in enumerate((2, 1, 3, 0)):
        for j in range(SIDE):
            untangle(4 * i + j)
        for dz in range(SIDE):
            if dy or dz:
                q_sends[dy * SIDE + dz].wait_recv()
        forwards.append(forward(dy))
        forwards[-1].start()
    for copy in forwards:
        copy.wait()
    for copy in q_sends.values():
        copy.wait_send()


def request_of(n):
    return ((n >> 4) & 15) * 32 + (n >> 8) * 16 + (n & 15)


def as_bf16(flags):
    return flags.astype(F32).astype(BF16)


def attend_kernel(
    base_s, qall, order, mask, kvd, newkv, pooled, newkv_o,
    scores, order_b, first_b, last_b, out_sem,
):
    leave = pltpu.make_async_copy(newkv, newkv_o, out_sem)
    leave.start()
    base = base_s[0]

    n_lane = [request_of(lax.broadcasted_iota(jnp.int32, (1, 128), 1) + 128 * t) for t in range(4)]
    for t in range(4):
        tile = jnp.broadcast_to(order[t:t + 1, :], (128, 128)).astype(F32)
        order_b[pl.ds(128 * t, 128), :] = jnp.transpose(tile).astype(jnp.int32)
    p_sub = lax.broadcasted_iota(jnp.int32, (REQS, 128), 0)
    here, upto = [], []
    for t in range(4):
        match = order_b[...] == n_lane[t]
        pos = jnp.sum(jnp.where(match, p_sub.astype(F32), 0.0), axis=0, keepdims=True).astype(jnp.int32)
        here.append(as_bf16(match))
        upto.append(as_bf16(pos <= p_sub))
    digits = qall[:, pl.ds(QW, 128)]

    def lengths_by(flags):
        found = jnp.dot(jnp.concatenate(flags, axis=1), digits, preferred_element_type=F32)
        return (found[:, 0:1] * 128.0 + found[:, 1:2]).astype(jnp.int32)

    ends = lengths_by(upto) - base
    starts = ends - lengths_by(here)
    first_b[...] = jnp.broadcast_to(starts, (REQS, 128))
    last_b[...] = jnp.broadcast_to(ends, (REQS, 128))
    low = jnp.sum((ends <= 0).astype(jnp.int32))
    high = jnp.sum((starts < SLOTS).astype(jnp.int32))
    low = (low // 16) * 16
    windows = (high - low + (WIN - 1)) // WIN

    pooled[...] = jnp.zeros_like(pooled)
    slot = lax.broadcasted_iota(jnp.int32, (1, 128), 1)
    ones = jnp.ones((CHUNK, 128), BF16)

    @pl.loop(0, windows)
    def _(w):
        at = pl.multiple_of(jnp.minimum(low + w * WIN, REQS - WIN), 16)
        own = order_b[pl.ds(at, WIN), :]
        pick = jnp.concatenate([as_bf16(own == n_lane[t]) for t in range(4)], axis=1)
        query = jnp.dot(pick, qall[:, pl.ds(0, QW)], preferred_element_type=F32).astype(BF16)
        first = first_b[pl.ds(at, WIN), :]
        last = last_b[pl.ds(at, WIN), :]
        chunk_from = jnp.maximum(jnp.min(first), 0) // CHUNK
        chunk_to = (jnp.minimum(jnp.max(last), SLOTS) + (CHUNK - 1)) // CHUNK
        first = jnp.concatenate([first, first], axis=0)
        last = jnp.concatenate([last, last], axis=0)
        rows = [jnp.concatenate([head(query, 2 * j), head(query, 2 * j + 1)], axis=0) for j in range(2)]

        def score(c, peaks):
            start = pl.multiple_of(c * CHUNK, CHUNK)
            s = [
                lax.dot_general(
                    rows[j], kvd[pl.ds(start, CHUNK), pl.ds(2 * j * 128, 128)],
                    (((1,), (1,)), ((), ())), preferred_element_type=F32,
                )
                for j in range(2)
            ]
            peaks = list(peaks)
            for i in range(CHUNK // 128):
                live = mask[pl.ds(c * (CHUNK // 128) + i, 1), :] == 1
                index = jnp.where(live, slot + (start + i * 128), -REQS * 8192)
                ok = (index >= first) & (index < last)
                for j in range(2):
                    found = jnp.where(ok, s[j][:, i * 128:(i + 1) * 128], FLOOR)
                    scores[j, :, pl.ds(pl.multiple_of(start + i * 128, 128), 128)] = found
                    peaks[j] = jnp.maximum(peaks[j], found)
            return tuple(peaks)

        least = jnp.full((2 * WIN, 128), FLOOR, F32)
        peaks = lax.fori_loop(chunk_from, chunk_to, score, (least, least))
        peaks = [jnp.max(peak, axis=1, keepdims=True) for peak in peaks]
        peaks = [jnp.where(peak > 0.5 * FLOOR, peak, 0.0) for peak in peaks]

        def weigh(c, sums):
            start = pl.multiple_of(c * CHUNK, CHUNK)
            out = []
            for j in range(2):
                weight = jnp.exp2((scores[j, :, pl.ds(start, CHUNK)] - peaks[j]) * (SCALE * LOG2E)).astype(BF16)
                values = kvd[pl.ds(start, CHUNK), pl.ds((2 * j + 1) * 128, 128)]
                both = jnp.concatenate([values, ones], axis=1)
                out.append(sums[j] + jnp.dot(weight, both, preferred_element_type=F32))
            return tuple(out)

        zero = jnp.zeros((2 * WIN, 256), F32)
        sums = lax.fori_loop(chunk_from, chunk_to, weigh, (zero, zero))
        top, totals = [], []
        for j in range(2):
            total = sums[j][:, 128:]
            mean = (sums[j][:, :128] / jnp.where(total > 0.0, total, 1.0)).astype(BF16)
            for g in range(2):
                h, part_rows = 2 * j + g, slice(g * WIN, (g + 1) * WIN)
                pooled[pl.ds(at, WIN), pl.ds(h * HEAD_DIM, HEAD_DIM)] = mean[part_rows]
                top.append(jnp.broadcast_to(peaks[j][part_rows] * SCALE, (WIN, 128)))
                totals.append(total[part_rows])
        pooled[pl.ds(at, WIN), pl.ds(QW, 128)] = stats_of(top, totals)

    leave.wait()


def pack_stats(stats):
    lane = lax.broadcasted_iota(jnp.int32, stats.shape, 1)
    top = stats.astype(BF16).astype(F32)
    rest = stats - top
    middle = rest.astype(BF16).astype(F32)
    rest = rest - middle
    kept = jnp.where(lane < 8, top, jnp.where(lane < 16, middle, jnp.where(lane < 24, rest, 0.0)))
    return kept.astype(BF16)


def stats_of(peaks, totals):
    value = lax.broadcasted_iota(jnp.int32, peaks[0].shape, 1) & 7
    stats = jnp.zeros(peaks[0].shape, F32)
    for h in range(4):
        stats = jnp.where(value == h, peaks[h], stats)
        stats = jnp.where(value == 4 + h, totals[h], stats)
    return pack_stats(stats)


def spreader():
    value = lax.broadcasted_iota(jnp.int32, (128, 2 * QW), 0)
    column = lax.broadcasted_iota(jnp.int32, (128, 2 * QW), 1)
    return ((value < 24) & ((value & 7) == (column >> 7))).astype(F32).astype(BF16)


def head(block, h):
    return block[:, h * HEAD_DIM:(h + 1) * HEAD_DIM]


def finish_kernel(
    pooled, order, qown, newkv, tok, gain, wo_h, wg_h, wu_h, wd_h, out,
    part, came, comb, rx, mix, down, spread, left_stats, right_stats, wo, wg, wu, wd,
    w_sem, p_sem, cs_sem, cr_sem, ms_sem, mr_sem, ds_sem, dr_sem,
):
    core, y, z, tp = place()
    chip = y * SIDE + z
    barrier = pltpu.get_barrier_semaphore()
    sibling = device(chip, 1 - core, tp)
    peers = [sibling] + [device(chip_at(y, z, k), core, tp) for k in range(1, CHIPS)]
    beside = [device(chip, core, lax.rem(tp + d, 4)) for d in range(1, 4)]
    for peer in peers + beside:
        pl.semaphore_signal(barrier, inc=1, device_id=peer, device_id_type=MESH)
    loads = [
        pltpu.make_async_copy(src, dst, w_sem.at[i])
        for i, (src, dst) in enumerate(((wo_h, wo), (wg_h, wg), (wu_h, wu), (wd_h, wd)))
    ]
    for copy in loads:
        copy.start()
    n_sub = request_of(lax.broadcasted_iota(jnp.int32, (REQS, 128), 0))
    place_n = jnp.concatenate([as_bf16(order[t:t + 1, :] == n_sub) for t in range(4)], axis=1)
    part[...] = jnp.dot(place_n, pooled[...], preferred_element_type=F32).astype(BF16)
    spread[...] = spreader()
    half = pl.multiple_of(core * HALF, HALF)
    left_stats[...] = jnp.dot(part[pl.ds(half, HALF), pl.ds(QW, 128)], spread[...], preferred_element_type=F32)
    own_peaks, own_values = [], []
    for h in range(4):
        keys = newkv[pl.ds(2 * (h // 2), ROWS, stride=4), :].astype(BF16).astype(F32)
        query = head(qown[...], h).astype(F32)
        score = jnp.sum(query * keys, axis=1, keepdims=True) * SCALE
        own_peaks.append(jnp.broadcast_to(score, (ROWS, HEAD_DIM)))
        own_values.append(newkv[pl.ds(2 * (h // 2) + 1, ROWS, stride=4), :].astype(BF16).astype(F32))
    pl.semaphore_wait(barrier, len(peers) + len(beside))

    def rows_of(dy):
        return pl.multiple_of(lax.rem(y + dy, SIDE) * 64, 64)

    turns = (2, 1, 3, 0)
    swap = pltpu.make_async_remote_copy(
        src_ref=part.at[pl.ds(pl.multiple_of(HALF - half, HALF), HALF)], dst_ref=came,
        send_sem=p_sem.at[0], recv_sem=p_sem.at[1], device_id=sibling, device_id_type=MESH,
    )
    swap.start()
    swap.wait_recv()
    right_stats[...] = jnp.dot(came[:, pl.ds(QW, 128)], spread[...], preferred_element_type=F32)

    def stat(ref, rows, h):
        totals = ref[rows, pl.ds(QW + h * HEAD_DIM, HEAD_DIM)]
        return jnp.where(totals > 0.0, ref[rows, pl.ds(h * HEAD_DIM, HEAD_DIM)], FLOOR), totals

    sends = []
    for dy in turns:
        rows = pl.ds(rows_of(dy), 64)
        mine = pl.ds(pl.multiple_of(half + rows_of(dy), 64), 64)
        peaks, totals = [], []
        for h in range(4):
            cols = pl.ds(h * HEAD_DIM, HEAD_DIM)
            peak_a, total_a = stat(left_stats, rows, h)
            peak_b, total_b = stat(right_stats, rows, h)
            peak = jnp.maximum(peak_a, peak_b)
            left = total_a * jnp.exp(peak_a - peak)
            right = total_b * jnp.exp(peak_b - peak)
            total = left + right
            summed = part[mine, cols].astype(F32) * left + came[rows, cols].astype(F32) * right
            comb[rows, cols] = (summed / jnp.where(total > 0.0, total, 1.0)).astype(BF16)
            peaks.append(jnp.where(total > 0.0, peak, 0.0))
            totals.append(total)
        comb[rows, pl.ds(QW, 128)] = stats_of(peaks, totals)
        for dz in (2, 1, 3, 0):
            k = dy * SIDE + dz
            if k == 0:
                continue
            block = comb.at[pl.ds(pl.multiple_of(chip_at(y, z, k) * ROWS, ROWS), ROWS)]
            sends.append(
                pltpu.make_async_remote_copy(
                    src_ref=block, dst_ref=rx.at[k], send_sem=cs_sem.at[k], recv_sem=cr_sem.at[k],
                    device_id=peers[k], device_id_type=MESH,
                )
            )
            sends[-1].start()
    rx[0] = comb[pl.ds(pl.multiple_of(chip * ROWS, ROWS), ROWS), :]

    for copy in sends:
        copy.wait_recv()
    found = [rx[k, :, pl.ds(QW, 128)] for k in range(CHIPS)]
    left_stats[...] = jnp.dot(jnp.concatenate(found, axis=0), spread[...], preferred_element_type=F32)
    context = []
    for h in range(4):
        cols = pl.ds(h * HEAD_DIM, HEAD_DIM)
        stats = [stat(left_stats, pl.ds(k * ROWS, ROWS), h) for k in range(CHIPS)]
        peak = own_peaks[h]
        for other, _ in stats:
            peak = jnp.maximum(peak, other)
        total = jnp.exp(own_peaks[h] - peak)
        summed = total * own_values[h]
        for k in range(CHIPS):
            weight = stats[k][1] * jnp.exp(stats[k][0] - peak)
            total = total + weight
            summed = summed + weight * rx[k, :, cols].astype(F32)
        context.append((summed / total).astype(BF16))
    context = jnp.concatenate(context, axis=1)

    def over_tp(left, right, width, terms, send, recv):
        copies = []
        for n in range(4):
            cols = pl.ds(n * width, width)
            terms[tp, :, cols] = jnp.dot(left, right[:, cols], preferred_element_type=F32).astype(BF16)
            for d in range(3):
                ref = terms.at[tp, :, cols]
                copies.append(
                    pltpu.make_async_remote_copy(
                        src_ref=ref, dst_ref=ref, send_sem=send.at[n, d], recv_sem=recv.at[n, d],
                        device_id=beside[d], device_id_type=MESH,
                    )
                )
                copies[-1].start()
        return copies

    def summed_terms(terms):
        total = terms[0].astype(F32)
        for t in range(1, 4):
            total = total + terms[t].astype(F32)
        return total

    loads[0].wait()
    mixes = over_tp(context, wo, 512, mix, ms_sem, mr_sem)
    for copy in mixes:
        copy.wait_recv()
    mid = tok[...].astype(F32) + summed_terms(mix)
    normed = rms_norm(mid, gain[...])
    loads[1].wait()
    loads[2].wait()
    acts = []
    for n in range(2):
        cols = pl.ds(n * 512, 512)
        gate = jnp.dot(normed, wg[:, cols], preferred_element_type=F32)
        upper = jnp.dot(normed, wu[:, cols], preferred_element_type=F32)
        acts.append((gate / (1.0 + jnp.exp(-gate)) * upper).astype(BF16))
    act = jnp.concatenate(acts, axis=1)
    loads[3].wait()
    downs = over_tp(act, wd, 512, down, ds_sem, dr_sem)
    for copy in downs:
        copy.wait_recv()
    out[...] = mid + summed_terms(down)
    for copy in [swap] + sends + mixes + downs:
        copy.wait_send()


def per_device(
    tokens, lengths, pool_order, positions, slot_mask, kv_cache, attn_gain,
    w_query, w_key, w_value, w_out, ffn_gain, w_gate, w_up, w_down,
):
    def stay(*arrays):
        return [pltpu.with_memory_space_constraint(a, pltpu.HBM) for a in arrays]

    vmem = pl.BlockSpec(memory_space=pltpu.VMEM)
    smem = pl.BlockSpec(memory_space=pltpu.SMEM)
    hbm = pl.BlockSpec(memory_space=pltpu.HBM)
    dma = pltpu.SemaphoreType.DMA
    pool = kv_cache.reshape(SLOTS, 2, 2, HEAD_DIM).transpose(0, 2, 1, 3).reshape(4 * SLOTS, HEAD_DIM)
    qall, qown, newkv, kvd = pl.pallas_call(
        project_kernel,
        out_shape=(
            jax.ShapeDtypeStruct((REQS, PW), BF16),
            jax.ShapeDtypeStruct((ROWS, QW), BF16),
            jax.ShapeDtypeStruct((4 * ROWS, HEAD_DIM), F32),
            jax.ShapeDtypeStruct((SLOTS, QW), BF16),
        ),
        in_specs=[hbm] * 9,
        out_specs=(vmem,) * 4,
        scratch_shapes=[
            pltpu.SMEM((ROWS,), jnp.int32),
            pltpu.SMEM((ROWS,), jnp.int32),
            pltpu.VMEM((ROWS, 2048), BF16),
            pltpu.VMEM((16, 128), BF16),
            pltpu.VMEM((8, 128), F32),
            pltpu.VMEM((2048, 512), BF16),
            pltpu.VMEM((2048, 256), BF16),
            pltpu.VMEM((2048, 256), BF16),
            pltpu.VMEM((4 * SLOTS, HEAD_DIM), BF16),
            pltpu.VMEM((1024, HEAD_DIM), F32),
            dma((5,)), dma((3,)), dma((4,)), dma((16,)), dma((16,)), dma((4,)), dma((4,)),
        ],
        compiler_params=pltpu.CompilerParams(
            collective_id=0, has_side_effects=True, vmem_limit_bytes=40 << 20
        ),
        name="project",
    )(
        *stay(
            lengths, positions, tokens, attn_gain.reshape(16, 128), jnp.asarray(frequency_table()),
            w_query, w_key, w_value, pool,
        )
    )
    base = (lax.axis_index("req") * SLOTS).astype(jnp.int32).reshape(1)
    part, new_kv = pl.pallas_call(
        attend_kernel,
        out_shape=(
            jax.ShapeDtypeStruct((REQS, PW), BF16),
            pltpu.HBM((4 * ROWS, HEAD_DIM), F32),
        ),
        in_specs=[smem, vmem, vmem, vmem, vmem, vmem],
        out_specs=(vmem, hbm),
        scratch_shapes=[
            pltpu.VMEM((2, 2 * WIN, SLOTS), F32),
            pltpu.VMEM((REQS, 128), jnp.int32),
            pltpu.VMEM((REQS, 128), jnp.int32),
            pltpu.VMEM((REQS, 128), jnp.int32),
            dma,
        ],
        compiler_params=pltpu.CompilerParams(vmem_limit_bytes=40 << 20),
        name="attend",
    )(base, qall, pool_order.reshape(4, 128), slot_mask.reshape(32, 128), kvd, newkv)
    hidden = pl.pallas_call(
        finish_kernel,
        out_shape=jax.ShapeDtypeStruct((ROWS, 2048), F32),
        in_specs=[vmem] * 6 + [hbm] * 4,
        out_specs=vmem,
        scratch_shapes=[
            pltpu.VMEM((REQS, PW), BF16),
            pltpu.VMEM((HALF, PW), BF16),
            pltpu.VMEM((HALF, PW), BF16),
            pltpu.VMEM((CHIPS, ROWS, PW), BF16),
            pltpu.VMEM((4, ROWS, 2048), BF16),
            pltpu.VMEM((4, ROWS, 2048), BF16),
            pltpu.VMEM((128, 2 * QW), BF16),
            pltpu.VMEM((HALF, 2 * QW), F32),
            pltpu.VMEM((HALF, 2 * QW), F32),
            pltpu.VMEM((512, 2048), BF16),
            pltpu.VMEM((2048, 1024), BF16),
            pltpu.VMEM((2048, 1024), BF16),
            pltpu.VMEM((1024, 2048), BF16),
            dma((4,)), dma((2,)), dma((16,)), dma((16,)),
            dma((4, 3)), dma((4, 3)), dma((4, 3)), dma((4, 3)),
        ],
        compiler_params=pltpu.CompilerParams(
            collective_id=1, has_side_effects=True, vmem_limit_bytes=40 << 20
        ),
        name="finish",
    )(part, pool_order.reshape(4, 128), qown, newkv, tokens, ffn_gain.reshape(16, 128), *stay(w_out, w_gate, w_up, w_down))
    new_kv = new_kv.reshape(ROWS, 2, 2, HEAD_DIM).transpose(0, 2, 1, 3).reshape(ROWS, 2, 256)
    return hidden, new_kv


def solution(mesh):
    placed = (
        P("req", None), P("req"), P(), P("req"), P("req"), P("req", None, "tp"), P(),
        P(None, "tp"), P(None, "tp"), P(None, "tp"), P("tp", None), P(),
        P(None, "tp"), P(None, "tp"), P("tp", None),
    )
    return jax.shard_map(
        per_device,
        mesh=mesh,
        in_specs=placed,
        out_specs=(P("req", None), P("req", None, "tp")),
        check_vma=False,
    )
```

```python
import functools
import math

import jax
import jax.numpy as jnp
import numpy as np
from jax import lax
from jax.experimental import pallas as pl
from jax.experimental.pallas import tpu as pltpu
from jax.sharding import PartitionSpec as P

MESH = pl.DeviceIdType.MESH
HEAD_DIM = 128
ROPE_BASE = 1000000.0
EPS = 1e-05
FLOOR = -1e30
SCALE = 1.0 / math.sqrt(HEAD_DIM)
SIDE = 4
CHIPS = SIDE * SIDE
ROWS = 16
REQS = 512
SLOTS = 4096
HALF = REQS // 2
QW = 512
PW = QW + 128
WIN = 64
CHUNK = 2048
PARTS = 4
WIDTH = 2048 // PARTS
TP_ORDER = (1, 0, 2)
LOG2E = 1.4426950408889634
BF16 = jnp.bfloat16
F32 = jnp.float32


def place():
    me = lax.axis_index("req")
    core = lax.rem(me, 2)
    chip = me // 2
    return core, chip // SIDE, lax.rem(chip, SIDE), lax.axis_index("tp")


def chip_at(y, z, k):
    return lax.rem(y + k // SIDE, SIDE) * SIDE + lax.rem(z + k % SIDE, SIDE)


def device(chip, core, tp):
    return {"req": chip * 2 + core, "tp": tp}


def rms_norm(rows, gain):
    scale = lax.rsqrt(jnp.mean(rows * rows, axis=-1, keepdims=True) + EPS)
    gain = gain.astype(F32)
    tiles = [rows[:, i * 128:(i + 1) * 128] * scale * gain[i:i + 1, :] for i in range(gain.shape[0])]
    return jnp.concatenate(tiles, axis=1).astype(BF16)


def frequency_table():
    half = HEAD_DIM // 2
    turns = ROPE_BASE ** (-(np.arange(half, dtype=np.float64) * 2.0) / HEAD_DIM) / (2.0 * np.pi)
    first = np.round(turns * 2.0**12) / 2.0**12
    second = np.round((turns - first) * 2.0**23) / 2.0**23
    third = turns - first - second
    table = np.zeros((8, HEAD_DIM), np.float64)
    for i, term in enumerate((first, second, third)):
        table[i] = np.concatenate([term, term])
    return table.astype(np.float32)


def cos_sin(where, table):
    turn = where * table[0:1, :]
    turn = turn - jnp.floor(turn + 0.5)
    turn = turn + where * table[1:2, :]
    turn = turn - jnp.floor(turn + 0.5)
    turn = turn + where * table[2:3, :]
    quarter = jnp.floor(turn * 4.0 + 0.5)
    x = (turn - quarter * 0.25) * np.float32(2.0 * np.pi)
    sq = x * x
    sine = x * (1.0 + sq * (-1.0 / 6 + sq * (1.0 / 120 + sq * (-1.0 / 5040 + sq * (1.0 / 362880)))))
    cosine = 1.0 + sq * (
        -0.5 + sq * (1.0 / 24 + sq * (-1.0 / 720 + sq * (1.0 / 40320 + sq * (-1.0 / 3628800))))
    )
    odd = (quarter == 1.0) | (quarter == -1.0)
    far = (quarter == 2.0) | (quarter == -2.0)
    c = jnp.where(odd, -quarter * sine, jnp.where(far, -cosine, cosine))
    s = jnp.where(odd, quarter * cosine, jnp.where(far, -sine, sine))
    return c, s


def project_kernel(
    len_h, pos_h, tok_h, gain_h, table_h, wq_h, wk_h, wv_h, pool_h,
    qall, qown_o, newkv_o, kvd,
    len_s, pos_s, tok, gain, table, wq, wk, wv, pool, tmp,
    s_sem, w_sem, pool_sem, qs_sem, qr_sem, fs_sem, fr_sem,
):
    core, y, z, tp = place()
    chip = y * SIDE + z
    small = [
        pltpu.make_async_copy(src, dst, s_sem.at[i])
        for i, (src, dst) in enumerate(
            ((len_h, len_s), (pos_h, pos_s), (table_h, table), (tok_h, tok), (gain_h, gain))
        )
    ]
    loads = [
        pltpu.make_async_copy(src, dst, w_sem.at[i])
        for i, (src, dst) in enumerate(((wq_h, wq), (wk_h, wk), (wv_h, wv)))
    ]
    piece = 4 * SLOTS // 4
    pool_loads = [
        pltpu.make_async_copy(pool_h.at[pl.ds(i * piece, piece)], pool.at[pl.ds(i * piece, piece)], pool_sem.at[i])
        for i in range(4)
    ]
    for copy in small + loads + pool_loads:
        copy.start()

    barrier = pltpu.get_barrier_semaphore()
    sibling = device(chip, 1 - core, tp)
    peers = [sibling] + [device(chip_at(y, z, k), core, tp) for k in range(1, CHIPS)]
    for peer in peers:
        pl.semaphore_signal(barrier, inc=1, device_id=peer, device_id_type=MESH)

    for copy in small:
        copy.wait()
    row = lax.broadcasted_iota(jnp.int32, (ROWS, 128), 0)
    lane = lax.broadcasted_iota(jnp.int32, (ROWS, 128), 1)
    where = jnp.zeros((ROWS, 128), jnp.int32)
    digits = jnp.zeros((ROWS, 128), jnp.int32)
    for i in range(ROWS):
        where = jnp.where(row == i, pos_s[i], where)
        digits = jnp.where(row == i, len_s[i], digits)
    digits = jnp.where(lane == 0, digits >> 7, jnp.where(lane == 1, digits & 127, 0)).astype(F32).astype(BF16)
    cosine, sine = cos_sin(where.astype(F32), table[...])
    sine = jnp.where(lane < HEAD_DIM // 2, -sine, sine)

    def rotate(vectors):
        return vectors * cosine + pltpu.roll(vectors, HEAD_DIM // 2, axis=1) * sine

    normed = rms_norm(tok[...].astype(F32), gain[...])

    pl.semaphore_wait(barrier, len(peers))
    loads[0].wait()
    query = jnp.dot(normed, wq[...], preferred_element_type=F32)
    mine_at = pl.multiple_of(core * HALF + chip * ROWS, ROWS)
    for h in range(QW // HEAD_DIM):
        cols = pl.ds(h * HEAD_DIM, HEAD_DIM)
        turned = rotate(query[:, h * HEAD_DIM:(h + 1) * HEAD_DIM]).astype(BF16)
        qall[pl.ds(mine_at, ROWS), cols] = turned
        qown_o[:, cols] = turned
    qall[pl.ds(mine_at, ROWS), pl.ds(QW, 128)] = digits
    my_rows = qall.at[pl.ds(mine_at, ROWS)]
    q_sends = {}
    for k in range(1, CHIPS):
        q_sends[k] = pltpu.make_async_remote_copy(
            src_ref=my_rows, dst_ref=my_rows, send_sem=qs_sem.at[k], recv_sem=qr_sem.at[k],
            device_id=peers[k], device_id_type=MESH,
        )
    far_first = (10, 9, 11, 8, 6, 5, 7, 4, 14, 13, 15, 12, 2, 1, 3)
    for k in far_first:
        q_sends[k].start()

    def forward(dy):
        source = lax.rem(y + SIDE - dy, SIDE) * SIDE * ROWS
        rows = qall.at[pl.ds(pl.multiple_of(core * HALF + source, SIDE * ROWS), SIDE * ROWS)]
        return pltpu.make_async_remote_copy(
            src_ref=rows, dst_ref=rows, send_sem=fs_sem.at[dy], recv_sem=fr_sem.at[dy],
            device_id=sibling, device_id_type=MESH,
        )

    loads[1].wait()
    key = jnp.dot(normed, wk[...], preferred_element_type=F32)
    loads[2].wait()
    value = jnp.dot(normed, wv[...], preferred_element_type=F32)
    for h in range(2):
        cols = slice(h * HEAD_DIM, (h + 1) * HEAD_DIM)
        newkv_o[pl.ds(2 * h, ROWS, stride=4), :] = rotate(key[:, cols])
        newkv_o[pl.ds(2 * h + 1, ROWS, stride=4), :] = value[:, cols]

    def untangle(i):
        tmp[...] = pool[pl.ds(i * 1024, 1024), :].astype(F32)
        for j in range(4):
            kvd[pl.ds(i * 256, 256), pl.ds(j * 128, 128)] = tmp[pl.ds(j, 256, stride=4), :].astype(BF16)

    for i in range(4):
        pool_loads[i].wait()
    forwards = []
    for i, dy in enumerate((2, 1, 3, 0)):
        for j in range(SIDE):
            untangle(4 * i + j)
        for dz in range(SIDE):
            if dy or dz:
                q_sends[dy * SIDE + dz].wait_recv()
        forwards.append(forward(dy))
        forwards[-1].start()
    for copy in forwards:
        copy.wait()
    for copy in q_sends.values():
        copy.wait_send()


def request_of(n):
    return ((n >> 4) & 15) * 32 + (n >> 8) * 16 + (n & 15)


def as_bf16(flags):
    return flags.astype(F32).astype(BF16)


def attend_kernel(
    base_s, qall, order, mask, kvd, newkv, pooled, newkv_o,
    scores, order_b, first_b, last_b, out_sem,
):
    leave = pltpu.make_async_copy(newkv, newkv_o, out_sem)
    leave.start()
    base = base_s[0]

    n_lane = [request_of(lax.broadcasted_iota(jnp.int32, (1, 128), 1) + 128 * t) for t in range(4)]
    for t in range(4):
        tile = jnp.broadcast_to(order[t:t + 1, :], (128, 128)).astype(F32)
        order_b[pl.ds(128 * t, 128), :] = jnp.transpose(tile).astype(jnp.int32)
    p_sub = lax.broadcasted_iota(jnp.int32, (REQS, 128), 0)
    here, upto = [], []
    for t in range(4):
        match = order_b[...] == n_lane[t]
        pos = jnp.sum(jnp.where(match, p_sub.astype(F32), 0.0), axis=0, keepdims=True).astype(jnp.int32)
        here.append(as_bf16(match))
        upto.append(as_bf16(pos <= p_sub))
    digits = qall[:, pl.ds(QW, 128)]

    def lengths_by(flags):
        found = jnp.dot(jnp.concatenate(flags, axis=1), digits, preferred_element_type=F32)
        return (found[:, 0:1] * 128.0 + found[:, 1:2]).astype(jnp.int32)

    ends = lengths_by(upto) - base
    starts = ends - lengths_by(here)
    first_b[...] = jnp.broadcast_to(starts, (REQS, 128))
    last_b[...] = jnp.broadcast_to(ends, (REQS, 128))
    low = jnp.sum((ends <= 0).astype(jnp.int32))
    high = jnp.sum((starts < SLOTS).astype(jnp.int32))
    low = (low // 16) * 16
    windows = (high - low + (WIN - 1)) // WIN

    pooled[...] = jnp.zeros_like(pooled)
    slot = lax.broadcasted_iota(jnp.int32, (1, 128), 1)
    ones = jnp.ones((CHUNK, 128), BF16)

    @pl.loop(0, windows)
    def _(w):
        at = pl.multiple_of(jnp.minimum(low + w * WIN, REQS - WIN), 16)
        own = order_b[pl.ds(at, WIN), :]
        pick = jnp.concatenate([as_bf16(own == n_lane[t]) for t in range(4)], axis=1)
        query = jnp.dot(pick, qall[:, pl.ds(0, QW)], preferred_element_type=F32).astype(BF16)
        first = first_b[pl.ds(at, WIN), :]
        last = last_b[pl.ds(at, WIN), :]
        chunk_from = jnp.maximum(jnp.min(first), 0) // CHUNK
        chunk_to = (jnp.minimum(jnp.max(last), SLOTS) + (CHUNK - 1)) // CHUNK
        first = jnp.concatenate([first, first], axis=0)
        last = jnp.concatenate([last, last], axis=0)
        rows = [jnp.concatenate([head(query, 2 * j), head(query, 2 * j + 1)], axis=0) for j in range(2)]

        def score(c, peaks):
            start = pl.multiple_of(c * CHUNK, CHUNK)
            s = [
                lax.dot_general(
                    rows[j], kvd[pl.ds(start, CHUNK), pl.ds(2 * j * 128, 128)],
                    (((1,), (1,)), ((), ())), preferred_element_type=F32,
                )
                for j in range(2)
            ]
            peaks = list(peaks)
            for i in range(CHUNK // 128):
                live = mask[pl.ds(c * (CHUNK // 128) + i, 1), :] == 1
                index = jnp.where(live, slot + (start + i * 128), -REQS * 8192)
                ok = (index >= first) & (index < last)
                for j in range(2):
                    found = jnp.where(ok, s[j][:, i * 128:(i + 1) * 128], FLOOR)
                    scores[j, :, pl.ds(pl.multiple_of(start + i * 128, 128), 128)] = found
                    peaks[j] = jnp.maximum(peaks[j], found)
            return tuple(peaks)

        least = jnp.full((2 * WIN, 128), FLOOR, F32)
        peaks = lax.fori_loop(chunk_from, chunk_to, score, (least, least))
        peaks = [jnp.max(peak, axis=1, keepdims=True) for peak in peaks]
        peaks = [jnp.where(peak > 0.5 * FLOOR, peak, 0.0) for peak in peaks]

        def weigh(c, sums):
            start = pl.multiple_of(c * CHUNK, CHUNK)
            out = []
            for j in range(2):
                weight = jnp.exp2((scores[j, :, pl.ds(start, CHUNK)] - peaks[j]) * (SCALE * LOG2E)).astype(BF16)
                values = kvd[pl.ds(start, CHUNK), pl.ds((2 * j + 1) * 128, 128)]
                both = jnp.concatenate([values, ones], axis=1)
                out.append(sums[j] + jnp.dot(weight, both, preferred_element_type=F32))
            return tuple(out)

        zero = jnp.zeros((2 * WIN, 256), F32)
        sums = lax.fori_loop(chunk_from, chunk_to, weigh, (zero, zero))
        top, totals = [], []
        for j in range(2):
            total = sums[j][:, 128:]
            mean = (sums[j][:, :128] / jnp.where(total > 0.0, total, 1.0)).astype(BF16)
            for g in range(2):
                h, part_rows = 2 * j + g, slice(g * WIN, (g + 1) * WIN)
                pooled[pl.ds(at, WIN), pl.ds(h * HEAD_DIM, HEAD_DIM)] = mean[part_rows]
                top.append(jnp.broadcast_to(peaks[j][part_rows] * SCALE, (WIN, 128)))
                totals.append(total[part_rows])
        pooled[pl.ds(at, WIN), pl.ds(QW, 128)] = stats_of(top, totals)

    leave.wait()


def pack_stats(stats):
    lane = lax.broadcasted_iota(jnp.int32, stats.shape, 1)
    top = stats.astype(BF16).astype(F32)
    rest = stats - top
    middle = rest.astype(BF16).astype(F32)
    rest = rest - middle
    kept = jnp.where(lane < 8, top, jnp.where(lane < 16, middle, jnp.where(lane < 24, rest, 0.0)))
    return kept.astype(BF16)


def stats_of(peaks, totals):
    value = lax.broadcasted_iota(jnp.int32, peaks[0].shape, 1) & 7
    stats = jnp.zeros(peaks[0].shape, F32)
    for h in range(4):
        stats = jnp.where(value == h, peaks[h], stats)
        stats = jnp.where(value == 4 + h, totals[h], stats)
    return pack_stats(stats)


def spreader():
    value = lax.broadcasted_iota(jnp.int32, (128, 2 * QW), 0)
    column = lax.broadcasted_iota(jnp.int32, (128, 2 * QW), 1)
    return ((value < 24) & ((value & 7) == (column >> 7))).astype(F32).astype(BF16)


def head(block, h):
    return block[:, h * HEAD_DIM:(h + 1) * HEAD_DIM]


def finish_kernel(
    pooled, order, qown, newkv, tok, gain, wo_h, wg_h, wu_h, wd_h, out,
    part, came, comb, rx, mix, down, spread, left_stats, right_stats, wo, wg, wu, wd,
    w_sem, p_sem, cs_sem, cr_sem, ms_sem, mr_sem, ds_sem, dr_sem,
):
    core, y, z, tp = place()
    chip = y * SIDE + z
    barrier = pltpu.get_barrier_semaphore()
    sibling = device(chip, 1 - core, tp)
    peers = [sibling] + [device(chip_at(y, z, k), core, tp) for k in range(1, CHIPS)]
    beside = [device(chip, core, lax.rem(tp + d, 4)) for d in range(1, 4)]
    for peer in peers + beside:
        pl.semaphore_signal(barrier, inc=1, device_id=peer, device_id_type=MESH)
    loads = [
        pltpu.make_async_copy(src, dst, w_sem.at[i])
        for i, (src, dst) in enumerate(((wo_h, wo), (wg_h, wg), (wu_h, wu), (wd_h, wd)))
    ]
    for copy in loads:
        copy.start()
    n_sub = request_of(lax.broadcasted_iota(jnp.int32, (REQS, 128), 0))
    place_n = jnp.concatenate([as_bf16(order[t:t + 1, :] == n_sub) for t in range(4)], axis=1)
    part[...] = jnp.dot(place_n, pooled[...], preferred_element_type=F32).astype(BF16)
    spread[...] = spreader()
    half = pl.multiple_of(core * HALF, HALF)
    left_stats[...] = jnp.dot(part[pl.ds(half, HALF), pl.ds(QW, 128)], spread[...], preferred_element_type=F32)
    own_peaks, own_values = [], []
    for h in range(4):
        keys = newkv[pl.ds(2 * (h // 2), ROWS, stride=4), :].astype(BF16).astype(F32)
        query = head(qown[...], h).astype(F32)
        score = jnp.sum(query * keys, axis=1, keepdims=True) * SCALE
        own_peaks.append(jnp.broadcast_to(score, (ROWS, HEAD_DIM)))
        own_values.append(newkv[pl.ds(2 * (h // 2) + 1, ROWS, stride=4), :].astype(BF16).astype(F32))
    pl.semaphore_wait(barrier, len(peers) + len(beside))

    def rows_of(dy):
        return pl.multiple_of(lax.rem(y + dy, SIDE) * 64, 64)

    turns = (2, 1, 3, 0)
    swap = pltpu.make_async_remote_copy(
        src_ref=part.at[pl.ds(pl.multiple_of(HALF - half, HALF), HALF)], dst_ref=came,
        send_sem=p_sem.at[0], recv_sem=p_sem.at[1], device_id=sibling, device_id_type=MESH,
    )
    swap.start()
    swap.wait_recv()
    right_stats[...] = jnp.dot(came[:, pl.ds(QW, 128)], spread[...], preferred_element_type=F32)

    def stat(ref, rows, h):
        totals = ref[rows, pl.ds(QW + h * HEAD_DIM, HEAD_DIM)]
        return jnp.where(totals > 0.0, ref[rows, pl.ds(h * HEAD_DIM, HEAD_DIM)], FLOOR), totals

    sends = []
    for dy in turns:
        rows = pl.ds(rows_of(dy), 64)
        mine = pl.ds(pl.multiple_of(half + rows_of(dy), 64), 64)
        peaks, totals = [], []
        for h in range(4):
            cols = pl.ds(h * HEAD_DIM, HEAD_DIM)
            peak_a, total_a = stat(left_stats, rows, h)
            peak_b, total_b = stat(right_stats, rows, h)
            peak = jnp.maximum(peak_a, peak_b)
            left = total_a * jnp.exp(peak_a - peak)
            right = total_b * jnp.exp(peak_b - peak)
            total = left + right
            summed = part[mine, cols].astype(F32) * left + came[rows, cols].astype(F32) * right
            comb[rows, cols] = (summed / jnp.where(total > 0.0, total, 1.0)).astype(BF16)
            peaks.append(jnp.where(total > 0.0, peak, 0.0))
            totals.append(total)
        comb[rows, pl.ds(QW, 128)] = stats_of(peaks, totals)
        for dz in (2, 1, 3, 0):
            k = dy * SIDE + dz
            if k == 0:
                continue
            block = comb.at[pl.ds(pl.multiple_of(chip_at(y, z, k) * ROWS, ROWS), ROWS)]
            sends.append(
                pltpu.make_async_remote_copy(
                    src_ref=block, dst_ref=rx.at[k], send_sem=cs_sem.at[k], recv_sem=cr_sem.at[k],
                    device_id=peers[k], device_id_type=MESH,
                )
            )
            sends[-1].start()
    rx[0] = comb[pl.ds(pl.multiple_of(chip * ROWS, ROWS), ROWS), :]

    for copy in sends:
        copy.wait_recv()
    found = [rx[k, :, pl.ds(QW, 128)] for k in range(CHIPS)]
    left_stats[...] = jnp.dot(jnp.concatenate(found, axis=0), spread[...], preferred_element_type=F32)
    context = []
    for h in range(4):
        cols = pl.ds(h * HEAD_DIM, HEAD_DIM)
        stats = [stat(left_stats, pl.ds(k * ROWS, ROWS), h) for k in range(CHIPS)]
        peak = own_peaks[h]
        for other, _ in stats:
            peak = jnp.maximum(peak, other)
        total = jnp.exp(own_peaks[h] - peak)
        summed = total * own_values[h]
        for k in range(CHIPS):
            weight = stats[k][1] * jnp.exp(stats[k][0] - peak)
            total = total + weight
            summed = summed + weight * rx[k, :, cols].astype(F32)
        context.append((summed / total).astype(BF16))
    context = jnp.concatenate(context, axis=1)

    def over_tp(left, right, terms, send, recv):
        copies = []
        for n in range(PARTS):
            cols = pl.ds(n * WIDTH, WIDTH)
            terms[tp, :, cols] = jnp.dot(left, right[:, cols], preferred_element_type=F32).astype(BF16)
            ref = terms.at[tp, :, cols]
            copies.append([
                pltpu.make_async_remote_copy(
                    src_ref=ref, dst_ref=ref, send_sem=send.at[n, d], recv_sem=recv.at[n, d],
                    device_id=beside[d], device_id_type=MESH,
                )
                for d in TP_ORDER
            ])
            for copy in copies[-1]:
                copy.start()
        return copies

    def summed_terms(first, terms, n):
        cols = pl.ds(n * WIDTH, WIDTH)
        total = first
        for t in range(4):
            total = total + terms[t, :, cols].astype(F32)
        return total

    loads[0].wait()
    mixes = over_tp(context, wo, mix, ms_sem, mr_sem)
    loads[1].wait()
    loads[2].wait()
    mids, squares = [], jnp.zeros((ROWS, 1), F32)
    gate = jnp.zeros((ROWS, 1024), F32)
    upper = jnp.zeros((ROWS, 1024), F32)
    for n in range(PARTS):
        for copy in mixes[n]:
            copy.wait_recv()
        cols = pl.ds(n * WIDTH, WIDTH)
        mid = summed_terms(tok[:, cols].astype(F32), mix, n)
        mids.append(mid)
        squares = squares + jnp.sum(mid * mid, axis=-1, keepdims=True)
        gains = [gain[pl.ds(n * (WIDTH // 128) + i, 1), :] for i in range(WIDTH // 128)]
        scaled = (mid * jnp.concatenate(gains, axis=1).astype(F32)).astype(BF16)
        gate = gate + jnp.dot(scaled, wg[cols, :], preferred_element_type=F32)
        upper = upper + jnp.dot(scaled, wu[cols, :], preferred_element_type=F32)
    scale = lax.rsqrt(squares * (1.0 / 2048) + EPS)
    gate = gate * scale
    act = (gate / (1.0 + jnp.exp(-gate)) * (upper * scale)).astype(BF16)
    loads[3].wait()
    downs = over_tp(act, wd, down, ds_sem, dr_sem)
    for n in range(PARTS):
        for copy in downs[n]:
            copy.wait_recv()
        out[:, pl.ds(n * WIDTH, WIDTH)] = summed_terms(mids[n], down, n)
    for copy in [swap] + sends + sum(mixes + downs, []):
        copy.wait_send()


def per_device(
    tokens, lengths, pool_order, positions, slot_mask, kv_cache, attn_gain,
    w_query, w_key, w_value, w_out, ffn_gain, w_gate, w_up, w_down,
):
    def stay(*arrays):
        return [pltpu.with_memory_space_constraint(a, pltpu.HBM) for a in arrays]

    vmem = pl.BlockSpec(memory_space=pltpu.VMEM)
    smem = pl.BlockSpec(memory_space=pltpu.SMEM)
    hbm = pl.BlockSpec(memory_space=pltpu.HBM)
    dma = pltpu.SemaphoreType.DMA
    pool = kv_cache.reshape(SLOTS, 2, 2, HEAD_DIM).transpose(0, 2, 1, 3).reshape(4 * SLOTS, HEAD_DIM)
    qall, qown, newkv, kvd = pl.pallas_call(
        project_kernel,
        out_shape=(
            jax.ShapeDtypeStruct((REQS, PW), BF16),
            jax.ShapeDtypeStruct((ROWS, QW), BF16),
            jax.ShapeDtypeStruct((4 * ROWS, HEAD_DIM), F32),
            jax.ShapeDtypeStruct((SLOTS, QW), BF16),
        ),
        in_specs=[hbm] * 9,
        out_specs=(vmem,) * 4,
        scratch_shapes=[
            pltpu.SMEM((ROWS,), jnp.int32),
            pltpu.SMEM((ROWS,), jnp.int32),
            pltpu.VMEM((ROWS, 2048), BF16),
            pltpu.VMEM((16, 128), BF16),
            pltpu.VMEM((8, 128), F32),
            pltpu.VMEM((2048, 512), BF16),
            pltpu.VMEM((2048, 256), BF16),
            pltpu.VMEM((2048, 256), BF16),
            pltpu.VMEM((4 * SLOTS, HEAD_DIM), BF16),
            pltpu.VMEM((1024, HEAD_DIM), F32),
            dma((5,)), dma((3,)), dma((4,)), dma((16,)), dma((16,)), dma((4,)), dma((4,)),
        ],
        compiler_params=pltpu.CompilerParams(
            collective_id=0, has_side_effects=True, vmem_limit_bytes=40 << 20
        ),
        name="project",
    )(
        *stay(
            lengths, positions, tokens, attn_gain.reshape(16, 128), jnp.asarray(frequency_table()),
            w_query, w_key, w_value, pool,
        )
    )
    base = (lax.axis_index("req") * SLOTS).astype(jnp.int32).reshape(1)
    part, new_kv = pl.pallas_call(
        attend_kernel,
        out_shape=(
            jax.ShapeDtypeStruct((REQS, PW), BF16),
            pltpu.HBM((4 * ROWS, HEAD_DIM), F32),
        ),
        in_specs=[smem, vmem, vmem, vmem, vmem, vmem],
        out_specs=(vmem, hbm),
        scratch_shapes=[
            pltpu.VMEM((2, 2 * WIN, SLOTS), F32),
            pltpu.VMEM((REQS, 128), jnp.int32),
            pltpu.VMEM((REQS, 128), jnp.int32),
            pltpu.VMEM((REQS, 128), jnp.int32),
            dma,
        ],
        compiler_params=pltpu.CompilerParams(vmem_limit_bytes=40 << 20),
        name="attend",
    )(base, qall, pool_order.reshape(4, 128), slot_mask.reshape(32, 128), kvd, newkv)
    hidden = pl.pallas_call(
        finish_kernel,
        out_shape=jax.ShapeDtypeStruct((ROWS, 2048), F32),
        in_specs=[vmem] * 6 + [hbm] * 4,
        out_specs=vmem,
        scratch_shapes=[
            pltpu.VMEM((REQS, PW), BF16),
            pltpu.VMEM((HALF, PW), BF16),
            pltpu.VMEM((HALF, PW), BF16),
            pltpu.VMEM((CHIPS, ROWS, PW), BF16),
            pltpu.VMEM((4, ROWS, 2048), BF16),
            pltpu.VMEM((4, ROWS, 2048), BF16),
            pltpu.VMEM((128, 2 * QW), BF16),
            pltpu.VMEM((HALF, 2 * QW), F32),
            pltpu.VMEM((HALF, 2 * QW), F32),
            pltpu.VMEM((512, 2048), BF16),
            pltpu.VMEM((2048, 1024), BF16),
            pltpu.VMEM((2048, 1024), BF16),
            pltpu.VMEM((1024, 2048), BF16),
            dma((4,)), dma((2,)), dma((16,)), dma((16,)),
            dma((4, 3)), dma((4, 3)), dma((4, 3)), dma((4, 3)),
        ],
        compiler_params=pltpu.CompilerParams(
            collective_id=1, has_side_effects=True, vmem_limit_bytes=40 << 20
        ),
        name="finish",
    )(part, pool_order.reshape(4, 128), qown, newkv, tokens, ffn_gain.reshape(16, 128), *stay(w_out, w_gate, w_up, w_down))
    new_kv = new_kv.reshape(ROWS, 2, 2, HEAD_DIM).transpose(0, 2, 1, 3).reshape(ROWS, 2, 256)
    return hidden, new_kv


def solution(mesh):
    placed = (
        P("req", None), P("req"), P(), P("req"), P("req"), P("req", None, "tp"), P(),
        P(None, "tp"), P(None, "tp"), P(None, "tp"), P("tp", None), P(),
        P(None, "tp"), P(None, "tp"), P("tp", None),
    )
    return jax.shard_map(
        per_device,
        mesh=mesh,
        in_specs=placed,
        out_specs=(P("req", None), P("req", None, "tp")),
        check_vma=False,
    )
```

```python
import functools
import math

import jax
import jax.numpy as jnp
import numpy as np
from jax import lax
from jax.experimental import pallas as pl
from jax.experimental.pallas import tpu as pltpu
from jax.sharding import PartitionSpec as P

MESH = pl.DeviceIdType.MESH
HEAD_DIM = 128
ROPE_BASE = 1000000.0
EPS = 1e-05
FLOOR = -1e30
SCALE = 1.0 / math.sqrt(HEAD_DIM)
SIDE = 4
CHIPS = SIDE * SIDE
ROWS = 16
REQS = 512
SLOTS = 4096
HALF = REQS // 2
QW = 512
PW = QW + 128
WIN = 64
STEP = 512
CHUNK = 4096
PARTS = 4
WIDTH = 2048 // PARTS
TP_ORDER = (1, 0, 2)
LOG2E = 1.4426950408889634
BF16 = jnp.bfloat16
F32 = jnp.float32


def place():
    me = lax.axis_index("req")
    core = lax.rem(me, 2)
    chip = me // 2
    return core, chip // SIDE, lax.rem(chip, SIDE), lax.axis_index("tp")


def chip_at(y, z, k):
    return lax.rem(y + k // SIDE, SIDE) * SIDE + lax.rem(z + k % SIDE, SIDE)


def device(chip, core, tp):
    return {"req": chip * 2 + core, "tp": tp}


def rms_norm(rows, gain):
    scale = lax.rsqrt(jnp.mean(rows * rows, axis=-1, keepdims=True) + EPS)
    gain = gain.astype(F32)
    tiles = [rows[:, i * 128:(i + 1) * 128] * scale * gain[i:i + 1, :] for i in range(gain.shape[0])]
    return jnp.concatenate(tiles, axis=1).astype(BF16)


def frequency_table():
    half = HEAD_DIM // 2
    turns = ROPE_BASE ** (-(np.arange(half, dtype=np.float64) * 2.0) / HEAD_DIM) / (2.0 * np.pi)
    first = np.round(turns * 2.0**12) / 2.0**12
    second = np.round((turns - first) * 2.0**23) / 2.0**23
    third = turns - first - second
    table = np.zeros((8, HEAD_DIM), np.float64)
    for i, term in enumerate((first, second, third)):
        table[i] = np.concatenate([term, term])
    return table.astype(np.float32)


def cos_sin(where, table):
    turn = where * table[0:1, :]
    turn = turn - jnp.floor(turn + 0.5)
    turn = turn + where * table[1:2, :]
    turn = turn - jnp.floor(turn + 0.5)
    turn = turn + where * table[2:3, :]
    quarter = jnp.floor(turn * 4.0 + 0.5)
    x = (turn - quarter * 0.25) * np.float32(2.0 * np.pi)
    sq = x * x
    sine = x * (1.0 + sq * (-1.0 / 6 + sq * (1.0 / 120 + sq * (-1.0 / 5040 + sq * (1.0 / 362880)))))
    cosine = 1.0 + sq * (
        -0.5 + sq * (1.0 / 24 + sq * (-1.0 / 720 + sq * (1.0 / 40320 + sq * (-1.0 / 3628800))))
    )
    odd = (quarter == 1.0) | (quarter == -1.0)
    far = (quarter == 2.0) | (quarter == -2.0)
    c = jnp.where(odd, -quarter * sine, jnp.where(far, -cosine, cosine))
    s = jnp.where(odd, quarter * cosine, jnp.where(far, -sine, sine))
    return c, s


def project_kernel(
    len_h, pos_h, tok_h, gain_h, table_h, wq_h, wk_h, wv_h, pool_h,
    qall, qown_o, newkv_o, kvd,
    len_s, pos_s, tok, gain, table, wq, wk, wv, pool, tmp,
    s_sem, w_sem, pool_sem, qs_sem, qr_sem, fs_sem, fr_sem, ds_sem, dr_sem,
):
    core, y, z, tp = place()
    chip = y * SIDE + z
    small = [
        pltpu.make_async_copy(src, dst, s_sem.at[i])
        for i, (src, dst) in enumerate(
            ((len_h, len_s), (pos_h, pos_s), (table_h, table), (tok_h, tok), (gain_h, gain))
        )
    ]
    loads = [
        pltpu.make_async_copy(src, dst, w_sem.at[i])
        for i, (src, dst) in enumerate(((wq_h, wq), (wk_h, wk), (wv_h, wv)))
    ]
    piece = 4 * SLOTS // 4
    pool_loads = [
        pltpu.make_async_copy(pool_h.at[pl.ds(i * piece, piece)], pool.at[pl.ds(i * piece, piece)], pool_sem.at[i])
        for i in range(4)
    ]
    for copy in small + loads + pool_loads:
        copy.start()

    barrier = pltpu.get_barrier_semaphore()
    sibling = device(chip, 1 - core, tp)
    peers = [sibling] + [device(chip_at(y, z, k), core, tp) for k in range(1, CHIPS)]
    across = [device(chip_at(y, z, k), 1 - core, tp) for k in range(1, SIDE)]
    for peer in peers + across:
        pl.semaphore_signal(barrier, inc=1, device_id=peer, device_id_type=MESH)

    for copy in small:
        copy.wait()
    row = lax.broadcasted_iota(jnp.int32, (ROWS, 128), 0)
    lane = lax.broadcasted_iota(jnp.int32, (ROWS, 128), 1)
    where = jnp.zeros((ROWS, 128), jnp.int32)
    digits = jnp.zeros((ROWS, 128), jnp.int32)
    for i in range(ROWS):
        where = jnp.where(row == i, pos_s[i], where)
        digits = jnp.where(row == i, len_s[i], digits)
    digits = jnp.where(lane == 0, digits >> 7, jnp.where(lane == 1, digits & 127, 0)).astype(F32).astype(BF16)
    cosine, sine = cos_sin(where.astype(F32), table[...])
    sine = jnp.where(lane < HEAD_DIM // 2, -sine, sine)

    def rotate(vectors):
        return vectors * cosine + pltpu.roll(vectors, HEAD_DIM // 2, axis=1) * sine

    normed = rms_norm(tok[...].astype(F32), gain[...])

    pl.semaphore_wait(barrier, len(peers) + len(across))
    loads[0].wait()
    query = jnp.dot(normed, wq[...], preferred_element_type=F32)
    mine_at = pl.multiple_of(core * HALF + chip * ROWS, ROWS)
    for h in range(QW // HEAD_DIM):
        cols = pl.ds(h * HEAD_DIM, HEAD_DIM)
        turned = rotate(query[:, h * HEAD_DIM:(h + 1) * HEAD_DIM]).astype(BF16)
        qall[pl.ds(mine_at, ROWS), cols] = turned
        qown_o[:, cols] = turned
    qall[pl.ds(mine_at, ROWS), pl.ds(QW, 128)] = digits
    my_rows = qall.at[pl.ds(mine_at, ROWS)]
    q_sends = {}
    for k in range(1, CHIPS):
        q_sends[k] = pltpu.make_async_remote_copy(
            src_ref=my_rows, dst_ref=my_rows, send_sem=qs_sem.at[k], recv_sem=qr_sem.at[k],
            device_id=peers[k], device_id_type=MESH,
        )
    own_forward = pltpu.make_async_remote_copy(
        src_ref=my_rows, dst_ref=my_rows, send_sem=fs_sem.at[0], recv_sem=fr_sem.at[0],
        device_id=sibling, device_id_type=MESH,
    )
    directs = [
        pltpu.make_async_remote_copy(
            src_ref=my_rows, dst_ref=my_rows, send_sem=ds_sem.at[k], recv_sem=dr_sem.at[k],
            device_id=across[k - 1], device_id_type=MESH,
        )
        for k in range(1, SIDE)
    ]
    for k in (10, 9, 11, 8, 6, 5, 7, 4, 14, 13, 15, 12):
        q_sends[k].start()
    own_forward.start()
    for k in (2, 1, 3):
        directs[k - 1].start()
        q_sends[k].start()

    def forward(dy):
        source = lax.rem(y + SIDE - dy, SIDE) * SIDE * ROWS
        rows = qall.at[pl.ds(pl.multiple_of(core * HALF + source, SIDE * ROWS), SIDE * ROWS)]
        return pltpu.make_async_remote_copy(
            src_ref=rows, dst_ref=rows, send_sem=fs_sem.at[dy], recv_sem=fr_sem.at[dy],
            device_id=sibling, device_id_type=MESH,
        )

    loads[1].wait()
    key = jnp.dot(normed, wk[...], preferred_element_type=F32)
    loads[2].wait()
    value = jnp.dot(normed, wv[...], preferred_element_type=F32)
    for h in range(2):
        cols = slice(h * HEAD_DIM, (h + 1) * HEAD_DIM)
        newkv_o[pl.ds(2 * h, ROWS, stride=4), :] = rotate(key[:, cols])
        newkv_o[pl.ds(2 * h + 1, ROWS, stride=4), :] = value[:, cols]

    def untangle(i):
        tmp[...] = pool[pl.ds(i * 1024, 1024), :].astype(F32)
        for j in range(4):
            kvd[pl.ds(i * 256, 256), pl.ds(j * 128, 128)] = tmp[pl.ds(j, 256, stride=4), :].astype(BF16)

    for i in range(4):
        pool_loads[i].wait()
    forwards = []
    for i, dy in enumerate((2, 1, 3, 0)):
        for j in range(SIDE):
            untangle(4 * i + j)
        for dz in range(SIDE):
            if dy:
                q_sends[dy * SIDE + dz].wait_recv()
        if dy:
            forwards.append(forward(dy))
            forwards[-1].start()
    for copy in forwards:
        copy.wait()
    own_forward.wait()
    for copy in directs:
        copy.wait()
    for k in range(1, SIDE):
        q_sends[k].wait_recv()
    for copy in q_sends.values():
        copy.wait_send()


def request_of(n):
    return ((n >> 4) & 15) * 32 + (n >> 8) * 16 + (n & 15)


def as_bf16(flags):
    return flags.astype(F32).astype(BF16)


def attend_kernel(
    base_s, qall, order, mask, kvd, newkv, pooled, newkv_o,
    scores, order_b, first_b, last_b, out_sem,
):
    leave = pltpu.make_async_copy(newkv, newkv_o, out_sem)
    leave.start()
    base = base_s[0]

    n_lane = [request_of(lax.broadcasted_iota(jnp.int32, (1, 128), 1) + 128 * t) for t in range(4)]
    for t in range(4):
        tile = jnp.broadcast_to(order[t:t + 1, :], (128, 128)).astype(F32)
        order_b[pl.ds(128 * t, 128), :] = jnp.transpose(tile).astype(jnp.int32)
    p_sub = lax.broadcasted_iota(jnp.int32, (REQS, 128), 0)
    here, upto = [], []
    for t in range(4):
        match = order_b[...] == n_lane[t]
        pos = jnp.sum(jnp.where(match, p_sub.astype(F32), 0.0), axis=0, keepdims=True).astype(jnp.int32)
        here.append(as_bf16(match))
        upto.append(as_bf16(pos <= p_sub))
    digits = qall[:, pl.ds(QW, 128)]

    def lengths_by(flags):
        found = jnp.dot(jnp.concatenate(flags, axis=1), digits, preferred_element_type=F32)
        return (found[:, 0:1] * 128.0 + found[:, 1:2]).astype(jnp.int32)

    ends = lengths_by(upto) - base
    starts = ends - lengths_by(here)
    first_b[...] = jnp.broadcast_to(starts, (REQS, 128))
    last_b[...] = jnp.broadcast_to(ends, (REQS, 128))
    low = jnp.sum((ends <= 0).astype(jnp.int32))
    high = jnp.sum((starts < SLOTS).astype(jnp.int32))
    low = (low // 16) * 16
    windows = (high - low + (WIN - 1)) // WIN

    pooled[...] = jnp.zeros_like(pooled)
    slot = lax.broadcasted_iota(jnp.int32, (1, 128), 1)
    ones = jnp.ones((STEP, 128), BF16)

    @pl.loop(0, windows)
    def _(w):
        at = pl.multiple_of(jnp.minimum(low + w * WIN, REQS - WIN), 16)
        own = order_b[pl.ds(at, WIN), :]
        pick = jnp.concatenate([as_bf16(own == n_lane[t]) for t in range(4)], axis=1)
        query = jnp.dot(pick, qall[:, pl.ds(0, QW)], preferred_element_type=F32).astype(BF16)
        first = first_b[pl.ds(at, WIN), :]
        last = last_b[pl.ds(at, WIN), :]
        chunk_from = jnp.maximum(jnp.min(first), 0) // CHUNK
        chunk_to = (jnp.minimum(jnp.max(last), SLOTS) + (CHUNK - 1)) // CHUNK
        first = jnp.concatenate([first, first], axis=0)
        last = jnp.concatenate([last, last], axis=0)
        rows = [jnp.concatenate([head(query, 2 * j), head(query, 2 * j + 1)], axis=0) for j in range(2)]

        def score(c, peaks):
            start = pl.multiple_of(c * CHUNK, CHUNK)
            peaks = list(peaks)
            for n in range(CHUNK // STEP):
                at_n = pl.multiple_of(start + n * STEP, STEP)
                oks = []
                for i in range(STEP // 128):
                    live = mask[pl.ds(c * (CHUNK // 128) + n * (STEP // 128) + i, 1), :] == 1
                    index = jnp.where(live, slot + (at_n + i * 128), -REQS * 8192)
                    oks.append((index >= first) & (index < last))
                for j in range(2):
                    s = lax.dot_general(
                        rows[j], kvd[pl.ds(at_n, STEP), pl.ds(2 * j * 128, 128)],
                        (((1,), (1,)), ((), ())), preferred_element_type=F32,
                    )
                    for i in range(STEP // 128):
                        found = jnp.where(oks[i], s[:, i * 128:(i + 1) * 128], FLOOR)
                        scores[j, :, pl.ds(pl.multiple_of(at_n + i * 128, 128), 128)] = found
                        peaks[j] = jnp.maximum(peaks[j], found)
            return tuple(peaks)

        least = jnp.full((2 * WIN, 128), FLOOR, F32)
        peaks = lax.fori_loop(chunk_from, chunk_to, score, (least, least))
        peaks = [jnp.max(peak, axis=1, keepdims=True) for peak in peaks]
        peaks = [jnp.where(peak > 0.5 * FLOOR, peak, 0.0) for peak in peaks]

        def weigh(c, sums):
            start = pl.multiple_of(c * CHUNK, CHUNK)
            sums = list(sums)
            for n in range(CHUNK // STEP):
                at_n = pl.multiple_of(start + n * STEP, STEP)
                for j in range(2):
                    weight = jnp.exp2((scores[j, :, pl.ds(at_n, STEP)] - peaks[j]) * (SCALE * LOG2E)).astype(BF16)
                    values = kvd[pl.ds(at_n, STEP), pl.ds((2 * j + 1) * 128, 128)]
                    both = jnp.concatenate([values, ones], axis=1)
                    sums[j] = sums[j] + jnp.dot(weight, both, preferred_element_type=F32)
            return tuple(sums)

        zero = jnp.zeros((2 * WIN, 256), F32)
        sums = lax.fori_loop(chunk_from, chunk_to, weigh, (zero, zero))
        top, totals = [], []
        for j in range(2):
            total = sums[j][:, 128:]
            mean = (sums[j][:, :128] / jnp.where(total > 0.0, total, 1.0)).astype(BF16)
            for g in range(2):
                h, part_rows = 2 * j + g, slice(g * WIN, (g + 1) * WIN)
                pooled[pl.ds(at, WIN), pl.ds(h * HEAD_DIM, HEAD_DIM)] = mean[part_rows]
                top.append(jnp.broadcast_to(peaks[j][part_rows] * SCALE, (WIN, 128)))
                totals.append(total[part_rows])
        pooled[pl.ds(at, WIN), pl.ds(QW, 128)] = stats_of(top, totals)

    leave.wait()


def pack_stats(stats):
    lane = lax.broadcasted_iota(jnp.int32, stats.shape, 1)
    top = stats.astype(BF16).astype(F32)
    rest = stats - top
    middle = rest.astype(BF16).astype(F32)
    rest = rest - middle
    kept = jnp.where(lane < 8, top, jnp.where(lane < 16, middle, jnp.where(lane < 24, rest, 0.0)))
    return kept.astype(BF16)


def stats_of(peaks, totals):
    value = lax.broadcasted_iota(jnp.int32, peaks[0].shape, 1) & 7
    stats = jnp.zeros(peaks[0].shape, F32)
    for h in range(4):
        stats = jnp.where(value == h, peaks[h], stats)
        stats = jnp.where(value == 4 + h, totals[h], stats)
    return pack_stats(stats)


def spreader():
    value = lax.broadcasted_iota(jnp.int32, (128, 2 * QW), 0)
    column = lax.broadcasted_iota(jnp.int32, (128, 2 * QW), 1)
    return ((value < 24) & ((value & 7) == (column >> 7))).astype(F32).astype(BF16)


def head(block, h):
    return block[:, h * HEAD_DIM:(h + 1) * HEAD_DIM]


def finish_kernel(
    pooled, order, qown, newkv, tok, gain, wo_h, wg_h, wu_h, wd_h, out,
    part, came, comb, rx, mix, down, spread, left_stats, right_stats, left_share, right_share, wo, wg, wu, wd,
    w_sem, ps_sem, pr_sem, cs_sem, cr_sem, ms_sem, mr_sem, ds_sem, dr_sem,
):
    core, y, z, tp = place()
    chip = y * SIDE + z
    barrier = pltpu.get_barrier_semaphore()
    sibling = device(chip, 1 - core, tp)
    peers = [sibling] + [device(chip_at(y, z, k), core, tp) for k in range(1, CHIPS)]
    beside = [device(chip, core, lax.rem(tp + d, 4)) for d in range(1, 4)]
    for peer in peers + beside:
        pl.semaphore_signal(barrier, inc=1, device_id=peer, device_id_type=MESH)
    loads = [
        pltpu.make_async_copy(src, dst, w_sem.at[i])
        for i, (src, dst) in enumerate(((wo_h, wo), (wg_h, wg), (wu_h, wu), (wd_h, wd)))
    ]
    for copy in loads:
        copy.start()
    n_sub = request_of(lax.broadcasted_iota(jnp.int32, (REQS, 128), 0))
    place_n = jnp.concatenate([as_bf16(order[t:t + 1, :] == n_sub) for t in range(4)], axis=1)
    part[...] = jnp.dot(place_n, pooled[...], preferred_element_type=F32).astype(BF16)
    spread[...] = spreader()
    half = pl.multiple_of(core * HALF, HALF)
    left_stats[...] = jnp.dot(part[pl.ds(half, HALF), pl.ds(QW, 128)], spread[...], preferred_element_type=F32)
    own_peaks, own_values = [], []
    for h in range(4):
        keys = newkv[pl.ds(2 * (h // 2), ROWS, stride=4), :].astype(BF16).astype(F32)
        query = head(qown[...], h).astype(F32)
        score = jnp.sum(query * keys, axis=1, keepdims=True) * SCALE
        own_peaks.append(jnp.broadcast_to(score, (ROWS, HEAD_DIM)))
        own_values.append(newkv[pl.ds(2 * (h // 2) + 1, ROWS, stride=4), :].astype(BF16).astype(F32))
    pl.semaphore_wait(barrier, len(peers) + len(beside))

    def rows_of(dy):
        return pl.multiple_of(lax.rem(y + dy, SIDE) * 64, 64)

    turns = (2, 1, 3, 0)
    theirs = pl.ds(pl.multiple_of(HALF - half, HALF), HALF)
    swaps = [
        pltpu.make_async_remote_copy(
            src_ref=part.at[theirs, cols], dst_ref=came.at[:, cols],
            send_sem=ps_sem.at[i], recv_sem=pr_sem.at[i], device_id=sibling, device_id_type=MESH,
        )
        for i, cols in enumerate((pl.ds(QW, 128), pl.ds(0, QW)))
    ]
    for swap in swaps:
        swap.start()

    def stat(ref, rows, h):
        totals = ref[rows, pl.ds(QW + h * HEAD_DIM, HEAD_DIM)]
        return jnp.where(totals > 0.0, ref[rows, pl.ds(h * HEAD_DIM, HEAD_DIM)], FLOOR), totals

    swaps[0].wait_recv()
    right_stats[...] = jnp.dot(came[:, pl.ds(QW, 128)], spread[...], preferred_element_type=F32)
    for dy in turns:
        rows = pl.ds(rows_of(dy), 64)
        peaks, totals = [], []
        for h in range(4):
            cols = pl.ds(h * HEAD_DIM, HEAD_DIM)
            peak_a, total_a = stat(left_stats, rows, h)
            peak_b, total_b = stat(right_stats, rows, h)
            peak = jnp.maximum(peak_a, peak_b)
            left = total_a * jnp.exp(peak_a - peak)
            right = total_b * jnp.exp(peak_b - peak)
            total = left + right
            kept = jnp.where(total > 0.0, total, 1.0)
            left_share[rows, cols] = left / kept
            right_share[rows, cols] = right / kept
            peaks.append(jnp.where(total > 0.0, peak, 0.0))
            totals.append(total)
        comb[rows, pl.ds(QW, 128)] = stats_of(peaks, totals)

    swaps[1].wait_recv()
    sends = []
    for dy in turns:
        rows = pl.ds(rows_of(dy), 64)
        mine = pl.ds(pl.multiple_of(half + rows_of(dy), 64), 64)
        for h in range(4):
            cols = pl.ds(h * HEAD_DIM, HEAD_DIM)
            summed = part[mine, cols].astype(F32) * left_share[rows, cols]
            comb[rows, cols] = (summed + came[rows, cols].astype(F32) * right_share[rows, cols]).astype(BF16)
        for dz in (2, 1, 3, 0):
            k = dy * SIDE + dz
            if k == 0:
                continue
            block = comb.at[pl.ds(pl.multiple_of(chip_at(y, z, k) * ROWS, ROWS), ROWS)]
            sends.append(
                pltpu.make_async_remote_copy(
                    src_ref=block, dst_ref=rx.at[k], send_sem=cs_sem.at[k], recv_sem=cr_sem.at[k],
                    device_id=peers[k], device_id_type=MESH,
                )
            )
            sends[-1].start()
    rx[0] = comb[pl.ds(pl.multiple_of(chip * ROWS, ROWS), ROWS), :]

    for copy in sends:
        copy.wait_recv()
    found = [rx[k, :, pl.ds(QW, 128)] for k in range(CHIPS)]
    left_stats[...] = jnp.dot(jnp.concatenate(found, axis=0), spread[...], preferred_element_type=F32)
    context = []
    for h in range(4):
        cols = pl.ds(h * HEAD_DIM, HEAD_DIM)
        stats = [stat(left_stats, pl.ds(k * ROWS, ROWS), h) for k in range(CHIPS)]
        peak = own_peaks[h]
        for other, _ in stats:
            peak = jnp.maximum(peak, other)
        total = jnp.exp(own_peaks[h] - peak)
        summed = total * own_values[h]
        for k in range(CHIPS):
            weight = stats[k][1] * jnp.exp(stats[k][0] - peak)
            total = total + weight
            summed = summed + weight * rx[k, :, cols].astype(F32)
        context.append((summed / total).astype(BF16))
    context = jnp.concatenate(context, axis=1)

    def over_tp(left, right, terms, send, recv):
        copies = []
        for n in range(PARTS):
            cols = pl.ds(n * WIDTH, WIDTH)
            terms[tp, :, cols] = jnp.dot(left, right[:, cols], preferred_element_type=F32).astype(BF16)
            ref = terms.at[tp, :, cols]
            copies.append([
                pltpu.make_async_remote_copy(
                    src_ref=ref, dst_ref=ref, send_sem=send.at[n, d], recv_sem=recv.at[n, d],
                    device_id=beside[d], device_id_type=MESH,
                )
                for d in TP_ORDER
            ])
            for copy in copies[-1]:
                copy.start()
        return copies

    def summed_terms(first, terms, n):
        cols = pl.ds(n * WIDTH, WIDTH)
        total = first
        for t in range(4):
            total = total + terms[t, :, cols].astype(F32)
        return total

    loads[0].wait()
    mixes = over_tp(context, wo, mix, ms_sem, mr_sem)
    loads[1].wait()
    loads[2].wait()
    mids, squares = [], jnp.zeros((ROWS, 1), F32)
    gate = jnp.zeros((ROWS, 1024), F32)
    upper = jnp.zeros((ROWS, 1024), F32)
    for n in range(PARTS):
        for copy in mixes[n]:
            copy.wait_recv()
        cols = pl.ds(n * WIDTH, WIDTH)
        mid = summed_terms(tok[:, cols].astype(F32), mix, n)
        mids.append(mid)
        squares = squares + jnp.sum(mid * mid, axis=-1, keepdims=True)
        gains = [gain[pl.ds(n * (WIDTH // 128) + i, 1), :] for i in range(WIDTH // 128)]
        scaled = (mid * jnp.concatenate(gains, axis=1).astype(F32)).astype(BF16)
        gate = gate + jnp.dot(scaled, wg[cols, :], preferred_element_type=F32)
        upper = upper + jnp.dot(scaled, wu[cols, :], preferred_element_type=F32)
    scale = lax.rsqrt(squares * (1.0 / 2048) + EPS)
    gate = gate * scale
    act = (gate / (1.0 + jnp.exp(-gate)) * (upper * scale)).astype(BF16)
    loads[3].wait()
    downs = over_tp(act, wd, down, ds_sem, dr_sem)
    for n in range(PARTS):
        for copy in downs[n]:
            copy.wait_recv()
        out[:, pl.ds(n * WIDTH, WIDTH)] = summed_terms(mids[n], down, n)
    for copy in swaps + sends + sum(mixes + downs, []):
        copy.wait_send()


def per_device(
    tokens, lengths, pool_order, positions, slot_mask, kv_cache, attn_gain,
    w_query, w_key, w_value, w_out, ffn_gain, w_gate, w_up, w_down,
):
    def stay(*arrays):
        return [pltpu.with_memory_space_constraint(a, pltpu.HBM) for a in arrays]

    vmem = pl.BlockSpec(memory_space=pltpu.VMEM)
    smem = pl.BlockSpec(memory_space=pltpu.SMEM)
    hbm = pl.BlockSpec(memory_space=pltpu.HBM)
    dma = pltpu.SemaphoreType.DMA
    pool = kv_cache.reshape(SLOTS, 2, 2, HEAD_DIM).transpose(0, 2, 1, 3).reshape(4 * SLOTS, HEAD_DIM)
    qall, qown, newkv, kvd = pl.pallas_call(
        project_kernel,
        out_shape=(
            jax.ShapeDtypeStruct((REQS, PW), BF16),
            jax.ShapeDtypeStruct((ROWS, QW), BF16),
            jax.ShapeDtypeStruct((4 * ROWS, HEAD_DIM), F32),
            jax.ShapeDtypeStruct((SLOTS, QW), BF16),
        ),
        in_specs=[hbm] * 9,
        out_specs=(vmem,) * 4,
        scratch_shapes=[
            pltpu.SMEM((ROWS,), jnp.int32),
            pltpu.SMEM((ROWS,), jnp.int32),
            pltpu.VMEM((ROWS, 2048), BF16),
            pltpu.VMEM((16, 128), BF16),
            pltpu.VMEM((8, 128), F32),
            pltpu.VMEM((2048, 512), BF16),
            pltpu.VMEM((2048, 256), BF16),
            pltpu.VMEM((2048, 256), BF16),
            pltpu.VMEM((4 * SLOTS, HEAD_DIM), BF16),
            pltpu.VMEM((1024, HEAD_DIM), F32),
            dma((5,)), dma((3,)), dma((4,)), dma((16,)), dma((16,)), dma((4,)), dma((4,)), dma((4,)), dma((4,)),
        ],
        compiler_params=pltpu.CompilerParams(
            collective_id=0, has_side_effects=True, vmem_limit_bytes=40 << 20
        ),
        name="project",
    )(
        *stay(
            lengths, positions, tokens, attn_gain.reshape(16, 128), jnp.asarray(frequency_table()),
            w_query, w_key, w_value, pool,
        )
    )
    base = (lax.axis_index("req") * SLOTS).astype(jnp.int32).reshape(1)
    part, new_kv = pl.pallas_call(
        attend_kernel,
        out_shape=(
            jax.ShapeDtypeStruct((REQS, PW), BF16),
            pltpu.HBM((4 * ROWS, HEAD_DIM), F32),
        ),
        in_specs=[smem, vmem, vmem, vmem, vmem, vmem],
        out_specs=(vmem, hbm),
        scratch_shapes=[
            pltpu.VMEM((2, 2 * WIN, SLOTS), F32),
            pltpu.VMEM((REQS, 128), jnp.int32),
            pltpu.VMEM((REQS, 128), jnp.int32),
            pltpu.VMEM((REQS, 128), jnp.int32),
            dma,
        ],
        compiler_params=pltpu.CompilerParams(vmem_limit_bytes=40 << 20),
        name="attend",
    )(base, qall, pool_order.reshape(4, 128), slot_mask.reshape(32, 128), kvd, newkv)
    hidden = pl.pallas_call(
        finish_kernel,
        out_shape=jax.ShapeDtypeStruct((ROWS, 2048), F32),
        in_specs=[vmem] * 6 + [hbm] * 4,
        out_specs=vmem,
        scratch_shapes=[
            pltpu.VMEM((REQS, PW), BF16),
            pltpu.VMEM((HALF, PW), BF16),
            pltpu.VMEM((HALF, PW), BF16),
            pltpu.VMEM((CHIPS, ROWS, PW), BF16),
            pltpu.VMEM((4, ROWS, 2048), BF16),
            pltpu.VMEM((4, ROWS, 2048), BF16),
            pltpu.VMEM((128, 2 * QW), BF16),
            pltpu.VMEM((HALF, 2 * QW), F32),
            pltpu.VMEM((HALF, 2 * QW), F32),
            pltpu.VMEM((HALF, QW), F32),
            pltpu.VMEM((HALF, QW), F32),
            pltpu.VMEM((512, 2048), BF16),
            pltpu.VMEM((2048, 1024), BF16),
            pltpu.VMEM((2048, 1024), BF16),
            pltpu.VMEM((1024, 2048), BF16),
            dma((4,)), dma((2,)), dma((2,)), dma((16,)), dma((16,)),
            dma((4, 3)), dma((4, 3)), dma((4, 3)), dma((4, 3)),
        ],
        compiler_params=pltpu.CompilerParams(
            collective_id=1, has_side_effects=True, vmem_limit_bytes=40 << 20
        ),
        name="finish",
    )(part, pool_order.reshape(4, 128), qown, newkv, tokens, ffn_gain.reshape(16, 128), *stay(w_out, w_gate, w_up, w_down))
    new_kv = new_kv.reshape(ROWS, 2, 2, HEAD_DIM).transpose(0, 2, 1, 3).reshape(ROWS, 2, 256)
    return hidden, new_kv


def solution(mesh):
    placed = (
        P("req", None), P("req"), P(), P("req"), P("req"), P("req", None, "tp"), P(),
        P(None, "tp"), P(None, "tp"), P(None, "tp"), P("tp", None), P(),
        P(None, "tp"), P(None, "tp"), P("tp", None),
    )
    return jax.shard_map(
        per_device,
        mesh=mesh,
        in_specs=placed,
        out_specs=(P("req", None), P("req", None, "tp")),
        check_vma=False,
    )
```

```python
import functools
import math

import jax
import jax.numpy as jnp
import numpy as np
from jax import lax
from jax.experimental import pallas as pl
from jax.experimental.pallas import tpu as pltpu
from jax.sharding import PartitionSpec as P

MESH = pl.DeviceIdType.MESH
HEAD_DIM = 128
ROPE_BASE = 1000000.0
EPS = 1e-05
FLOOR = -1e30
SCALE = 1.0 / math.sqrt(HEAD_DIM)
SIDE = 4
CHIPS = SIDE * SIDE
ROWS = 16
REQS = 512
SLOTS = 4096
HALF = REQS // 2
QW = 512
PW = QW + 128
WIN = 64
STEP = 512
CHUNK = 4096
PARTS = 4
WIDTH = 2048 // PARTS
TP_ORDER = (1, 0, 2)
FAR_FIRST = (10, 9, 11, 6, 14, 8, 2, 5, 7, 13, 15, 4, 12, 1, 3)
LOG2E = 1.4426950408889634
BF16 = jnp.bfloat16
F32 = jnp.float32


def place():
    me = lax.axis_index("req")
    core = lax.rem(me, 2)
    chip = me // 2
    return core, chip // SIDE, lax.rem(chip, SIDE), lax.axis_index("tp")


def chip_at(y, z, k):
    return lax.rem(y + k // SIDE, SIDE) * SIDE + lax.rem(z + k % SIDE, SIDE)


def device(chip, core, tp):
    return {"req": chip * 2 + core, "tp": tp}


def rms_norm(rows, gain):
    scale = lax.rsqrt(jnp.mean(rows * rows, axis=-1, keepdims=True) + EPS)
    gain = gain.astype(F32)
    tiles = [rows[:, i * 128:(i + 1) * 128] * scale * gain[i:i + 1, :] for i in range(gain.shape[0])]
    return jnp.concatenate(tiles, axis=1).astype(BF16)


def frequency_table():
    half = HEAD_DIM // 2
    turns = ROPE_BASE ** (-(np.arange(half, dtype=np.float64) * 2.0) / HEAD_DIM) / (2.0 * np.pi)
    first = np.round(turns * 2.0**12) / 2.0**12
    second = np.round((turns - first) * 2.0**23) / 2.0**23
    third = turns - first - second
    table = np.zeros((8, HEAD_DIM), np.float64)
    for i, term in enumerate((first, second, third)):
        table[i] = np.concatenate([term, term])
    return table.astype(np.float32)


def cos_sin(where, table):
    turn = where * table[0:1, :]
    turn = turn - jnp.floor(turn + 0.5)
    turn = turn + where * table[1:2, :]
    turn = turn - jnp.floor(turn + 0.5)
    turn = turn + where * table[2:3, :]
    quarter = jnp.floor(turn * 4.0 + 0.5)
    x = (turn - quarter * 0.25) * np.float32(2.0 * np.pi)
    sq = x * x
    sine = x * (1.0 + sq * (-1.0 / 6 + sq * (1.0 / 120 + sq * (-1.0 / 5040 + sq * (1.0 / 362880)))))
    cosine = 1.0 + sq * (
        -0.5 + sq * (1.0 / 24 + sq * (-1.0 / 720 + sq * (1.0 / 40320 + sq * (-1.0 / 3628800))))
    )
    odd = (quarter == 1.0) | (quarter == -1.0)
    far = (quarter == 2.0) | (quarter == -2.0)
    c = jnp.where(odd, -quarter * sine, jnp.where(far, -cosine, cosine))
    s = jnp.where(odd, quarter * cosine, jnp.where(far, -sine, sine))
    return c, s


def project_kernel(
    len_h, pos_h, tok_h, gain_h, table_h, wq_h, wk_h, wv_h, pool_h,
    qall, qown_o, newkv_o, kvd,
    len_s, pos_s, tok, gain, table, wq, wk, wv, pool, tmp,
    s_sem, w_sem, pool_sem, qs_sem, qr_sem, fs_sem, fr_sem, ds_sem, dr_sem,
):
    core, y, z, tp = place()
    chip = y * SIDE + z
    small = [
        pltpu.make_async_copy(src, dst, s_sem.at[i])
        for i, (src, dst) in enumerate(
            ((len_h, len_s), (pos_h, pos_s), (table_h, table), (tok_h, tok), (gain_h, gain))
        )
    ]
    loads = [
        pltpu.make_async_copy(src, dst, w_sem.at[i])
        for i, (src, dst) in enumerate(((wq_h, wq), (wk_h, wk), (wv_h, wv)))
    ]
    piece = 4 * SLOTS // 4
    pool_loads = [
        pltpu.make_async_copy(pool_h.at[pl.ds(i * piece, piece)], pool.at[pl.ds(i * piece, piece)], pool_sem.at[i])
        for i in range(4)
    ]
    for copy in small + loads + pool_loads:
        copy.start()

    barrier = pltpu.get_barrier_semaphore()
    sibling = device(chip, 1 - core, tp)
    peers = [sibling] + [device(chip_at(y, z, k), core, tp) for k in range(1, CHIPS)]
    across = [device(chip_at(y, z, k), 1 - core, tp) for k in range(1, SIDE)]
    for peer in [peers[k] for k in FAR_FIRST] + across + [sibling]:
        pl.semaphore_signal(barrier, inc=1, device_id=peer, device_id_type=MESH)

    for copy in small:
        copy.wait()
    row = lax.broadcasted_iota(jnp.int32, (ROWS, 128), 0)
    lane = lax.broadcasted_iota(jnp.int32, (ROWS, 128), 1)
    where = jnp.zeros((ROWS, 128), jnp.int32)
    digits = jnp.zeros((ROWS, 128), jnp.int32)
    for i in range(ROWS):
        where = jnp.where(row == i, pos_s[i], where)
        digits = jnp.where(row == i, len_s[i], digits)
    digits = jnp.where(lane == 0, digits >> 7, jnp.where(lane == 1, digits & 127, 0)).astype(F32).astype(BF16)
    cosine, sine = cos_sin(where.astype(F32), table[...])
    sine = jnp.where(lane < HEAD_DIM // 2, -sine, sine)

    def rotate(vectors):
        return vectors * cosine + pltpu.roll(vectors, HEAD_DIM // 2, axis=1) * sine

    normed = rms_norm(tok[...].astype(F32), gain[...])

    pl.semaphore_wait(barrier, len(peers) + len(across))
    loads[0].wait()
    query = jnp.dot(normed, wq[...], preferred_element_type=F32)
    mine_at = pl.multiple_of(core * HALF + chip * ROWS, ROWS)
    for h in range(QW // HEAD_DIM):
        cols = pl.ds(h * HEAD_DIM, HEAD_DIM)
        turned = rotate(query[:, h * HEAD_DIM:(h + 1) * HEAD_DIM]).astype(BF16)
        qall[pl.ds(mine_at, ROWS), cols] = turned
        qown_o[:, cols] = turned
    qall[pl.ds(mine_at, ROWS), pl.ds(QW, 128)] = digits
    my_rows = qall.at[pl.ds(mine_at, ROWS)]
    q_sends = {}
    for k in range(1, CHIPS):
        q_sends[k] = pltpu.make_async_remote_copy(
            src_ref=my_rows, dst_ref=my_rows, send_sem=qs_sem.at[k], recv_sem=qr_sem.at[k],
            device_id=peers[k], device_id_type=MESH,
        )
    own_forward = pltpu.make_async_remote_copy(
        src_ref=my_rows, dst_ref=my_rows, send_sem=fs_sem.at[0], recv_sem=fr_sem.at[0],
        device_id=sibling, device_id_type=MESH,
    )
    directs = [
        pltpu.make_async_remote_copy(
            src_ref=my_rows, dst_ref=my_rows, send_sem=ds_sem.at[k], recv_sem=dr_sem.at[k],
            device_id=across[k - 1], device_id_type=MESH,
        )
        for k in range(1, SIDE)
    ]
    for k in (10, 9, 11, 8, 6, 5, 7, 4, 14, 13, 15, 12):
        q_sends[k].start()
    own_forward.start()
    for k in (2, 1, 3):
        directs[k - 1].start()
        q_sends[k].start()

    def forward(dy):
        source = lax.rem(y + SIDE - dy, SIDE) * SIDE * ROWS
        rows = qall.at[pl.ds(pl.multiple_of(core * HALF + source, SIDE * ROWS), SIDE * ROWS)]
        return pltpu.make_async_remote_copy(
            src_ref=rows, dst_ref=rows, send_sem=fs_sem.at[dy], recv_sem=fr_sem.at[dy],
            device_id=sibling, device_id_type=MESH,
        )

    loads[1].wait()
    key = jnp.dot(normed, wk[...], preferred_element_type=F32)
    loads[2].wait()
    value = jnp.dot(normed, wv[...], preferred_element_type=F32)
    for h in range(2):
        cols = slice(h * HEAD_DIM, (h + 1) * HEAD_DIM)
        newkv_o[pl.ds(2 * h, ROWS, stride=4), :] = rotate(key[:, cols])
        newkv_o[pl.ds(2 * h + 1, ROWS, stride=4), :] = value[:, cols]

    def untangle(i):
        tmp[...] = pool[pl.ds(i * 1024, 1024), :].astype(F32)
        for j in range(4):
            kvd[pl.ds(i * 256, 256), pl.ds(j * 128, 128)] = tmp[pl.ds(j, 256, stride=4), :].astype(BF16)

    for i in range(4):
        pool_loads[i].wait()
    forwards = []
    for i, dy in enumerate((2, 1, 3, 0)):
        for j in range(SIDE):
            untangle(4 * i + j)
        for dz in range(SIDE):
            if dy:
                q_sends[dy * SIDE + dz].wait_recv()
        if dy:
            forwards.append(forward(dy))
            forwards[-1].start()
    for copy in forwards:
        copy.wait()
    own_forward.wait()
    for copy in directs:
        copy.wait()
    for k in range(1, SIDE):
        q_sends[k].wait_recv()
    for copy in q_sends.values():
        copy.wait_send()


def request_of(n):
    return ((n >> 4) & 15) * 32 + (n >> 8) * 16 + (n & 15)


def as_bf16(flags):
    return flags.astype(F32).astype(BF16)


def attend_kernel(
    base_s, qall, order, mask, kvd, newkv, pooled, newkv_o,
    scores, order_b, first_b, last_b, out_sem,
):
    leave = pltpu.make_async_copy(newkv, newkv_o, out_sem)
    leave.start()
    base = base_s[0]

    n_lane = [request_of(lax.broadcasted_iota(jnp.int32, (1, 128), 1) + 128 * t) for t in range(4)]
    for t in range(4):
        tile = jnp.broadcast_to(order[t:t + 1, :], (128, 128)).astype(F32)
        order_b[pl.ds(128 * t, 128), :] = jnp.transpose(tile).astype(jnp.int32)
    p_sub = lax.broadcasted_iota(jnp.int32, (REQS, 128), 0)
    here, upto = [], []
    for t in range(4):
        match = order_b[...] == n_lane[t]
        pos = jnp.sum(jnp.where(match, p_sub.astype(F32), 0.0), axis=0, keepdims=True).astype(jnp.int32)
        here.append(as_bf16(match))
        upto.append(as_bf16(pos <= p_sub))
    digits = qall[:, pl.ds(QW, 128)]

    def lengths_by(flags):
        found = jnp.dot(jnp.concatenate(flags, axis=1), digits, preferred_element_type=F32)
        return (found[:, 0:1] * 128.0 + found[:, 1:2]).astype(jnp.int32)

    ends = lengths_by(upto) - base
    starts = ends - lengths_by(here)
    first_b[...] = jnp.broadcast_to(starts, (REQS, 128))
    last_b[...] = jnp.broadcast_to(ends, (REQS, 128))
    low = jnp.sum((ends <= 0).astype(jnp.int32))
    high = jnp.sum((starts < SLOTS).astype(jnp.int32))
    low = (low // 16) * 16
    windows = (high - low + (WIN - 1)) // WIN

    pooled[...] = jnp.zeros_like(pooled)
    slot = lax.broadcasted_iota(jnp.int32, (1, 128), 1)
    ones = jnp.ones((STEP, 128), BF16)

    @pl.loop(0, windows)
    def _(w):
        at = pl.multiple_of(jnp.minimum(low + w * WIN, REQS - WIN), 16)
        own = order_b[pl.ds(at, WIN), :]
        pick = jnp.concatenate([as_bf16(own == n_lane[t]) for t in range(4)], axis=1)
        query = jnp.dot(pick, qall[:, pl.ds(0, QW)], preferred_element_type=F32).astype(BF16)
        first = first_b[pl.ds(at, WIN), :]
        last = last_b[pl.ds(at, WIN), :]
        chunk_from = jnp.maximum(jnp.min(first), 0) // CHUNK
        chunk_to = (jnp.minimum(jnp.max(last), SLOTS) + (CHUNK - 1)) // CHUNK
        first = jnp.concatenate([first, first], axis=0)
        last = jnp.concatenate([last, last], axis=0)
        rows = [jnp.concatenate([head(query, 2 * j), head(query, 2 * j + 1)], axis=0) for j in range(2)]

        def score(c, peaks):
            start = pl.multiple_of(c * CHUNK, CHUNK)
            peaks = list(peaks)
            for n in range(CHUNK // STEP):
                at_n = pl.multiple_of(start + n * STEP, STEP)
                oks = []
                for i in range(STEP // 128):
                    live = mask[pl.ds(c * (CHUNK // 128) + n * (STEP // 128) + i, 1), :] == 1
                    index = jnp.where(live, slot + (at_n + i * 128), -REQS * 8192)
                    oks.append((index >= first) & (index < last))
                for j in range(2):
                    s = lax.dot_general(
                        rows[j], kvd[pl.ds(at_n, STEP), pl.ds(2 * j * 128, 128)],
                        (((1,), (1,)), ((), ())), preferred_element_type=F32,
                    )
                    for i in range(STEP // 128):
                        found = jnp.where(oks[i], s[:, i * 128:(i + 1) * 128], FLOOR)
                        scores[j, :, pl.ds(pl.multiple_of(at_n + i * 128, 128), 128)] = found
                        peaks[j] = jnp.maximum(peaks[j], found)
            return tuple(peaks)

        least = jnp.full((2 * WIN, 128), FLOOR, F32)
        peaks = lax.fori_loop(chunk_from, chunk_to, score, (least, least))
        peaks = [jnp.max(peak, axis=1, keepdims=True) for peak in peaks]
        peaks = [jnp.where(peak > 0.5 * FLOOR, peak, 0.0) for peak in peaks]

        def weigh(c, sums):
            start = pl.multiple_of(c * CHUNK, CHUNK)
            sums = list(sums)
            for n in range(CHUNK // STEP):
                at_n = pl.multiple_of(start + n * STEP, STEP)
                for j in range(2):
                    weight = jnp.exp2((scores[j, :, pl.ds(at_n, STEP)] - peaks[j]) * (SCALE * LOG2E)).astype(BF16)
                    values = kvd[pl.ds(at_n, STEP), pl.ds((2 * j + 1) * 128, 128)]
                    both = jnp.concatenate([values, ones], axis=1)
                    sums[j] = sums[j] + jnp.dot(weight, both, preferred_element_type=F32)
            return tuple(sums)

        zero = jnp.zeros((2 * WIN, 256), F32)
        sums = lax.fori_loop(chunk_from, chunk_to, weigh, (zero, zero))
        top, totals = [], []
        for j in range(2):
            total = sums[j][:, 128:]
            mean = (sums[j][:, :128] / jnp.where(total > 0.0, total, 1.0)).astype(BF16)
            for g in range(2):
                h, part_rows = 2 * j + g, slice(g * WIN, (g + 1) * WIN)
                pooled[pl.ds(at, WIN), pl.ds(h * HEAD_DIM, HEAD_DIM)] = mean[part_rows]
                top.append(jnp.broadcast_to(peaks[j][part_rows] * SCALE, (WIN, 128)))
                totals.append(total[part_rows])
        pooled[pl.ds(at, WIN), pl.ds(QW, 128)] = stats_of(top, totals)

    leave.wait()


def pack_stats(stats):
    lane = lax.broadcasted_iota(jnp.int32, stats.shape, 1)
    top = stats.astype(BF16).astype(F32)
    rest = stats - top
    middle = rest.astype(BF16).astype(F32)
    rest = rest - middle
    kept = jnp.where(lane < 8, top, jnp.where(lane < 16, middle, jnp.where(lane < 24, rest, 0.0)))
    return kept.astype(BF16)


def stats_of(peaks, totals):
    value = lax.broadcasted_iota(jnp.int32, peaks[0].shape, 1) & 7
    stats = jnp.zeros(peaks[0].shape, F32)
    for h in range(4):
        stats = jnp.where(value == h, peaks[h], stats)
        stats = jnp.where(value == 4 + h, totals[h], stats)
    return pack_stats(stats)


def spreader():
    value = lax.broadcasted_iota(jnp.int32, (128, 2 * QW), 0)
    column = lax.broadcasted_iota(jnp.int32, (128, 2 * QW), 1)
    return ((value < 24) & ((value & 7) == (column >> 7))).astype(F32).astype(BF16)


def head(block, h):
    return block[:, h * HEAD_DIM:(h + 1) * HEAD_DIM]


def finish_kernel(
    pooled, order, qown, newkv, tok, gain, wo_h, wg_h, wu_h, wd_h, out,
    part, came, comb, rx, mix, down, spread, left_stats, right_stats, left_share, right_share, wo, wg, wu, wd,
    w_sem, ps_sem, pr_sem, cs_sem, cr_sem, ms_sem, mr_sem, ds_sem, dr_sem,
):
    core, y, z, tp = place()
    chip = y * SIDE + z
    barrier = pltpu.get_barrier_semaphore()
    sibling = device(chip, 1 - core, tp)
    peers = [sibling] + [device(chip_at(y, z, k), core, tp) for k in range(1, CHIPS)]
    beside = [device(chip, core, lax.rem(tp + d, 4)) for d in range(1, 4)]
    for peer in [peers[k] for k in FAR_FIRST] + [beside[d] for d in TP_ORDER] + [sibling]:
        pl.semaphore_signal(barrier, inc=1, device_id=peer, device_id_type=MESH)
    loads = [
        pltpu.make_async_copy(src, dst, w_sem.at[i])
        for i, (src, dst) in enumerate(((wo_h, wo), (wg_h, wg), (wu_h, wu), (wd_h, wd)))
    ]
    for copy in loads:
        copy.start()
    n_sub = request_of(lax.broadcasted_iota(jnp.int32, (REQS, 128), 0))
    place_n = jnp.concatenate([as_bf16(order[t:t + 1, :] == n_sub) for t in range(4)], axis=1)
    part[...] = jnp.dot(place_n, pooled[...], preferred_element_type=F32).astype(BF16)
    spread[...] = spreader()
    half = pl.multiple_of(core * HALF, HALF)
    left_stats[...] = jnp.dot(part[pl.ds(half, HALF), pl.ds(QW, 128)], spread[...], preferred_element_type=F32)
    own_peaks, own_values = [], []
    for h in range(4):
        keys = newkv[pl.ds(2 * (h // 2), ROWS, stride=4), :].astype(BF16).astype(F32)
        query = head(qown[...], h).astype(F32)
        score = jnp.sum(query * keys, axis=1, keepdims=True) * SCALE
        own_peaks.append(jnp.broadcast_to(score, (ROWS, HEAD_DIM)))
        own_values.append(newkv[pl.ds(2 * (h // 2) + 1, ROWS, stride=4), :].astype(BF16).astype(F32))
    pl.semaphore_wait(barrier, len(peers) + len(beside))

    def rows_of(dy):
        return pl.multiple_of(lax.rem(y + dy, SIDE) * 64, 64)

    turns = (2, 1, 3, 0)
    theirs = pl.ds(pl.multiple_of(HALF - half, HALF), HALF)
    swaps = [
        pltpu.make_async_remote_copy(
            src_ref=part.at[theirs, cols], dst_ref=came.at[:, cols],
            send_sem=ps_sem.at[i], recv_sem=pr_sem.at[i], device_id=sibling, device_id_type=MESH,
        )
        for i, cols in enumerate((pl.ds(QW, 128), pl.ds(0, QW)))
    ]
    for swap in swaps:
        swap.start()

    def stat(ref, rows, h):
        totals = ref[rows, pl.ds(QW + h * HEAD_DIM, HEAD_DIM)]
        return jnp.where(totals > 0.0, ref[rows, pl.ds(h * HEAD_DIM, HEAD_DIM)], FLOOR), totals

    swaps[0].wait_recv()
    right_stats[...] = jnp.dot(came[:, pl.ds(QW, 128)], spread[...], preferred_element_type=F32)
    for dy in turns:
        rows = pl.ds(rows_of(dy), 64)
        peaks, totals = [], []
        for h in range(4):
            cols = pl.ds(h * HEAD_DIM, HEAD_DIM)
            peak_a, total_a = stat(left_stats, rows, h)
            peak_b, total_b = stat(right_stats, rows, h)
            peak = jnp.maximum(peak_a, peak_b)
            left = total_a * jnp.exp(peak_a - peak)
            right = total_b * jnp.exp(peak_b - peak)
            total = left + right
            kept = jnp.where(total > 0.0, total, 1.0)
            inverse = 1.0 / kept
            left_share[rows, cols] = left * inverse
            right_share[rows, cols] = right * inverse
            peaks.append(jnp.where(total > 0.0, peak, 0.0))
            totals.append(total)
        comb[rows, pl.ds(QW, 128)] = stats_of(peaks, totals)

    swaps[1].wait_recv()
    sends = []
    for dy in turns:
        rows = pl.ds(rows_of(dy), 64)
        mine = pl.ds(pl.multiple_of(half + rows_of(dy), 64), 64)
        for h in range(4):
            cols = pl.ds(h * HEAD_DIM, HEAD_DIM)
            summed = part[mine, cols].astype(F32) * left_share[rows, cols]
            comb[rows, cols] = (summed + came[rows, cols].astype(F32) * right_share[rows, cols]).astype(BF16)
        for dz in (2, 1, 3, 0):
            k = dy * SIDE + dz
            if k == 0:
                continue
            block = comb.at[pl.ds(pl.multiple_of(chip_at(y, z, k) * ROWS, ROWS), ROWS)]
            sends.append(
                pltpu.make_async_remote_copy(
                    src_ref=block, dst_ref=rx.at[k], send_sem=cs_sem.at[k], recv_sem=cr_sem.at[k],
                    device_id=peers[k], device_id_type=MESH,
                )
            )
            sends[-1].start()
    rx[0] = comb[pl.ds(pl.multiple_of(chip * ROWS, ROWS), ROWS), :]

    for copy in sends:
        copy.wait_recv()
    found = [rx[k, :, pl.ds(QW, 128)] for k in range(CHIPS)]
    left_stats[...] = jnp.dot(jnp.concatenate(found, axis=0), spread[...], preferred_element_type=F32)
    context = []
    for h in range(4):
        cols = pl.ds(h * HEAD_DIM, HEAD_DIM)
        stats = [stat(left_stats, pl.ds(k * ROWS, ROWS), h) for k in range(CHIPS)]
        peak = own_peaks[h]
        for other, _ in stats:
            peak = jnp.maximum(peak, other)
        total = jnp.exp(own_peaks[h] - peak)
        summed = total * own_values[h]
        for k in range(CHIPS):
            weight = stats[k][1] * jnp.exp(stats[k][0] - peak)
            total = total + weight
            summed = summed + weight * rx[k, :, cols].astype(F32)
        context.append((summed / total).astype(BF16))
    context = jnp.concatenate(context, axis=1)

    def over_tp(left, right, terms, send, recv):
        copies = []
        for n in range(PARTS):
            cols = pl.ds(n * WIDTH, WIDTH)
            terms[tp, :, cols] = jnp.dot(left, right[:, cols], preferred_element_type=F32).astype(BF16)
            ref = terms.at[tp, :, cols]
            copies.append([
                pltpu.make_async_remote_copy(
                    src_ref=ref, dst_ref=ref, send_sem=send.at[n, d], recv_sem=recv.at[n, d],
                    device_id=beside[d], device_id_type=MESH,
                )
                for d in TP_ORDER
            ])
            for copy in copies[-1]:
                copy.start()
        return copies

    def summed_terms(first, terms, n):
        cols = pl.ds(n * WIDTH, WIDTH)
        total = first
        for t in range(4):
            total = total + terms[t, :, cols].astype(F32)
        return total

    loads[0].wait()
    mixes = over_tp(context, wo, mix, ms_sem, mr_sem)
    loads[1].wait()
    loads[2].wait()
    mids, squares = [], jnp.zeros((ROWS, 1), F32)
    gate = jnp.zeros((ROWS, 1024), F32)
    upper = jnp.zeros((ROWS, 1024), F32)
    for n in range(PARTS):
        for copy in mixes[n]:
            copy.wait_recv()
        cols = pl.ds(n * WIDTH, WIDTH)
        mid = summed_terms(tok[:, cols].astype(F32), mix, n)
        mids.append(mid)
        squares = squares + jnp.sum(mid * mid, axis=-1, keepdims=True)
        gains = [gain[pl.ds(n * (WIDTH // 128) + i, 1), :] for i in range(WIDTH // 128)]
        scaled = (mid * jnp.concatenate(gains, axis=1).astype(F32)).astype(BF16)
        gate = gate + jnp.dot(scaled, wg[cols, :], preferred_element_type=F32)
        upper = upper + jnp.dot(scaled, wu[cols, :], preferred_element_type=F32)
    scale = lax.rsqrt(squares * (1.0 / 2048) + EPS)
    gate = gate * scale
    act = (gate / (1.0 + jnp.exp(-gate)) * (upper * scale)).astype(BF16)
    loads[3].wait()
    downs = over_tp(act, wd, down, ds_sem, dr_sem)
    for n in range(PARTS):
        for copy in downs[n]:
            copy.wait_recv()
        out[:, pl.ds(n * WIDTH, WIDTH)] = summed_terms(mids[n], down, n)
    for copy in swaps + sends + sum(mixes + downs, []):
        copy.wait_send()


def per_device(
    tokens, lengths, pool_order, positions, slot_mask, kv_cache, attn_gain,
    w_query, w_key, w_value, w_out, ffn_gain, w_gate, w_up, w_down,
):
    def stay(*arrays):
        return [pltpu.with_memory_space_constraint(a, pltpu.HBM) for a in arrays]

    vmem = pl.BlockSpec(memory_space=pltpu.VMEM)
    smem = pl.BlockSpec(memory_space=pltpu.SMEM)
    hbm = pl.BlockSpec(memory_space=pltpu.HBM)
    dma = pltpu.SemaphoreType.DMA
    pool = kv_cache.reshape(SLOTS, 2, 2, HEAD_DIM).transpose(0, 2, 1, 3).reshape(4 * SLOTS, HEAD_DIM)
    qall, qown, newkv, kvd = pl.pallas_call(
        project_kernel,
        out_shape=(
            jax.ShapeDtypeStruct((REQS, PW), BF16),
            jax.ShapeDtypeStruct((ROWS, QW), BF16),
            jax.ShapeDtypeStruct((4 * ROWS, HEAD_DIM), F32),
            jax.ShapeDtypeStruct((SLOTS, QW), BF16),
        ),
        in_specs=[hbm] * 9,
        out_specs=(vmem,) * 4,
        scratch_shapes=[
            pltpu.SMEM((ROWS,), jnp.int32),
            pltpu.SMEM((ROWS,), jnp.int32),
            pltpu.VMEM((ROWS, 2048), BF16),
            pltpu.VMEM((16, 128), BF16),
            pltpu.VMEM((8, 128), F32),
            pltpu.VMEM((2048, 512), BF16),
            pltpu.VMEM((2048, 256), BF16),
            pltpu.VMEM((2048, 256), BF16),
            pltpu.VMEM((4 * SLOTS, HEAD_DIM), BF16),
            pltpu.VMEM((1024, HEAD_DIM), F32),
            dma((5,)), dma((3,)), dma((4,)), dma((16,)), dma((16,)), dma((4,)), dma((4,)), dma((4,)), dma((4,)),
        ],
        compiler_params=pltpu.CompilerParams(
            collective_id=0, has_side_effects=True, vmem_limit_bytes=40 << 20
        ),
        name="project",
    )(
        *stay(
            lengths, positions, tokens, attn_gain.reshape(16, 128), jnp.asarray(frequency_table()),
            w_query, w_key, w_value, pool,
        )
    )
    base = (lax.axis_index("req") * SLOTS).astype(jnp.int32).reshape(1)
    part, new_kv = pl.pallas_call(
        attend_kernel,
        out_shape=(
            jax.ShapeDtypeStruct((REQS, PW), BF16),
            pltpu.HBM((4 * ROWS, HEAD_DIM), F32),
        ),
        in_specs=[smem, vmem, vmem, vmem, vmem, vmem],
        out_specs=(vmem, hbm),
        scratch_shapes=[
            pltpu.VMEM((2, 2 * WIN, SLOTS), F32),
            pltpu.VMEM((REQS, 128), jnp.int32),
            pltpu.VMEM((REQS, 128), jnp.int32),
            pltpu.VMEM((REQS, 128), jnp.int32),
            dma,
        ],
        compiler_params=pltpu.CompilerParams(vmem_limit_bytes=40 << 20),
        name="attend",
    )(base, qall, pool_order.reshape(4, 128), slot_mask.reshape(32, 128), kvd, newkv)
    hidden = pl.pallas_call(
        finish_kernel,
        out_shape=jax.ShapeDtypeStruct((ROWS, 2048), F32),
        in_specs=[vmem] * 6 + [hbm] * 4,
        out_specs=vmem,
        scratch_shapes=[
            pltpu.VMEM((REQS, PW), BF16),
            pltpu.VMEM((HALF, PW), BF16),
            pltpu.VMEM((HALF, PW), BF16),
            pltpu.VMEM((CHIPS, ROWS, PW), BF16),
            pltpu.VMEM((4, ROWS, 2048), BF16),
            pltpu.VMEM((4, ROWS, 2048), BF16),
            pltpu.VMEM((128, 2 * QW), BF16),
            pltpu.VMEM((HALF, 2 * QW), F32),
            pltpu.VMEM((HALF, 2 * QW), F32),
            pltpu.VMEM((HALF, QW), F32),
            pltpu.VMEM((HALF, QW), F32),
            pltpu.VMEM((512, 2048), BF16),
            pltpu.VMEM((2048, 1024), BF16),
            pltpu.VMEM((2048, 1024), BF16),
            pltpu.VMEM((1024, 2048), BF16),
            dma((4,)), dma((2,)), dma((2,)), dma((16,)), dma((16,)),
            dma((4, 3)), dma((4, 3)), dma((4, 3)), dma((4, 3)),
        ],
        compiler_params=pltpu.CompilerParams(
            collective_id=1, has_side_effects=True, vmem_limit_bytes=40 << 20
        ),
        name="finish",
    )(part, pool_order.reshape(4, 128), qown, newkv, tokens, ffn_gain.reshape(16, 128), *stay(w_out, w_gate, w_up, w_down))
    new_kv = new_kv.reshape(ROWS, 2, 2, HEAD_DIM).transpose(0, 2, 1, 3).reshape(ROWS, 2, 256)
    return hidden, new_kv


def solution(mesh):
    placed = (
        P("req", None), P("req"), P(), P("req"), P("req"), P("req", None, "tp"), P(),
        P(None, "tp"), P(None, "tp"), P(None, "tp"), P("tp", None), P(),
        P(None, "tp"), P(None, "tp"), P("tp", None),
    )
    return jax.shard_map(
        per_device,
        mesh=mesh,
        in_specs=placed,
        out_specs=(P("req", None), P("req", None, "tp")),
        check_vma=False,
    )
```

```python
import functools
import math

import jax
import jax.numpy as jnp
import numpy as np
from jax import lax
from jax.experimental import pallas as pl
from jax.experimental.pallas import tpu as pltpu
from jax.sharding import PartitionSpec as P

MESH = pl.DeviceIdType.MESH
HEAD_DIM = 128
ROPE_BASE = 1000000.0
EPS = 1e-05
FLOOR = -1e30
SCALE = 1.0 / math.sqrt(HEAD_DIM)
SIDE = 4
CHIPS = SIDE * SIDE
ROWS = 16
REQS = 512
SLOTS = 4096
HALF = REQS // 2
QW = 512
PW = QW + 128
WIN = 64
STEP = 1024
CHUNK = 4096
PARTS = 4
WIDTH = 2048 // PARTS
TP_ORDER = (1, 0, 2)
LOG2E = 1.4426950408889634
BF16 = jnp.bfloat16
F32 = jnp.float32


def place():
    me = lax.axis_index("req")
    core = lax.rem(me, 2)
    chip = me // 2
    return core, chip // SIDE, lax.rem(chip, SIDE), lax.axis_index("tp")


def chip_at(y, z, k):
    return lax.rem(y + k // SIDE, SIDE) * SIDE + lax.rem(z + k % SIDE, SIDE)


def device(chip, core, tp):
    return {"req": chip * 2 + core, "tp": tp}


def rms_norm(rows, gain):
    scale = lax.rsqrt(jnp.mean(rows * rows, axis=-1, keepdims=True) + EPS)
    gain = gain.astype(F32)
    tiles = [rows[:, i * 128:(i + 1) * 128] * scale * gain[i:i + 1, :] for i in range(gain.shape[0])]
    return jnp.concatenate(tiles, axis=1).astype(BF16)


def frequency_table():
    half = HEAD_DIM // 2
    turns = ROPE_BASE ** (-(np.arange(half, dtype=np.float64) * 2.0) / HEAD_DIM) / (2.0 * np.pi)
    first = np.round(turns * 2.0**12) / 2.0**12
    second = np.round((turns - first) * 2.0**23) / 2.0**23
    third = turns - first - second
    table = np.zeros((8, HEAD_DIM), np.float64)
    for i, term in enumerate((first, second, third)):
        table[i] = np.concatenate([term, term])
    return table.astype(np.float32)


def cos_sin(where, table):
    turn = where * table[0:1, :]
    turn = turn - jnp.floor(turn + 0.5)
    turn = turn + where * table[1:2, :]
    turn = turn - jnp.floor(turn + 0.5)
    turn = turn + where * table[2:3, :]
    quarter = jnp.floor(turn * 4.0 + 0.5)
    x = (turn - quarter * 0.25) * np.float32(2.0 * np.pi)
    sq = x * x
    sine = x * (1.0 + sq * (-1.0 / 6 + sq * (1.0 / 120 + sq * (-1.0 / 5040 + sq * (1.0 / 362880)))))
    cosine = 1.0 + sq * (
        -0.5 + sq * (1.0 / 24 + sq * (-1.0 / 720 + sq * (1.0 / 40320 + sq * (-1.0 / 3628800))))
    )
    odd = (quarter == 1.0) | (quarter == -1.0)
    far = (quarter == 2.0) | (quarter == -2.0)
    c = jnp.where(odd, -quarter * sine, jnp.where(far, -cosine, cosine))
    s = jnp.where(odd, quarter * cosine, jnp.where(far, -sine, sine))
    return c, s


def project_kernel(
    len_h, pos_h, tok_h, gain_h, table_h, wq_h, wk_h, wv_h, pool_h,
    qall, qown_o, newkv_o, kvd,
    len_s, pos_s, tok, gain, table, wq, wk, wv, pool, tmp,
    s_sem, w_sem, pool_sem, qs_sem, qr_sem, fs_sem, fr_sem, ds_sem, dr_sem,
):
    core, y, z, tp = place()
    chip = y * SIDE + z
    small = [
        pltpu.make_async_copy(src, dst, s_sem.at[i])
        for i, (src, dst) in enumerate(
            ((len_h, len_s), (pos_h, pos_s), (table_h, table), (tok_h, tok), (gain_h, gain))
        )
    ]
    loads = [
        pltpu.make_async_copy(src, dst, w_sem.at[i])
        for i, (src, dst) in enumerate(((wq_h, wq), (wk_h, wk), (wv_h, wv)))
    ]
    piece = 4 * SLOTS // 4
    pool_loads = [
        pltpu.make_async_copy(pool_h.at[pl.ds(i * piece, piece)], pool.at[pl.ds(i * piece, piece)], pool_sem.at[i])
        for i in range(4)
    ]
    for copy in small + loads + pool_loads:
        copy.start()

    barrier = pltpu.get_barrier_semaphore()
    sibling = device(chip, 1 - core, tp)
    peers = [sibling] + [device(chip_at(y, z, k), core, tp) for k in range(1, CHIPS)]
    across = [device(chip_at(y, z, k), 1 - core, tp) for k in range(1, SIDE)]
    for peer in peers + across:
        pl.semaphore_signal(barrier, inc=1, device_id=peer, device_id_type=MESH)

    for copy in small:
        copy.wait()
    row = lax.broadcasted_iota(jnp.int32, (ROWS, 128), 0)
    lane = lax.broadcasted_iota(jnp.int32, (ROWS, 128), 1)
    where = jnp.zeros((ROWS, 128), jnp.int32)
    digits = jnp.zeros((ROWS, 128), jnp.int32)
    for i in range(ROWS):
        where = jnp.where(row == i, pos_s[i], where)
        digits = jnp.where(row == i, len_s[i], digits)
    digits = jnp.where(lane == 0, digits >> 7, jnp.where(lane == 1, digits & 127, 0)).astype(F32).astype(BF16)
    cosine, sine = cos_sin(where.astype(F32), table[...])
    sine = jnp.where(lane < HEAD_DIM // 2, -sine, sine)

    def rotate(vectors):
        return vectors * cosine + pltpu.roll(vectors, HEAD_DIM // 2, axis=1) * sine

    normed = rms_norm(tok[...].astype(F32), gain[...])

    pl.semaphore_wait(barrier, len(peers) + len(across))
    loads[0].wait()
    query = jnp.dot(normed, wq[...], preferred_element_type=F32)
    mine_at = pl.multiple_of(core * HALF + chip * ROWS, ROWS)
    for h in range(QW // HEAD_DIM):
        cols = pl.ds(h * HEAD_DIM, HEAD_DIM)
        turned = rotate(query[:, h * HEAD_DIM:(h + 1) * HEAD_DIM]).astype(BF16)
        qall[pl.ds(mine_at, ROWS), cols] = turned
        qown_o[:, cols] = turned
    qall[pl.ds(mine_at, ROWS), pl.ds(QW, 128)] = digits
    my_rows = qall.at[pl.ds(mine_at, ROWS)]
    q_sends = {}
    for k in range(1, CHIPS):
        q_sends[k] = pltpu.make_async_remote_copy(
            src_ref=my_rows, dst_ref=my_rows, send_sem=qs_sem.at[k], recv_sem=qr_sem.at[k],
            device_id=peers[k], device_id_type=MESH,
        )
    own_forward = pltpu.make_async_remote_copy(
        src_ref=my_rows, dst_ref=my_rows, send_sem=fs_sem.at[0], recv_sem=fr_sem.at[0],
        device_id=sibling, device_id_type=MESH,
    )
    directs = [
        pltpu.make_async_remote_copy(
            src_ref=my_rows, dst_ref=my_rows, send_sem=ds_sem.at[k], recv_sem=dr_sem.at[k],
            device_id=across[k - 1], device_id_type=MESH,
        )
        for k in range(1, SIDE)
    ]
    for k in (10, 9, 11, 8, 6, 5, 7, 4, 14, 13, 15, 12):
        q_sends[k].start()
    own_forward.start()
    for k in (2, 1, 3):
        directs[k - 1].start()
        q_sends[k].start()

    def forward(dy):
        source = lax.rem(y + SIDE - dy, SIDE) * SIDE * ROWS
        rows = qall.at[pl.ds(pl.multiple_of(core * HALF + source, SIDE * ROWS), SIDE * ROWS)]
        return pltpu.make_async_remote_copy(
            src_ref=rows, dst_ref=rows, send_sem=fs_sem.at[dy], recv_sem=fr_sem.at[dy],
            device_id=sibling, device_id_type=MESH,
        )

    loads[1].wait()
    key = jnp.dot(normed, wk[...], preferred_element_type=F32)
    loads[2].wait()
    value = jnp.dot(normed, wv[...], preferred_element_type=F32)
    for h in range(2):
        cols = slice(h * HEAD_DIM, (h + 1) * HEAD_DIM)
        newkv_o[pl.ds(2 * h, ROWS, stride=4), :] = rotate(key[:, cols])
        newkv_o[pl.ds(2 * h + 1, ROWS, stride=4), :] = value[:, cols]

    def untangle(i):
        tmp[...] = pool[pl.ds(i * 1024, 1024), :].astype(F32)
        for j in range(4):
            kvd[pl.ds(i * 256, 256), pl.ds(j * 128, 128)] = tmp[pl.ds(j, 256, stride=4), :].astype(BF16)

    for i in range(4):
        pool_loads[i].wait()
    forwards = []
    for i, dy in enumerate((2, 1, 3, 0)):
        for j in range(SIDE):
            untangle(4 * i + j)
        for dz in range(SIDE):
            if dy:
                q_sends[dy * SIDE + dz].wait_recv()
        if dy:
            forwards.append(forward(dy))
            forwards[-1].start()
    for copy in forwards:
        copy.wait()
    own_forward.wait()
    for copy in directs:
        copy.wait()
    for k in range(1, SIDE):
        q_sends[k].wait_recv()
    for copy in q_sends.values():
        copy.wait_send()


def request_of(n):
    return ((n >> 4) & 15) * 32 + (n >> 8) * 16 + (n & 15)


def as_bf16(flags):
    return flags.astype(F32).astype(BF16)


def attend_kernel(
    base_s, qall, order, mask, kvd, newkv, pooled, newkv_o,
    scores, order_b, first_b, last_b, out_sem,
):
    leave = pltpu.make_async_copy(newkv, newkv_o, out_sem)
    leave.start()
    base = base_s[0]

    n_lane = [request_of(lax.broadcasted_iota(jnp.int32, (1, 128), 1) + 128 * t) for t in range(4)]
    for t in range(4):
        tile = jnp.broadcast_to(order[t:t + 1, :], (128, 128)).astype(F32)
        order_b[pl.ds(128 * t, 128), :] = jnp.transpose(tile).astype(jnp.int32)
    p_sub = lax.broadcasted_iota(jnp.int32, (REQS, 128), 0)
    here, upto = [], []
    for t in range(4):
        match = order_b[...] == n_lane[t]
        pos = jnp.sum(jnp.where(match, p_sub.astype(F32), 0.0), axis=0, keepdims=True).astype(jnp.int32)
        here.append(as_bf16(match))
        upto.append(as_bf16(pos <= p_sub))
    digits = qall[:, pl.ds(QW, 128)]

    def lengths_by(flags):
        found = jnp.dot(jnp.concatenate(flags, axis=1), digits, preferred_element_type=F32)
        return (found[:, 0:1] * 128.0 + found[:, 1:2]).astype(jnp.int32)

    ends = lengths_by(upto) - base
    starts = ends - lengths_by(here)
    first_b[...] = jnp.broadcast_to(starts, (REQS, 128))
    last_b[...] = jnp.broadcast_to(ends, (REQS, 128))
    low = jnp.sum((ends <= 0).astype(jnp.int32))
    high = jnp.sum((starts < SLOTS).astype(jnp.int32))
    low = (low // 16) * 16
    windows = (high - low + (WIN - 1)) // WIN

    pooled[...] = jnp.zeros_like(pooled)
    slot = lax.broadcasted_iota(jnp.int32, (1, 128), 1)
    ones = jnp.ones((STEP, 128), BF16)

    @pl.loop(0, windows)
    def _(w):
        at = pl.multiple_of(jnp.minimum(low + w * WIN, REQS - WIN), 16)
        own = order_b[pl.ds(at, WIN), :]
        pick = jnp.concatenate([as_bf16(own == n_lane[t]) for t in range(4)], axis=1)
        query = jnp.dot(pick, qall[:, pl.ds(0, QW)], preferred_element_type=F32).astype(BF16)
        first = first_b[pl.ds(at, WIN), :]
        last = last_b[pl.ds(at, WIN), :]
        chunk_from = jnp.maximum(jnp.min(first), 0) // CHUNK
        chunk_to = (jnp.minimum(jnp.max(last), SLOTS) + (CHUNK - 1)) // CHUNK
        first = jnp.concatenate([first, first], axis=0)
        last = jnp.concatenate([last, last], axis=0)
        rows = [jnp.concatenate([head(query, 2 * j), head(query, 2 * j + 1)], axis=0) for j in range(2)]

        def score(c, peaks):
            start = pl.multiple_of(c * CHUNK, CHUNK)
            peaks = list(peaks)
            for n in range(CHUNK // STEP):
                at_n = pl.multiple_of(start + n * STEP, STEP)
                oks = []
                for i in range(STEP // 128):
                    live = mask[pl.ds(c * (CHUNK // 128) + n * (STEP // 128) + i, 1), :] == 1
                    index = jnp.where(live, slot + (at_n + i * 128), -REQS * 8192)
                    oks.append((index >= first) & (index < last))
                for j in range(2):
                    s = lax.dot_general(
                        rows[j], kvd[pl.ds(at_n, STEP), pl.ds(2 * j * 128, 128)],
                        (((1,), (1,)), ((), ())), preferred_element_type=F32,
                    )
                    for i in range(STEP // 128):
                        found = jnp.where(oks[i], s[:, i * 128:(i + 1) * 128], FLOOR)
                        scores[j, :, pl.ds(pl.multiple_of(at_n + i * 128, 128), 128)] = found
                        peaks[j] = jnp.maximum(peaks[j], found)
            return tuple(peaks)

        least = jnp.full((2 * WIN, 128), FLOOR, F32)
        peaks = lax.fori_loop(chunk_from, chunk_to, score, (least, least))
        peaks = [jnp.max(peak, axis=1, keepdims=True) for peak in peaks]
        peaks = [jnp.where(peak > 0.5 * FLOOR, peak, 0.0) for peak in peaks]

        def weigh(c, sums):
            start = pl.multiple_of(c * CHUNK, CHUNK)
            sums = list(sums)
            for n in range(CHUNK // STEP):
                at_n = pl.multiple_of(start + n * STEP, STEP)
                for j in range(2):
                    weight = jnp.exp2((scores[j, :, pl.ds(at_n, STEP)] - peaks[j]) * (SCALE * LOG2E)).astype(BF16)
                    values = kvd[pl.ds(at_n, STEP), pl.ds((2 * j + 1) * 128, 128)]
                    both = jnp.concatenate([values, ones], axis=1)
                    sums[j] = sums[j] + jnp.dot(weight, both, preferred_element_type=F32)
            return tuple(sums)

        zero = jnp.zeros((2 * WIN, 256), F32)
        sums = lax.fori_loop(chunk_from, chunk_to, weigh, (zero, zero))
        top, totals = [], []
        for j in range(2):
            total = sums[j][:, 128:]
            mean = (sums[j][:, :128] / jnp.where(total > 0.0, total, 1.0)).astype(BF16)
            for g in range(2):
                h, part_rows = 2 * j + g, slice(g * WIN, (g + 1) * WIN)
                pooled[pl.ds(at, WIN), pl.ds(h * HEAD_DIM, HEAD_DIM)] = mean[part_rows]
                top.append(jnp.broadcast_to(peaks[j][part_rows] * SCALE, (WIN, 128)))
                totals.append(total[part_rows])
        pooled[pl.ds(at, WIN), pl.ds(QW, 128)] = stats_of(top, totals)

    leave.wait()


def pack_stats(stats):
    lane = lax.broadcasted_iota(jnp.int32, stats.shape, 1)
    top = stats.astype(BF16).astype(F32)
    rest = stats - top
    middle = rest.astype(BF16).astype(F32)
    rest = rest - middle
    kept = jnp.where(lane < 8, top, jnp.where(lane < 16, middle, jnp.where(lane < 24, rest, 0.0)))
    return kept.astype(BF16)


def stats_of(peaks, totals):
    value = lax.broadcasted_iota(jnp.int32, peaks[0].shape, 1) & 7
    stats = jnp.zeros(peaks[0].shape, F32)
    for h in range(4):
        stats = jnp.where(value == h, peaks[h], stats)
        stats = jnp.where(value == 4 + h, totals[h], stats)
    return pack_stats(stats)


def spreader():
    value = lax.broadcasted_iota(jnp.int32, (128, 2 * QW), 0)
    column = lax.broadcasted_iota(jnp.int32, (128, 2 * QW), 1)
    return ((value < 24) & ((value & 7) == (column >> 7))).astype(F32).astype(BF16)


def head(block, h):
    return block[:, h * HEAD_DIM:(h + 1) * HEAD_DIM]


def finish_kernel(
    pooled, order, qown, newkv, tok, gain, wo_h, wg_h, wu_h, wd_h, out,
    part, came, comb, rx, mix, down, spread, left_stats, right_stats, left_share, right_share, wo, wg, wu, wd,
    w_sem, ps_sem, pr_sem, cs_sem, cr_sem, ms_sem, mr_sem, ds_sem, dr_sem,
):
    core, y, z, tp = place()
    chip = y * SIDE + z
    barrier = pltpu.get_barrier_semaphore()
    sibling = device(chip, 1 - core, tp)
    peers = [sibling] + [device(chip_at(y, z, k), core, tp) for k in range(1, CHIPS)]
    beside = [device(chip, core, lax.rem(tp + d, 4)) for d in range(1, 4)]
    for peer in peers + beside:
        pl.semaphore_signal(barrier, inc=1, device_id=peer, device_id_type=MESH)
    loads = [
        pltpu.make_async_copy(src, dst, w_sem.at[i])
        for i, (src, dst) in enumerate(((wo_h, wo), (wg_h, wg), (wu_h, wu), (wd_h, wd)))
    ]
    for copy in loads:
        copy.start()
    n_sub = request_of(lax.broadcasted_iota(jnp.int32, (REQS, 128), 0))
    place_n = jnp.concatenate([as_bf16(order[t:t + 1, :] == n_sub) for t in range(4)], axis=1)
    part[...] = jnp.dot(place_n, pooled[...], preferred_element_type=F32).astype(BF16)
    spread[...] = spreader()
    half = pl.multiple_of(core * HALF, HALF)
    left_stats[...] = jnp.dot(part[pl.ds(half, HALF), pl.ds(QW, 128)], spread[...], preferred_element_type=F32)
    own_peaks, own_values = [], []
    for h in range(4):
        keys = newkv[pl.ds(2 * (h // 2), ROWS, stride=4), :].astype(BF16).astype(F32)
        query = head(qown[...], h).astype(F32)
        score = jnp.sum(query * keys, axis=1, keepdims=True) * SCALE
        own_peaks.append(jnp.broadcast_to(score, (ROWS, HEAD_DIM)))
        own_values.append(newkv[pl.ds(2 * (h // 2) + 1, ROWS, stride=4), :].astype(BF16).astype(F32))
    pl.semaphore_wait(barrier, len(peers) + len(beside))

    def rows_of(dy):
        return pl.multiple_of(lax.rem(y + dy, SIDE) * 64, 64)

    turns = (2, 1, 3, 0)
    theirs = pl.ds(pl.multiple_of(HALF - half, HALF), HALF)
    swaps = [
        pltpu.make_async_remote_copy(
            src_ref=part.at[theirs, cols], dst_ref=came.at[:, cols],
            send_sem=ps_sem.at[i], recv_sem=pr_sem.at[i], device_id=sibling, device_id_type=MESH,
        )
        for i, cols in enumerate((pl.ds(QW, 128), pl.ds(0, QW)))
    ]
    for swap in swaps:
        swap.start()

    def stat(ref, rows, h):
        totals = ref[rows, pl.ds(QW + h * HEAD_DIM, HEAD_DIM)]
        return jnp.where(totals > 0.0, ref[rows, pl.ds(h * HEAD_DIM, HEAD_DIM)], FLOOR), totals

    swaps[0].wait_recv()
    right_stats[...] = jnp.dot(came[:, pl.ds(QW, 128)], spread[...], preferred_element_type=F32)
    for dy in turns:
        rows = pl.ds(rows_of(dy), 64)
        peaks, totals = [], []
        for h in range(4):
            cols = pl.ds(h * HEAD_DIM, HEAD_DIM)
            peak_a, total_a = stat(left_stats, rows, h)
            peak_b, total_b = stat(right_stats, rows, h)
            peak = jnp.maximum(peak_a, peak_b)
            left = total_a * jnp.exp(peak_a - peak)
            right = total_b * jnp.exp(peak_b - peak)
            total = left + right
            kept = jnp.where(total > 0.0, total, 1.0)
            left_share[rows, cols] = left / kept
            right_share[rows, cols] = right / kept
            peaks.append(jnp.where(total > 0.0, peak, 0.0))
            totals.append(total)
        comb[rows, pl.ds(QW, 128)] = stats_of(peaks, totals)

    swaps[1].wait_recv()
    sends = []
    for dy in turns:
        rows = pl.ds(rows_of(dy), 64)
        mine = pl.ds(pl.multiple_of(half + rows_of(dy), 64), 64)
        for h in range(4):
            cols = pl.ds(h * HEAD_DIM, HEAD_DIM)
            summed = part[mine, cols].astype(F32) * left_share[rows, cols]
            comb[rows, cols] = (summed + came[rows, cols].astype(F32) * right_share[rows, cols]).astype(BF16)
        for dz in (2, 1, 3, 0):
            k = dy * SIDE + dz
            if k == 0:
                continue
            block = comb.at[pl.ds(pl.multiple_of(chip_at(y, z, k) * ROWS, ROWS), ROWS)]
            sends.append(
                pltpu.make_async_remote_copy(
                    src_ref=block, dst_ref=rx.at[k], send_sem=cs_sem.at[k], recv_sem=cr_sem.at[k],
                    device_id=peers[k], device_id_type=MESH,
                )
            )
            sends[-1].start()
    rx[0] = comb[pl.ds(pl.multiple_of(chip * ROWS, ROWS), ROWS), :]

    for copy in sends:
        copy.wait_recv()
    found = [rx[k, :, pl.ds(QW, 128)] for k in range(CHIPS)]
    left_stats[...] = jnp.dot(jnp.concatenate(found, axis=0), spread[...], preferred_element_type=F32)
    context = []
    for h in range(4):
        cols = pl.ds(h * HEAD_DIM, HEAD_DIM)
        stats = [stat(left_stats, pl.ds(k * ROWS, ROWS), h) for k in range(CHIPS)]
        peak = own_peaks[h]
        for other, _ in stats:
            peak = jnp.maximum(peak, other)
        total = jnp.exp(own_peaks[h] - peak)
        summed = total * own_values[h]
        for k in range(CHIPS):
            weight = stats[k][1] * jnp.exp(stats[k][0] - peak)
            total = total + weight
            summed = summed + weight * rx[k, :, cols].astype(F32)
        context.append((summed / total).astype(BF16))
    context = jnp.concatenate(context, axis=1)

    def over_tp(left, right, terms, send, recv):
        copies = []
        for n in range(PARTS):
            cols = pl.ds(n * WIDTH, WIDTH)
            terms[tp, :, cols] = jnp.dot(left, right[:, cols], preferred_element_type=F32).astype(BF16)
            ref = terms.at[tp, :, cols]
            copies.append([
                pltpu.make_async_remote_copy(
                    src_ref=ref, dst_ref=ref, send_sem=send.at[n, d], recv_sem=recv.at[n, d],
                    device_id=beside[d], device_id_type=MESH,
                )
                for d in TP_ORDER
            ])
            for copy in copies[-1]:
                copy.start()
        return copies

    def summed_terms(first, terms, n):
        cols = pl.ds(n * WIDTH, WIDTH)
        total = first
        for t in range(4):
            total = total + terms[t, :, cols].astype(F32)
        return total

    loads[0].wait()
    mixes = over_tp(context, wo, mix, ms_sem, mr_sem)
    loads[1].wait()
    loads[2].wait()
    mids, squares = [], jnp.zeros((ROWS, 1), F32)
    gate = jnp.zeros((ROWS, 1024), F32)
    upper = jnp.zeros((ROWS, 1024), F32)
    for n in range(PARTS):
        for copy in mixes[n]:
            copy.wait_recv()
        cols = pl.ds(n * WIDTH, WIDTH)
        mid = summed_terms(tok[:, cols].astype(F32), mix, n)
        mids.append(mid)
        squares = squares + jnp.sum(mid * mid, axis=-1, keepdims=True)
        gains = [gain[pl.ds(n * (WIDTH // 128) + i, 1), :] for i in range(WIDTH // 128)]
        scaled = (mid * jnp.concatenate(gains, axis=1).astype(F32)).astype(BF16)
        gate = gate + jnp.dot(scaled, wg[cols, :], preferred_element_type=F32)
        upper = upper + jnp.dot(scaled, wu[cols, :], preferred_element_type=F32)
    scale = lax.rsqrt(squares * (1.0 / 2048) + EPS)
    gate = gate * scale
    act = (gate / (1.0 + jnp.exp(-gate)) * (upper * scale)).astype(BF16)
    loads[3].wait()
    downs = over_tp(act, wd, down, ds_sem, dr_sem)
    for n in range(PARTS):
        for copy in downs[n]:
            copy.wait_recv()
        out[:, pl.ds(n * WIDTH, WIDTH)] = summed_terms(mids[n], down, n)
    for copy in swaps + sends + sum(mixes + downs, []):
        copy.wait_send()


def per_device(
    tokens, lengths, pool_order, positions, slot_mask, kv_cache, attn_gain,
    w_query, w_key, w_value, w_out, ffn_gain, w_gate, w_up, w_down,
):
    def stay(*arrays):
        return [pltpu.with_memory_space_constraint(a, pltpu.HBM) for a in arrays]

    vmem = pl.BlockSpec(memory_space=pltpu.VMEM)
    smem = pl.BlockSpec(memory_space=pltpu.SMEM)
    hbm = pl.BlockSpec(memory_space=pltpu.HBM)
    dma = pltpu.SemaphoreType.DMA
    pool = kv_cache.reshape(SLOTS, 2, 2, HEAD_DIM).transpose(0, 2, 1, 3).reshape(4 * SLOTS, HEAD_DIM)
    qall, qown, newkv, kvd = pl.pallas_call(
        project_kernel,
        out_shape=(
            jax.ShapeDtypeStruct((REQS, PW), BF16),
            jax.ShapeDtypeStruct((ROWS, QW), BF16),
            jax.ShapeDtypeStruct((4 * ROWS, HEAD_DIM), F32),
            jax.ShapeDtypeStruct((SLOTS, QW), BF16),
        ),
        in_specs=[hbm] * 9,
        out_specs=(vmem,) * 4,
        scratch_shapes=[
            pltpu.SMEM((ROWS,), jnp.int32),
            pltpu.SMEM((ROWS,), jnp.int32),
            pltpu.VMEM((ROWS, 2048), BF16),
            pltpu.VMEM((16, 128), BF16),
            pltpu.VMEM((8, 128), F32),
            pltpu.VMEM((2048, 512), BF16),
            pltpu.VMEM((2048, 256), BF16),
            pltpu.VMEM((2048, 256), BF16),
            pltpu.VMEM((4 * SLOTS, HEAD_DIM), BF16),
            pltpu.VMEM((1024, HEAD_DIM), F32),
            dma((5,)), dma((3,)), dma((4,)), dma((16,)), dma((16,)), dma((4,)), dma((4,)), dma((4,)), dma((4,)),
        ],
        compiler_params=pltpu.CompilerParams(
            collective_id=0, has_side_effects=True, vmem_limit_bytes=40 << 20
        ),
        name="project",
    )(
        *stay(
            lengths, positions, tokens, attn_gain.reshape(16, 128), jnp.asarray(frequency_table()),
            w_query, w_key, w_value, pool,
        )
    )
    base = (lax.axis_index("req") * SLOTS).astype(jnp.int32).reshape(1)
    part, new_kv = pl.pallas_call(
        attend_kernel,
        out_shape=(
            jax.ShapeDtypeStruct((REQS, PW), BF16),
            pltpu.HBM((4 * ROWS, HEAD_DIM), F32),
        ),
        in_specs=[smem, vmem, vmem, vmem, vmem, vmem],
        out_specs=(vmem, hbm),
        scratch_shapes=[
            pltpu.VMEM((2, 2 * WIN, SLOTS), F32),
            pltpu.VMEM((REQS, 128), jnp.int32),
            pltpu.VMEM((REQS, 128), jnp.int32),
            pltpu.VMEM((REQS, 128), jnp.int32),
            dma,
        ],
        compiler_params=pltpu.CompilerParams(vmem_limit_bytes=40 << 20),
        name="attend",
    )(base, qall, pool_order.reshape(4, 128), slot_mask.reshape(32, 128), kvd, newkv)
    hidden = pl.pallas_call(
        finish_kernel,
        out_shape=jax.ShapeDtypeStruct((ROWS, 2048), F32),
        in_specs=[vmem] * 6 + [hbm] * 4,
        out_specs=vmem,
        scratch_shapes=[
            pltpu.VMEM((REQS, PW), BF16),
            pltpu.VMEM((HALF, PW), BF16),
            pltpu.VMEM((HALF, PW), BF16),
            pltpu.VMEM((CHIPS, ROWS, PW), BF16),
            pltpu.VMEM((4, ROWS, 2048), BF16),
            pltpu.VMEM((4, ROWS, 2048), BF16),
            pltpu.VMEM((128, 2 * QW), BF16),
            pltpu.VMEM((HALF, 2 * QW), F32),
            pltpu.VMEM((HALF, 2 * QW), F32),
            pltpu.VMEM((HALF, QW), F32),
            pltpu.VMEM((HALF, QW), F32),
            pltpu.VMEM((512, 2048), BF16),
            pltpu.VMEM((2048, 1024), BF16),
            pltpu.VMEM((2048, 1024), BF16),
            pltpu.VMEM((1024, 2048), BF16),
            dma((4,)), dma((2,)), dma((2,)), dma((16,)), dma((16,)),
            dma((4, 3)), dma((4, 3)), dma((4, 3)), dma((4, 3)),
        ],
        compiler_params=pltpu.CompilerParams(
            collective_id=1, has_side_effects=True, vmem_limit_bytes=40 << 20
        ),
        name="finish",
    )(part, pool_order.reshape(4, 128), qown, newkv, tokens, ffn_gain.reshape(16, 128), *stay(w_out, w_gate, w_up, w_down))
    new_kv = new_kv.reshape(ROWS, 2, 2, HEAD_DIM).transpose(0, 2, 1, 3).reshape(ROWS, 2, 256)
    return hidden, new_kv


def solution(mesh):
    placed = (
        P("req", None), P("req"), P(), P("req"), P("req"), P("req", None, "tp"), P(),
        P(None, "tp"), P(None, "tp"), P(None, "tp"), P("tp", None), P(),
        P(None, "tp"), P(None, "tp"), P("tp", None),
    )
    return jax.shard_map(
        per_device,
        mesh=mesh,
        in_specs=placed,
        out_specs=(P("req", None), P("req", None, "tp")),
        check_vma=False,
    )
```
